32 devices in a mesh: sample: 4 (over y, x), tile: 8 (over z, core).
Axes of the slice: x: 2, y: 2, z: 4, core: 2. Of those that a mesh axis runs over, the one named last changes fastest.
Arguments:
- points: bfloat16 [4, 8192, 64], P('sample', 'tile'), may hold values from -6 to 6
- slot: int32 [4, 8192], P('sample', 'tile'), may hold values from 0 to 2047, as said below
- voxel: int32 [4, 8192], P('sample', 'tile'), may hold values from 0 to 1023
- conv_weight: bfloat16 [1728, 128], replicated, may hold values from -0.15625 to 0.15625
- down_weight: bfloat16 [1024, 256], replicated, may hold values from -0.1875 to 0.1875
- cotangent: bfloat16 [4, 16, 16, 4, 256], P('sample', 'tile'), may hold values from -0.09375 to 0.09375
Outputs:
- down_features: bfloat16 [4, 16, 16, 4, 256], P('sample', 'tile')
- conv_grad: float32 [1728, 128], P('sample')
- down_grad: float32 [1024, 256], P('sample')
The draws below stay inside these ranges and needn't reach their ends.
Inputs may be any that keep to these rules, and one draw needn't show every extreme that they name: Within one scene, the 1024 points held by one device have distinct slots; slot // 256 names the slab owner, so at most 256 points go from one device to one owner; in every scene one owner receives exactly 256 points from every device.
All inputs are finite; a program needn't handle non-finite values.
Results may differ from the reference program's by a relative error of at most 0.0056.
Values may be sent and summed in bfloat16 or wider, within the bound.
No kernel may reach another device: no remote copies, remote signals or barrier semaphores. Data moves between devices by JAX's collectives and lax.ppermute only.
A program may use at most 64 MiB of HBM per device.

```python
import jax
import jax.numpy as jnp
from jax import lax

CIN = 64
C1 = 128
C2 = 256
SX = 4
SY = 32
SZ = 8
PTS_DEV = 1024
CAP = 256
VOX = 1024
SCENES = 4
PTS = 8192
XX = 32
N_SAMPLE = 4
N_TILE = 8


def draw_slot(key, part):
    capacity = CAP
    tile_count = N_TILE
    hot_owners = jax.random.randint(jax.random.fold_in(key, 11), (SCENES,), 0, tile_count).astype(jnp.int32)
    base_key = jax.random.fold_in(key, 23)

    def one_block(block_key, hot_owner):
        perm_key, order_key = jax.random.split(block_key)
        rest_draw = jax.random.permutation(perm_key, (tile_count - 1) * capacity).astype(jnp.int32)[:PTS_DEV - capacity]
        other_owner = rest_draw // capacity
        other_owner = other_owner + (other_owner >= hot_owner).astype(jnp.int32)
        rest_slots = other_owner * capacity + rest_draw % capacity
        hot_slots = hot_owner * capacity + jnp.arange(capacity, dtype=jnp.int32)
        slot_ids = jnp.concatenate([hot_slots, rest_slots])
        return jax.random.permutation(order_key, slot_ids).astype(jnp.int32)

    def one_scene(scene_index):
        hot_owner = hot_owners[scene_index]

        def block(block_index):
            return one_block(jax.random.fold_in(base_key, scene_index * tile_count + block_index), hot_owner)
        return jax.vmap(block)(jnp.arange(tile_count, dtype=jnp.int32)).reshape(-1)
    return jax.vmap(one_scene)(jnp.arange(SCENES, dtype=jnp.int32))


def set_ends(drawn, stream_key, smallest, high):
    longest = drawn.shape.index(max(drawn.shape))
    spots = []
    for shift in (0, 1):
        where = [jax.random.randint(jax.random.fold_in(stream_key, axis), (), 0, length) for axis, length in enumerate(drawn.shape)]
        where[longest] = (where[longest] + shift) % drawn.shape[longest]
        spots.append(tuple(where))
    return drawn.at[spots[0]].set(smallest).at[spots[1]].set(high)


def block_scale(key, dims, cuts, low, largest):
    loudness = 1.0
    for axis_at, parts in cuts:
        heights = jax.random.uniform(jax.random.fold_in(jax.random.fold_in(key, 6), axis_at), (parts,), jnp.float32, low / len(cuts), largest / len(cuts))
        loudness = loudness * jnp.repeat(jnp.exp(heights), dims[axis_at] // parts).reshape((-1,) + (1,) * (len(dims) - 1 - axis_at))
    return loudness


def scatter_about(rng, dims, width, reach, cuts=(), held_as=jnp.bfloat16):
    loudness = block_scale(rng, dims, cuts, -0.22, 0.18) if cuts else 1.0
    result = jax.random.normal(rng, dims, jnp.float32) * width * loudness
    return jnp.minimum(jnp.maximum(result, -reach), reach).astype(held_as)


def setup_inputs(seed: int = 0) -> dict:
    arg_keys = jax.random.split(jax.random.key(seed), 7)
    return {
        "points": scatter_about(arg_keys[0], (SCENES, PTS, CIN), 1.0, 6.0, ((0, 4), (1, 8))),
        "slot": draw_slot(jax.random.fold_in(arg_keys[6], 71), 0),
        "voxel": set_ends(jax.random.randint(arg_keys[2], (SCENES, PTS), 0, VOX), jax.random.fold_in(arg_keys[2], 1), 0, VOX - 1).astype(jnp.int32),
        "conv_weight": scatter_about(arg_keys[3], (27 * CIN, C1), (27 * CIN) ** -0.5, 0.15625),
        "down_weight": scatter_about(arg_keys[4], (8 * C1, C2), (8 * C1) ** -0.5, 0.1875),
        "cotangent": scatter_about(arg_keys[5], (SCENES, XX // 2, SY // 2, SZ // 2, C2), (1.0 / (N_SAMPLE * N_TILE * VOX // 8) ** 0.5), 0.09375, ((0, 4), (1, 8))),
    }


def silu_slope(value):
    sigmoid = jax.nn.sigmoid(value)
    return sigmoid * (1.0 + value * (1.0 - sigmoid))


def stack_taps(padded, depth):
    pieces = []
    for shift_x in range(3):
        for shift_y in range(3):
            for shift_z in range(3):
                pieces.append(padded[shift_x:shift_x + depth, shift_y:shift_y + SY, shift_z:shift_z + SZ, :])
    return jnp.concatenate(pieces, axis=-1).reshape(-1, 27 * CIN)


def regroup(values, depth):
    shaped = values.reshape(depth // 2, 2, SY // 2, 2, SZ // 2, 2, C1)
    return shaped.transpose(0, 2, 4, 1, 3, 5, 6).reshape(-1, 8 * C1)


def ungroup(values, depth):
    shaped = values.reshape(depth // 2, SY // 2, SZ // 2, 2, 2, 2, C1)
    return shaped.transpose(0, 3, 1, 4, 2, 5, 6).reshape(-1, C1)


def reference(points, slot, voxel, conv_weight, down_weight, cotangent):
    slab_size = SX * SY * SZ
    depth = SX * N_TILE

    def one_scene(carry, inputs):
        scene_points, scene_slot, scene_voxel, scene_cot = inputs
        target = (scene_slot // CAP) * slab_size + scene_voxel
        summed = jnp.zeros((depth * SY * SZ, CIN), jnp.float32).at[target].add(scene_points.astype(jnp.float32))
        counts = jnp.zeros((depth * SY * SZ,), jnp.int32).at[target].add(1)
        grid = summed.astype(jnp.bfloat16).reshape(depth, SY, SZ, CIN)
        active = (counts > 0)[:, None]
        padded = jnp.pad(grid, ((1, 1), (1, 1), (1, 1), (0, 0)))
        columns = stack_taps(padded, depth)
        pre = jnp.dot(columns, conv_weight, preferred_element_type=jnp.float32)
        activated = jnp.where(active, jax.nn.silu(pre), 0.0).astype(jnp.bfloat16)
        grouped = regroup(activated, depth)
        output_rows = jnp.dot(grouped, down_weight, preferred_element_type=jnp.float32).astype(jnp.bfloat16)
        cot_rows = scene_cot.reshape(-1, C2)
        grad_down = jnp.dot(grouped.T, cot_rows, preferred_element_type=jnp.float32)
        back = ungroup(jnp.dot(cot_rows, down_weight.T, preferred_element_type=jnp.float32), depth)
        pre_grad = jnp.where(active, back * silu_slope(pre), 0.0).astype(jnp.bfloat16)
        grad_conv = jnp.dot(columns.T, pre_grad, preferred_element_type=jnp.float32)
        new_carry = (carry[0] + grad_conv, carry[1] + grad_down)
        return new_carry, output_rows.reshape(depth // 2, SY // 2, SZ // 2, C2)

    start = (jnp.zeros((27 * CIN, C1), jnp.float32), jnp.zeros((8 * C1, C2), jnp.float32))
    totals, outputs = lax.scan(one_scene, start, (points, slot, voxel, cotangent))
    return outputs, totals[0], totals[1]
```

```python
import functools

import jax
import jax.numpy as jnp
from jax import lax
from jax.experimental import pallas as pl
from jax.experimental.pallas import tpu as pltpu
from jax.sharding import PartitionSpec as P

CIN = 64
C1 = 128
C2 = 256
SX = 4
SY = 32
SZ = 8
PTS_DEV = 1024
TAPS = 27
CODED = CIN + 8
LAYER = SZ * SY // 2
BF16 = jnp.bfloat16
F32 = jnp.float32
I32 = jnp.int32
NT = (((1,), (1,)), ((), ()))
TN = (((0,), (0,)), ((), ()))
VMEM_LIMIT = 56 * 1024 * 1024


def in_vmem(count):
    return [pl.BlockSpec(memory_space=pltpu.VMEM)] * count


def call(body, outs, scratch=(), inputs=0):
    single = not isinstance(outs, (list, tuple))
    return pl.pallas_call(
        body,
        out_shape=outs,
        in_specs=in_vmem(inputs),
        out_specs=in_vmem(1)[0] if single else in_vmem(len(outs)),
        scratch_shapes=list(scratch),
        compiler_params=pltpu.CompilerParams(vmem_limit_bytes=VMEM_LIMIT),
    )


def target(index, k, count):
    if count & (count - 1) == 0:
        return index ^ k
    return (index + k) % count


def origin(index, k, count):
    if count & (count - 1) == 0:
        return index ^ k
    return (index - k + count) % count


def swap_core(value, tiles):
    return lax.ppermute(value, "tile", [(i, i ^ 1) for i in range(tiles)])


def send_column(value, k, tiles):
    chips = tiles // 2
    pairs = [(2 * i + c, 2 * target(i, k, chips) + c) for i in range(chips) for c in range(2)]
    return lax.ppermute(value, "tile", pairs)


def send_sample(value, k, samples):
    return lax.ppermute(value, "sample", [(i, target(i, k, samples)) for i in range(samples)])


def encode_kernel(capacity, points_ref, slot_ref, voxel_ref, out_ref):
    slot = slot_ref[...]
    voxel = voxel_ref[...]
    if capacity & (capacity - 1) == 0:
        owner = slot >> (capacity.bit_length() - 1)
    else:
        owner = jnp.floor((slot.astype(F32) + 0.5) * (1.0 / capacity)).astype(I32)
    layer = owner * SX + (voxel >> 8) + 1
    z = voxel & 7
    y = (voxel >> 3) & 31
    place = ((z * 16 + (y >> 1)) << 1) + (y & 1)
    row = lax.broadcasted_iota(I32, (8, slot.shape[1]), 0)
    codes = jnp.where(row == 0, layer, jnp.where(row == 1, place, 0))
    out_ref[0:CIN, :] = points_ref[...]
    out_ref[CIN:CODED, :] = codes.astype(F32).astype(BF16)


def scene_kernel(sources, samples, half_rows, *refs):
    coded = refs[:sources]
    conv_ref, down_ref, cot_ref, out_ref, mine_ref, other_ref, es_ref, pg_ref, wide_ref, tall_ref = refs[sources:]
    tile = lax.axis_index("tile")
    rows = 3 * LAYER
    row_iota = lax.broadcasted_iota(I32, (rows, PTS_DEV), 0)
    small_iota = lax.broadcasted_iota(I32, (32, PTS_DEV), 0)

    grid = jnp.zeros((rows, 4 * CIN), F32)
    counts = jnp.zeros((32, 32), F32)
    for ref in coded:
        codes = ref[CIN:CODED, :].astype(F32).astype(I32)
        layer = codes[0:1, :]
        place = codes[1:2, :]
        pair = (layer >> 1) - 2 * tile
        odd = layer & 1
        spot = place >> 1
        side = place & 1
        hot = (row_iota == pair * LAYER + spot).astype(F32).astype(BF16)
        group = odd * 2 + side
        features = ref[0:CIN, :]
        spread = jnp.concatenate(
            [features * (group == g).astype(F32).astype(BF16) for g in range(4)], axis=0
        )
        grid = grid + lax.dot_general(hot, spread, NT, preferred_element_type=F32)
        plane = (2 * pair + odd - 1) * SZ + (spot >> 4)
        hot_plane = (small_iota == plane).astype(F32).astype(BF16)
        hot_line = (small_iota == (spot & 15) * 2 + side).astype(F32).astype(BF16)
        counts = counts + lax.dot_general(hot_plane, hot_line, NT, preferred_element_type=F32)

    es_ref[...] = jnp.zeros_like(es_ref)
    pg_ref[...] = jnp.zeros_like(pg_ref)
    line = lax.broadcasted_iota(I32, (LAYER, 2 * CIN), 0) & 15
    lane = lax.broadcasted_iota(I32, (LAYER, 2 * CIN), 1)
    for x in range(SX + 2):
        both = grid[(x // 2) * LAYER : (x // 2 + 1) * LAYER, (x % 2) * 128 : (x % 2 + 1) * 128]
        turned = pltpu.roll(both, CIN, 1)
        before = jnp.where(line == 0, 0.0, pltpu.roll(turned, 1, 0))
        after = jnp.where(line == 15, 0.0, pltpu.roll(turned, LAYER - 1, 0))
        sides = jnp.where(lane < CIN, before, after)
        es_ref[x, 1 : SZ + 1, :, 0:128] = both.astype(BF16).reshape(SZ, 16, 128)
        es_ref[x, 1 : SZ + 1, :, 128:256] = sides.astype(BF16).reshape(SZ, 16, 128)

    full = SX * LAYER
    flags = (counts > 0.5).astype(F32).astype(BF16)
    row_plane = lax.broadcasted_iota(I32, (full, 32), 0) >> 4
    pick = (row_plane == lax.broadcasted_iota(I32, (full, 32), 1)).astype(F32).astype(BF16)
    lines = jnp.dot(pick, flags, preferred_element_type=F32)
    row_line = lax.broadcasted_iota(I32, (full, 32), 0) & 15
    lines = jnp.where(row_line == (lax.broadcasted_iota(I32, (full, 32), 1) >> 1), lines, 0.0).astype(BF16)
    expand = (
        (lax.broadcasted_iota(I32, (32, 256), 0) & 1) == (lax.broadcasted_iota(I32, (32, 256), 1) >> 7)
    ).astype(F32).astype(BF16)
    active = jnp.dot(lines, expand, preferred_element_type=F32) > 0.5

    zero_tap = jnp.zeros((CIN, C1), BF16)

    def tap(dx, dy, dz):
        start = ((dx * 3 + dy) * 3 + dz) * CIN
        return conv_ref[start : start + CIN, :]

    pre = jnp.zeros((full, 2 * C1), F32)
    for dx in range(3):
        for dz in range(3):
            weight = jnp.concatenate(
                [
                    jnp.concatenate([tap(dx, 1, dz), tap(dx, 0, dz)], axis=1),
                    jnp.concatenate([tap(dx, 2, dz), tap(dx, 1, dz)], axis=1),
                    jnp.concatenate([tap(dx, 0, dz), zero_tap], axis=1),
                    jnp.concatenate([zero_tap, tap(dx, 2, dz)], axis=1),
                ],
                axis=0,
            )
            part = es_ref[dx : dx + SX, dz : dz + SZ].reshape(full, 4 * CIN)
            pre = pre + jnp.dot(part, weight, preferred_element_type=F32)

    sigmoid = 1.0 / (1.0 + jnp.exp(-pre))
    act = jnp.where(active, pre * sigmoid, 0.0).astype(BF16)
    slope = jnp.where(active, sigmoid * (1.0 + pre * (1.0 - sigmoid)), 0.0)

    act = act.reshape(2, 2, 4, 2, 16, 2 * C1)
    slope = slope.reshape(2, 2, 4, 2, 16, 2 * C1)
    here = lax.broadcasted_iota(I32, (128, 128), 0)
    there = lax.broadcasted_iota(I32, (128, 128), 1)
    turn = ((here >> 6) * 64 + (here & 3) * 16 + ((here >> 2) & 15) == there).astype(F32).astype(BF16)
    cot = lax.dot_general(turn, cot_ref[...], TN, preferred_element_type=F32).astype(BF16)
    down = jnp.zeros((128, C2), F32)
    for ox in range(2):
        for oz in range(2):
            block = act[:, ox, :, oz].reshape(128, 2 * C1)
            first = (ox * 4 + oz) * C1
            second = first + 2 * C1
            weight = jnp.concatenate(
                [down_ref[first : first + C1, :], down_ref[second : second + C1, :]], axis=0
            )
            down = down + jnp.dot(block, weight, preferred_element_type=F32)
            grad = lax.dot_general(block, cot, TN, preferred_element_type=F32)
            wide_ref[first : first + C1, :] = grad[0:C1]
            wide_ref[second : second + C1, :] = grad[C1:]
            back = lax.dot_general(cot, weight, NT, preferred_element_type=F32)
            part = (back * slope[:, ox, :, oz].reshape(128, 2 * C1)).astype(BF16).reshape(2, 4, 16, 2 * C1)
            for u in range(2):
                for w in range(4):
                    pg_ref[2 * u + ox, 1 + 2 * w + oz] = part[u, w]
    out_ref[...] = jnp.dot(turn, down.astype(BF16), preferred_element_type=F32).astype(BF16)

    flipped = es_ref[:, 1 : SZ + 1].reshape((SX + 2) * LAYER, 4 * CIN).T
    for dz in range(3):
        part = pg_ref[:, 2 - dz : 2 - dz + SZ].reshape(full, 2 * C1)
        for dx in range(3):
            grad = jnp.dot(
                flipped[:, dx * LAYER : dx * LAYER + full], part, preferred_element_type=F32
            )
            sums = (
                grad[0:64, 128:256] + grad[128:192, 0:128],
                grad[0:64, 0:128] + grad[64:128, 128:256],
                grad[64:128, 0:128] + grad[192:256, 128:256],
            )
            for dy in range(3):
                start = ((dx * 3 + dy) * 3 + dz) * CIN
                tall_ref[start : start + CIN, :] = sums[dy]

    conv_rows = TAPS * CIN // samples
    down_rows = 8 * C1 // samples
    filler = 2 * half_rows - conv_rows - 2 * down_rows

    def leave(low_ref, high_ref):
        for s in range(samples):
            pieces = [
                tall_ref[s * conv_rows : (s + 1) * conv_rows, :],
                wide_ref[s * down_rows : (s + 1) * down_rows, 0:128],
                wide_ref[s * down_rows : (s + 1) * down_rows, 128:256],
            ]
            if filler:
                pieces.append(jnp.zeros((filler, 128), F32))
            chunk = jnp.concatenate(pieces, axis=0).astype(BF16)
            low_ref[s] = chunk[:half_rows]
            high_ref[s] = chunk[half_rows:]

    core = tile & 1

    @pl.when(core == 0)
    def _():
        leave(mine_ref, other_ref)

    @pl.when(core == 1)
    def _():
        leave(other_ref, mine_ref)


def share_samples_kernel(samples, mine_ref, got_ref, keep_ref, *send_refs):
    me = lax.axis_index("sample")
    keep_ref[...] = mine_ref[me].astype(F32) + got_ref[me].astype(F32)
    for k, ref in enumerate(send_refs, 1):
        to = target(me, k, samples)
        ref[...] = (mine_ref[to].astype(F32) + got_ref[to].astype(F32)).astype(BF16)


def share_column_kernel(samples, chips, rows, keep_ref, *refs):
    got = refs[: samples - 1]
    own_ref = refs[samples - 1]
    sends = refs[samples : samples + chips - 1]
    total_ref = refs[-1]
    total = keep_ref[...]
    for ref in got:
        total = total + ref[...].astype(F32)
    for i in range(chips):
        total_ref[i] = total[i * rows : (i + 1) * rows]
    me = lax.axis_index("tile") >> 1
    own_ref[...] = total_ref[me]
    for k, ref in enumerate(sends, 1):
        ref[...] = total_ref[target(me, k, chips)].astype(BF16)


def sum_kernel(own_ref, *refs):
    total = own_ref[...]
    for ref in refs[:-1]:
        total = total + ref[...].astype(F32)
    refs[-1][...] = total.astype(BF16)


def finish_kernel(chips, rows, conv_rows, down_rows, own_ref, got_ref, conv_ref, down_ref, hold_ref):
    tile = lax.axis_index("tile")
    core = tile & 1
    me = tile >> 1
    for k in range(chips):
        place = origin(me, k, chips)
        hold_ref[core * chips + place] = own_ref[k].astype(F32)
        hold_ref[(1 - core) * chips + place] = got_ref[k].astype(F32)
    whole = jnp.concatenate([hold_ref[i] for i in range(2 * chips)], axis=0)
    conv_ref[...] = whole[:conv_rows]
    down_ref[:, 0:128] = whole[conv_rows : conv_rows + down_rows]
    down_ref[:, 128:256] = whole[conv_rows + down_rows : conv_rows + 2 * down_rows]


def local(points, slot, voxel, conv_weight, down_weight, cotangent):
    tiles = lax.axis_size("tile")
    samples = lax.axis_size("sample")
    chips = tiles // 2
    capacity = 2 * (PTS_DEV // tiles)
    conv_rows = TAPS * CIN // samples
    down_rows = 8 * C1 // samples
    unit = 16 * chips
    total_rows = -(-(conv_rows + 2 * down_rows) // unit) * unit
    half_rows = total_rows // 2
    piece_rows = half_rows // chips

    shape = jax.ShapeDtypeStruct
    coded = call(functools.partial(encode_kernel, capacity), shape((CODED, PTS_DEV), BF16), inputs=3)(
        points[0].T, slot, voxel
    )
    near = [coded] + [send_column(coded, k, tiles) for k in range(1, chips)]
    gathered = near + [swap_core(value, tiles) for value in near]

    down, mine, other = call(
        functools.partial(scene_kernel, tiles, samples, half_rows),
        (
            shape((128, C2), BF16),
            shape((samples, half_rows, 128), BF16),
            shape((samples, half_rows, 128), BF16),
        ),
        scratch=(
            pltpu.VMEM((SX + 2, SZ + 2, 16, 4 * CIN), BF16),
            pltpu.VMEM((SX, SZ + 2, 16, 2 * C1), BF16),
            pltpu.VMEM((8 * C1, C2), F32),
            pltpu.VMEM((TAPS * CIN, C1), F32),
        ),
        inputs=tiles + 3,
    )(*gathered, conv_weight, down_weight, cotangent.reshape(128, C2))

    got = swap_core(other, tiles)
    keep, *sends = call(
        functools.partial(share_samples_kernel, samples),
        [shape((half_rows, 128), F32)] + [shape((half_rows, 128), BF16)] * (samples - 1),
        inputs=2,
    )(mine, got)
    got = [send_sample(value, k, samples) for k, value in enumerate(sends, 1)]
    own, *sends = call(
        functools.partial(share_column_kernel, samples, chips, piece_rows),
        [shape((piece_rows, 128), F32)] + [shape((piece_rows, 128), BF16)] * (chips - 1),
        scratch=(pltpu.VMEM((chips, piece_rows, 128), F32),),
        inputs=samples,
    )(keep, *got)
    got = [send_column(value, k, tiles) for k, value in enumerate(sends, 1)]
    piece = call(sum_kernel, shape((piece_rows, 128), BF16), inputs=chips)(own, *got)
    pieces = jnp.stack([piece] + [send_column(piece, k, tiles) for k in range(1, chips)])
    got = swap_core(pieces, tiles)
    conv_grad, down_grad = call(
        functools.partial(finish_kernel, chips, piece_rows, conv_rows, down_rows),
        (shape((conv_rows, C1), F32), shape((down_rows, C2), F32)),
        scratch=(pltpu.VMEM((tiles, piece_rows, 128), F32),),
        inputs=2,
    )(pieces, got)
    return (down.reshape(1, SX // 2, SY // 2, SZ // 2, C2), conv_grad, down_grad)


def solution(mesh):
    placed = (
        P("sample", "tile", None),
        P("sample", "tile"),
        P("sample", "tile"),
        P(),
        P(),
        P("sample", "tile", None, None, None),
    )
    return jax.shard_map(
        local,
        mesh=mesh,
        in_specs=placed,
        out_specs=(P("sample", "tile", None, None, None), P("sample", None), P("sample", None)),
        check_vma=False,
    )
```

```python
import functools

import jax
import jax.numpy as jnp
from jax import lax
from jax.experimental import pallas as pl
from jax.experimental.pallas import tpu as pltpu
from jax.sharding import PartitionSpec as P

CIN = 64
C1 = 128
C2 = 256
SX = 4
SY = 32
SZ = 8
PTS_DEV = 1024
TAPS = 27
CODED = CIN + 8
LAYER = SZ * SY // 2
BF16 = jnp.bfloat16
F32 = jnp.float32
I32 = jnp.int32
NT = (((1,), (1,)), ((), ()))
TN = (((0,), (0,)), ((), ()))
VMEM_LIMIT = 24 * 1024 * 1024


def in_vmem(count):
    return [pl.BlockSpec(memory_space=pltpu.VMEM)] * count


def call(body, outs, scratch=(), inputs=0):
    single = not isinstance(outs, (list, tuple))
    kernel = pl.pallas_call(
        body,
        out_shape=outs,
        in_specs=in_vmem(inputs),
        out_specs=in_vmem(1)[0] if single else in_vmem(len(outs)),
        scratch_shapes=list(scratch),
        compiler_params=pltpu.CompilerParams(vmem_limit_bytes=VMEM_LIMIT),
    )
    return lambda *args: kernel(*[pltpu.with_memory_space_constraint(a, pltpu.VMEM) for a in args])


def target(index, k, count):
    if count & (count - 1) == 0:
        return index ^ k
    return (index + k) % count


def origin(index, k, count):
    if count & (count - 1) == 0:
        return index ^ k
    return (index - k + count) % count


def swap_core(value, tiles):
    return lax.ppermute(value, "tile", [(i, i ^ 1) for i in range(tiles)])


def send_column(value, k, tiles):
    chips = tiles // 2
    pairs = [(2 * i + c, 2 * target(i, k, chips) + c) for i in range(chips) for c in range(2)]
    return lax.ppermute(value, "tile", pairs)


def send_sample(value, k, samples):
    return lax.ppermute(value, "sample", [(i, target(i, k, samples)) for i in range(samples)])


def encode_kernel(capacity, points_ref, slot_ref, voxel_ref, out_ref):
    slot = slot_ref[...]
    voxel = voxel_ref[...]
    if capacity & (capacity - 1) == 0:
        owner = slot >> (capacity.bit_length() - 1)
    else:
        owner = jnp.floor((slot.astype(F32) + 0.5) * (1.0 / capacity)).astype(I32)
    layer = owner * SX + (voxel >> 8) + 1
    z = voxel & 7
    y = (voxel >> 3) & 31
    place = ((z * 16 + (y >> 1)) << 1) + (y & 1)
    row = lax.broadcasted_iota(I32, (8, slot.shape[1]), 0)
    codes = jnp.where(row == 0, layer, jnp.where(row == 1, place, 0))
    out_ref[0:CIN, :] = points_ref[...]
    out_ref[CIN:CODED, :] = codes.astype(F32).astype(BF16)


def scene_kernel(sources, samples, half_rows, *refs):
    coded = refs[:sources]
    conv_ref, down_ref, cot_ref, out_ref, mine_ref, other_ref, es_ref, pg_ref, wide_ref, tall_ref = refs[sources:]
    tile = lax.axis_index("tile")
    rows = 3 * LAYER
    row_iota = lax.broadcasted_iota(I32, (rows, PTS_DEV), 0)
    small_iota = lax.broadcasted_iota(I32, (32, PTS_DEV), 0)

    grid = jnp.zeros((rows, 4 * CIN), F32)
    counts = jnp.zeros((32, 32), F32)
    for ref in coded:
        codes = ref[CIN:CODED, :].astype(F32).astype(I32)
        layer = codes[0:1, :]
        place = codes[1:2, :]
        pair = (layer >> 1) - 2 * tile
        odd = layer & 1
        spot = place >> 1
        side = place & 1
        hot = (row_iota == pair * LAYER + spot).astype(F32).astype(BF16)
        group = odd * 2 + side
        features = ref[0:CIN, :]
        spread = jnp.concatenate(
            [features * (group == g).astype(F32).astype(BF16) for g in range(4)], axis=0
        )
        grid = grid + lax.dot_general(hot, spread, NT, preferred_element_type=F32)
        plane = (2 * pair + odd - 1) * SZ + (spot >> 4)
        hot_plane = (small_iota == plane).astype(F32).astype(BF16)
        hot_line = (small_iota == (spot & 15) * 2 + side).astype(F32).astype(BF16)
        counts = counts + lax.dot_general(hot_plane, hot_line, NT, preferred_element_type=F32)

    es_ref[...] = jnp.zeros_like(es_ref)
    pg_ref[...] = jnp.zeros_like(pg_ref)
    line = lax.broadcasted_iota(I32, (LAYER, 2 * CIN), 0) & 15
    lane = lax.broadcasted_iota(I32, (LAYER, 2 * CIN), 1)
    for x in range(SX + 2):
        both = grid[(x // 2) * LAYER : (x // 2 + 1) * LAYER, (x % 2) * 128 : (x % 2 + 1) * 128]
        turned = pltpu.roll(both, CIN, 1)
        before = jnp.where(line == 0, 0.0, pltpu.roll(turned, 1, 0))
        after = jnp.where(line == 15, 0.0, pltpu.roll(turned, LAYER - 1, 0))
        sides = jnp.where(lane < CIN, before, after)
        es_ref[x, 1 : SZ + 1, :, 0:128] = both.astype(BF16).reshape(SZ, 16, 128)
        es_ref[x, 1 : SZ + 1, :, 128:256] = sides.astype(BF16).reshape(SZ, 16, 128)

    full = SX * LAYER
    flags = (counts > 0.5).astype(F32).astype(BF16)
    row_plane = lax.broadcasted_iota(I32, (full, 32), 0) >> 4
    pick = (row_plane == lax.broadcasted_iota(I32, (full, 32), 1)).astype(F32).astype(BF16)
    lines = jnp.dot(pick, flags, preferred_element_type=F32)
    row_line = lax.broadcasted_iota(I32, (full, 32), 0) & 15
    lines = jnp.where(row_line == (lax.broadcasted_iota(I32, (full, 32), 1) >> 1), lines, 0.0).astype(BF16)
    expand = (
        (lax.broadcasted_iota(I32, (32, 256), 0) & 1) == (lax.broadcasted_iota(I32, (32, 256), 1) >> 7)
    ).astype(F32).astype(BF16)
    active = jnp.dot(lines, expand, preferred_element_type=F32) > 0.5

    zero_tap = jnp.zeros((CIN, C1), BF16)

    def tap(dx, dy, dz):
        start = ((dx * 3 + dy) * 3 + dz) * CIN
        return conv_ref[start : start + CIN, :]

    pre = jnp.zeros((full, 2 * C1), F32)
    for dx in range(3):
        for dz in range(3):
            weight = jnp.concatenate(
                [
                    jnp.concatenate([tap(dx, 1, dz), tap(dx, 0, dz)], axis=1),
                    jnp.concatenate([tap(dx, 2, dz), tap(dx, 1, dz)], axis=1),
                    jnp.concatenate([tap(dx, 0, dz), zero_tap], axis=1),
                    jnp.concatenate([zero_tap, tap(dx, 2, dz)], axis=1),
                ],
                axis=0,
            )
            part = es_ref[dx : dx + SX, dz : dz + SZ].reshape(full, 4 * CIN)
            pre = pre + jnp.dot(part, weight, preferred_element_type=F32)

    sigmoid = 1.0 / (1.0 + jnp.exp(-pre))
    act = jnp.where(active, pre * sigmoid, 0.0).astype(BF16)
    slope = jnp.where(active, sigmoid * (1.0 + pre * (1.0 - sigmoid)), 0.0)

    act = act.reshape(2, 2, 4, 2, 16, 2 * C1)
    slope = slope.reshape(2, 2, 4, 2, 16, 2 * C1)
    here = lax.broadcasted_iota(I32, (128, 128), 0)
    there = lax.broadcasted_iota(I32, (128, 128), 1)
    turn = ((here >> 6) * 64 + (here & 3) * 16 + ((here >> 2) & 15) == there).astype(F32).astype(BF16)
    cot = lax.dot_general(turn, cot_ref[...], TN, preferred_element_type=F32).astype(BF16)
    down = jnp.zeros((128, C2), F32)
    for ox in range(2):
        for oz in range(2):
            block = act[:, ox, :, oz].reshape(128, 2 * C1)
            first = (ox * 4 + oz) * C1
            second = first + 2 * C1
            weight = jnp.concatenate(
                [down_ref[first : first + C1, :], down_ref[second : second + C1, :]], axis=0
            )
            down = down + jnp.dot(block, weight, preferred_element_type=F32)
            grad = lax.dot_general(block, cot, TN, preferred_element_type=F32)
            wide_ref[first : first + C1, :] = grad[0:C1]
            wide_ref[second : second + C1, :] = grad[C1:]
            back = lax.dot_general(cot, weight, NT, preferred_element_type=F32)
            part = (back * slope[:, ox, :, oz].reshape(128, 2 * C1)).astype(BF16).reshape(2, 4, 16, 2 * C1)
            for u in range(2):
                for w in range(4):
                    pg_ref[2 * u + ox, 1 + 2 * w + oz] = part[u, w]
    out_ref[...] = jnp.dot(turn, down.astype(BF16), preferred_element_type=F32).astype(BF16)

    flipped = es_ref[:, 1 : SZ + 1].reshape((SX + 2) * LAYER, 4 * CIN).T
    for dz in range(3):
        part = pg_ref[:, 2 - dz : 2 - dz + SZ].reshape(full, 2 * C1)
        for dx in range(3):
            grad = jnp.dot(
                flipped[:, dx * LAYER : dx * LAYER + full], part, preferred_element_type=F32
            )
            sums = (
                grad[0:64, 128:256] + grad[128:192, 0:128],
                grad[0:64, 0:128] + grad[64:128, 128:256],
                grad[64:128, 0:128] + grad[192:256, 128:256],
            )
            for dy in range(3):
                start = ((dx * 3 + dy) * 3 + dz) * CIN
                tall_ref[start : start + CIN, :] = sums[dy]

    conv_rows = TAPS * CIN // samples
    down_rows = 8 * C1 // samples
    filler = 2 * half_rows - conv_rows - 2 * down_rows

    def leave(low_ref, high_ref):
        for s in range(samples):
            pieces = [
                tall_ref[s * conv_rows : (s + 1) * conv_rows, :],
                wide_ref[s * down_rows : (s + 1) * down_rows, 0:128],
                wide_ref[s * down_rows : (s + 1) * down_rows, 128:256],
            ]
            if filler:
                pieces.append(jnp.zeros((filler, 128), F32))
            chunk = jnp.concatenate(pieces, axis=0).astype(BF16)
            low_ref[s] = chunk[:half_rows]
            high_ref[s] = chunk[half_rows:]

    core = tile & 1

    @pl.when(core == 0)
    def _():
        leave(mine_ref, other_ref)

    @pl.when(core == 1)
    def _():
        leave(other_ref, mine_ref)


def share_samples_kernel(samples, mine_ref, got_ref, keep_ref, *send_refs):
    me = lax.axis_index("sample")
    keep_ref[...] = mine_ref[me].astype(F32) + got_ref[me].astype(F32)
    for k, ref in enumerate(send_refs, 1):
        to = target(me, k, samples)
        ref[...] = (mine_ref[to].astype(F32) + got_ref[to].astype(F32)).astype(BF16)


def share_column_kernel(samples, chips, rows, keep_ref, *refs):
    got = refs[: samples - 1]
    own_ref = refs[samples - 1]
    sends = refs[samples : samples + chips - 1]
    total_ref = refs[-1]
    total = keep_ref[...]
    for ref in got:
        total = total + ref[...].astype(F32)
    for i in range(chips):
        total_ref[i] = total[i * rows : (i + 1) * rows]
    me = lax.axis_index("tile") >> 1
    own_ref[...] = total_ref[me]
    for k, ref in enumerate(sends, 1):
        ref[...] = total_ref[target(me, k, chips)].astype(BF16)


def sum_kernel(own_ref, *refs):
    total = own_ref[...]
    for ref in refs[:-1]:
        total = total + ref[...].astype(F32)
    refs[-1][...] = total.astype(BF16)


def finish_kernel(chips, rows, conv_rows, down_rows, own_ref, got_ref, conv_ref, down_ref, hold_ref):
    tile = lax.axis_index("tile")
    core = tile & 1
    me = tile >> 1
    for k in range(chips):
        place = origin(me, k, chips)
        hold_ref[core * chips + place] = own_ref[k].astype(F32)
        hold_ref[(1 - core) * chips + place] = got_ref[k].astype(F32)
    whole = jnp.concatenate([hold_ref[i] for i in range(2 * chips)], axis=0)
    conv_ref[...] = whole[:conv_rows]
    down_ref[:, 0:128] = whole[conv_rows : conv_rows + down_rows]
    down_ref[:, 128:256] = whole[conv_rows + down_rows : conv_rows + 2 * down_rows]


def local(points, slot, voxel, conv_weight, down_weight, cotangent):
    tiles = lax.axis_size("tile")
    samples = lax.axis_size("sample")
    chips = tiles // 2
    capacity = 2 * (PTS_DEV // tiles)
    conv_rows = TAPS * CIN // samples
    down_rows = 8 * C1 // samples
    unit = 16 * chips
    total_rows = -(-(conv_rows + 2 * down_rows) // unit) * unit
    half_rows = total_rows // 2
    piece_rows = half_rows // chips

    shape = pltpu.VMEM
    coded = call(functools.partial(encode_kernel, capacity), shape((CODED, PTS_DEV), BF16), inputs=3)(
        points[0].T, slot, voxel
    )
    near = [coded] + [send_column(coded, k, tiles) for k in range(1, chips)]
    gathered = near + [swap_core(value, tiles) for value in near]

    down, mine, other = call(
        functools.partial(scene_kernel, tiles, samples, half_rows),
        (
            shape((128, C2), BF16),
            shape((samples, half_rows, 128), BF16),
            shape((samples, half_rows, 128), BF16),
        ),
        scratch=(
            pltpu.VMEM((SX + 2, SZ + 2, 16, 4 * CIN), BF16),
            pltpu.VMEM((SX, SZ + 2, 16, 2 * C1), BF16),
            pltpu.VMEM((8 * C1, C2), F32),
            pltpu.VMEM((TAPS * CIN, C1), F32),
        ),
        inputs=tiles + 3,
    )(*gathered, conv_weight, down_weight, cotangent.reshape(128, C2))

    got = swap_core(other, tiles)
    keep, *sends = call(
        functools.partial(share_samples_kernel, samples),
        [shape((half_rows, 128), F32)] + [shape((half_rows, 128), BF16)] * (samples - 1),
        inputs=2,
    )(mine, got)
    got = [send_sample(value, k, samples) for k, value in enumerate(sends, 1)]
    own, *sends = call(
        functools.partial(share_column_kernel, samples, chips, piece_rows),
        [shape((piece_rows, 128), F32)] + [shape((piece_rows, 128), BF16)] * (chips - 1),
        scratch=(pltpu.VMEM((chips, piece_rows, 128), F32),),
        inputs=samples,
    )(keep, *got)
    got = [send_column(value, k, tiles) for k, value in enumerate(sends, 1)]
    piece = call(sum_kernel, shape((piece_rows, 128), BF16), inputs=chips)(own, *got)
    pieces = jnp.stack([piece] + [send_column(piece, k, tiles) for k in range(1, chips)])
    got = swap_core(pieces, tiles)
    conv_grad, down_grad = call(
        functools.partial(finish_kernel, chips, piece_rows, conv_rows, down_rows),
        (
            jax.ShapeDtypeStruct((conv_rows, C1), F32),
            jax.ShapeDtypeStruct((down_rows, C2), F32),
        ),
        scratch=(pltpu.VMEM((tiles, piece_rows, 128), F32),),
        inputs=2,
    )(pieces, got)
    return (down.reshape(1, SX // 2, SY // 2, SZ // 2, C2), conv_grad, down_grad)


def solution(mesh):
    placed = (
        P("sample", "tile", None),
        P("sample", "tile"),
        P("sample", "tile"),
        P(),
        P(),
        P("sample", "tile", None, None, None),
    )
    return jax.shard_map(
        local,
        mesh=mesh,
        in_specs=placed,
        out_specs=(P("sample", "tile", None, None, None), P("sample", None), P("sample", None)),
        check_vma=False,
    )
```

```python
import functools

import jax
import jax.numpy as jnp
from jax import lax
from jax.experimental import pallas as pl
from jax.experimental.pallas import tpu as pltpu
from jax.sharding import PartitionSpec as P

CIN = 64
C1 = 128
C2 = 256
SX = 4
SY = 32
SZ = 8
PTS_DEV = 1024
TAPS = 27
CODED = CIN + 8
LAYER = SZ * SY // 2
BF16 = jnp.bfloat16
F32 = jnp.float32
I32 = jnp.int32
NT = (((1,), (1,)), ((), ()))
TN = (((0,), (0,)), ((), ()))
VMEM_LIMIT = 24 * 1024 * 1024


def call(body, outs, scratch=(), pinned=0, loose=0, raw=0):
    single = not isinstance(outs, (list, tuple))
    vmem = pl.BlockSpec(memory_space=pltpu.VMEM)
    kernel = pl.pallas_call(
        body,
        out_shape=outs,
        in_specs=[vmem] * (pinned + loose) + [pl.BlockSpec(memory_space=pl.ANY)] * raw,
        out_specs=vmem if single else [vmem] * len(outs),
        scratch_shapes=list(scratch),
        compiler_params=pltpu.CompilerParams(vmem_limit_bytes=VMEM_LIMIT),
    )

    def run(*args):
        held = [pltpu.with_memory_space_constraint(a, pltpu.VMEM) for a in args[:pinned]]
        return kernel(*held, *args[pinned:])

    return run


def target(index, k, count):
    if count & (count - 1) == 0:
        return index ^ k
    return (index + k) % count


def swap_core(value, tiles):
    return lax.ppermute(value, "tile", [(i, i ^ 1) for i in range(tiles)])


def send_column_by(value, to, tiles):
    pairs = [(2 * i + c, 2 * to(i) + c) for i in range(tiles // 2) for c in range(2)]
    return lax.ppermute(value, "tile", pairs)


def send_column(value, k, tiles):
    return send_column_by(value, lambda i: target(i, k, tiles // 2), tiles)


def send_sample(value, k, samples):
    return lax.ppermute(value, "sample", [(i, target(i, k, samples)) for i in range(samples)])


def encode_kernel(capacity, points_hbm, slot_hbm, voxel_hbm, out_ref, slot_ref, voxel_ref, sems):
    copies = [
        pltpu.make_async_copy(slot_hbm, slot_ref, sems.at[0]),
        pltpu.make_async_copy(voxel_hbm, voxel_ref, sems.at[1]),
        pltpu.make_async_copy(points_hbm, out_ref.at[0:CIN], sems.at[2]),
    ]
    for copy in copies:
        copy.start()
    copies[0].wait()
    copies[1].wait()
    slot = slot_ref[...]
    voxel = voxel_ref[...]
    if capacity & (capacity - 1) == 0:
        owner = slot >> (capacity.bit_length() - 1)
    else:
        owner = jnp.floor((slot.astype(F32) + 0.5) * (1.0 / capacity)).astype(I32)
    layer = owner * SX + (voxel >> 8) + 1
    z = voxel & 7
    y = (voxel >> 3) & 31
    place = ((z * 16 + (y >> 1)) << 1) + (y & 1)
    row = lax.broadcasted_iota(I32, (8, slot.shape[1]), 0)
    codes = jnp.where(row == 0, layer, jnp.where(row == 1, place, 0))
    out_ref[CIN:CODED, :] = codes.astype(F32).astype(BF16)
    copies[2].wait()


def weights_kernel(conv_ref, down_ref, cot_ref, taps_ref, pairs_ref, cot_out_ref, back_ref):
    zero_tap = jnp.zeros((CIN, C1), BF16)

    def tap(dx, dy, dz):
        start = ((dx * 3 + dy) * 3 + dz) * CIN
        return conv_ref[start : start + CIN, :]

    for dx in range(3):
        for dz in range(3):
            taps_ref[dx * 3 + dz] = jnp.concatenate(
                [
                    jnp.concatenate([tap(dx, 1, dz), tap(dx, 0, dz)], axis=1),
                    jnp.concatenate([tap(dx, 2, dz), tap(dx, 1, dz)], axis=1),
                    jnp.concatenate([tap(dx, 0, dz), zero_tap], axis=1),
                    jnp.concatenate([zero_tap, tap(dx, 2, dz)], axis=1),
                ],
                axis=0,
            )
    cot = lax.dot_general(turn_matrix(), cot_ref[...], TN, preferred_element_type=F32).astype(BF16)
    cot_out_ref[...] = cot
    for ox in range(2):
        for oz in range(2):
            first = (ox * 4 + oz) * C1
            second = first + 2 * C1
            weight = jnp.concatenate(
                [down_ref[first : first + C1, :], down_ref[second : second + C1, :]], axis=0
            )
            pairs_ref[ox * 2 + oz] = weight
            back_ref[ox * 2 + oz] = lax.dot_general(cot, weight, NT, preferred_element_type=F32)


def turn_matrix():
    here = lax.broadcasted_iota(I32, (128, 128), 0)
    there = lax.broadcasted_iota(I32, (128, 128), 1)
    return ((here >> 6) * 64 + (here & 3) * 16 + ((here >> 2) & 15) == there).astype(F32).astype(BF16)


def voxelize(refs, grid, counts):
    tile = lax.axis_index("tile")
    row_iota = lax.broadcasted_iota(I32, (3 * LAYER, PTS_DEV), 0)
    small_iota = lax.broadcasted_iota(I32, (32, PTS_DEV), 0)
    for ref in refs:
        codes = ref[CIN:CODED, :].astype(F32).astype(I32)
        layer = codes[0:1, :]
        place = codes[1:2, :]
        pair = (layer >> 1) - 2 * tile
        odd = layer & 1
        spot = place >> 1
        side = place & 1
        hot = (row_iota == pair * LAYER + spot).astype(F32).astype(BF16)
        group = odd * 2 + side
        features = ref[0:CIN, :]
        spread = jnp.concatenate(
            [features * (group == g).astype(F32).astype(BF16) for g in range(4)], axis=0
        )
        part = lax.dot_general(hot, spread, NT, preferred_element_type=F32)
        grid = part if grid is None else grid + part
        plane = (2 * pair + odd - 1) * SZ + (spot >> 4)
        hot_plane = (small_iota == plane).astype(F32).astype(BF16)
        hot_line = (small_iota == (spot & 15) * 2 + side).astype(F32).astype(BF16)
        part = lax.dot_general(hot_plane, hot_line, NT, preferred_element_type=F32)
        counts = part if counts is None else counts + part
    return grid, counts


def first_points_kernel(*refs):
    grid_ref, counts_ref = refs[-2:]
    grid_ref[...], counts_ref[...] = voxelize(refs[:-2], None, None)


def more_points_kernel(old_grid_ref, old_counts_ref, *refs):
    grid_ref, counts_ref = refs[-2:]
    grid_ref[...], counts_ref[...] = voxelize(refs[:-2], old_grid_ref[...], old_counts_ref[...])


def scene_kernel(
    samples, half_rows,
    grid_ref, counts_ref, coded_ref, other_coded_ref, taps_ref, pairs_ref, cot_ref, back_ref,
    out_ref, mine_ref, other_ref, es_ref, pg_ref, wide_ref, tall_ref,
):
    grid, counts = voxelize((coded_ref, other_coded_ref), grid_ref[...], counts_ref[...])

    es_ref[...] = jnp.zeros_like(es_ref)
    pg_ref[...] = jnp.zeros_like(pg_ref)
    line = lax.broadcasted_iota(I32, (LAYER, 2 * CIN), 0) & 15
    lane = lax.broadcasted_iota(I32, (LAYER, 2 * CIN), 1)
    for x in range(SX + 2):
        both = grid[(x // 2) * LAYER : (x // 2 + 1) * LAYER, (x % 2) * 128 : (x % 2 + 1) * 128]
        turned = pltpu.roll(both, CIN, 1)
        before = jnp.where(line == 0, 0.0, pltpu.roll(turned, 1, 0))
        after = jnp.where(line == 15, 0.0, pltpu.roll(turned, LAYER - 1, 0))
        sides = jnp.where(lane < CIN, before, after)
        es_ref[x, 1 : SZ + 1, :, 0:128] = both.astype(BF16).reshape(SZ, 16, 128)
        es_ref[x, 1 : SZ + 1, :, 128:256] = sides.astype(BF16).reshape(SZ, 16, 128)

    full = SX * LAYER
    flags = (counts > 0.5).astype(F32).astype(BF16)
    row_plane = lax.broadcasted_iota(I32, (full, 32), 0) >> 4
    pick = (row_plane == lax.broadcasted_iota(I32, (full, 32), 1)).astype(F32).astype(BF16)
    lines = jnp.dot(pick, flags, preferred_element_type=F32)
    row_line = lax.broadcasted_iota(I32, (full, 32), 0) & 15
    lines = jnp.where(row_line == (lax.broadcasted_iota(I32, (full, 32), 1) >> 1), lines, 0.0).astype(BF16)
    expand = (
        (lax.broadcasted_iota(I32, (32, 256), 0) & 1) == (lax.broadcasted_iota(I32, (32, 256), 1) >> 7)
    ).astype(F32).astype(BF16)
    active = jnp.dot(lines, expand, preferred_element_type=F32) > 0.5

    pre = jnp.zeros((full, 2 * C1), F32)
    for dx in range(3):
        for dz in range(3):
            part = es_ref[dx : dx + SX, dz : dz + SZ].reshape(full, 4 * CIN)
            pre = pre + jnp.dot(part, taps_ref[dx * 3 + dz], preferred_element_type=F32)

    sigmoid = 1.0 / (1.0 + jnp.exp(-pre))
    act = jnp.where(active, pre * sigmoid, 0.0).astype(BF16)
    slope = jnp.where(active, sigmoid * (1.0 + pre * (1.0 - sigmoid)), 0.0)

    act = act.reshape(2, 2, 4, 2, 16, 2 * C1)
    slope = slope.reshape(2, 2, 4, 2, 16, 2 * C1)
    cot = cot_ref[...]
    down = jnp.zeros((128, C2), F32)
    for ox in range(2):
        for oz in range(2):
            block = act[:, ox, :, oz].reshape(128, 2 * C1)
            first = (ox * 4 + oz) * C1
            second = first + 2 * C1
            down = down + jnp.dot(block, pairs_ref[ox * 2 + oz], preferred_element_type=F32)
            grad = lax.dot_general(block, cot, TN, preferred_element_type=F32)
            wide_ref[first : first + C1, :] = grad[0:C1]
            wide_ref[second : second + C1, :] = grad[C1:]
            back = back_ref[ox * 2 + oz]
            part = (back * slope[:, ox, :, oz].reshape(128, 2 * C1)).astype(BF16).reshape(2, 4, 16, 2 * C1)
            for u in range(2):
                for w in range(4):
                    pg_ref[2 * u + ox, 1 + 2 * w + oz] = part[u, w]
    out_ref[...] = jnp.dot(turn_matrix(), down.astype(BF16), preferred_element_type=F32).astype(BF16)

    flipped = es_ref[:, 1 : SZ + 1].reshape((SX + 2) * LAYER, 4 * CIN).T
    for dz in range(3):
        part = pg_ref[:, 2 - dz : 2 - dz + SZ].reshape(full, 2 * C1)
        for dx in range(3):
            grad = jnp.dot(
                flipped[:, dx * LAYER : dx * LAYER + full], part, preferred_element_type=F32
            )
            sums = (
                grad[0:64, 128:256] + grad[128:192, 0:128],
                grad[0:64, 0:128] + grad[64:128, 128:256],
                grad[64:128, 0:128] + grad[192:256, 128:256],
            )
            for dy in range(3):
                start = ((dx * 3 + dy) * 3 + dz) * CIN
                tall_ref[start : start + CIN, :] = sums[dy]

    conv_rows = TAPS * CIN // samples
    down_rows = 8 * C1 // samples
    filler = 2 * half_rows - conv_rows - 2 * down_rows

    def leave(mine_first):
        for s in range(samples):
            pieces = [
                tall_ref[s * conv_rows : (s + 1) * conv_rows, :],
                wide_ref[s * down_rows : (s + 1) * down_rows, 0:128],
                wide_ref[s * down_rows : (s + 1) * down_rows, 128:256],
            ]
            if filler:
                pieces.append(jnp.zeros((filler, 128), F32))
            chunk = jnp.concatenate(pieces, axis=0)
            low, high = chunk[:half_rows], chunk[half_rows:]
            mine, other = (low, high) if mine_first else (high, low)
            mine_ref[s] = mine
            other_ref[s] = other.astype(BF16)

    core = lax.axis_index("tile") & 1

    @pl.when(core == 0)
    def _():
        leave(True)

    @pl.when(core == 1)
    def _():
        leave(False)


def share_samples_kernel(samples, mine_ref, got_ref, keep_ref, *send_refs):
    me = lax.axis_index("sample")
    keep_ref[...] = mine_ref[me] + got_ref[me].astype(F32)
    for k, ref in enumerate(send_refs, 1):
        to = target(me, k, samples)
        ref[...] = (mine_ref[to] + got_ref[to].astype(F32)).astype(BF16)


def sum_kernel(*refs):
    total = refs[0][...].astype(F32)
    for ref in refs[1:-1]:
        total = total + ref[...].astype(F32)
    refs[-1][...] = total.astype(refs[-1].dtype)


def ordered_sum_kernel(block, own_ref, *refs):
    held_ref, out_ref = refs[-1], refs[-2]
    count = len(refs) - 1
    me = (lax.axis_index("tile") >> 1) // block
    held_ref[me] = own_ref[...].astype(F32)
    for j, ref in enumerate(refs[:-2], 1):
        held_ref[(me - j + count) % count] = ref[...].astype(F32)
    total = held_ref[0]
    for i in range(1, count):
        total = total + held_ref[i]
    out_ref[...] = total


def finish_kernel(conv_rows, down_rows, own_ref, got_ref, conv_ref, down_ref):
    first = (lax.axis_index("tile") & 1) == 0
    own = own_ref[...]
    got = got_ref[...]
    whole = jnp.concatenate([jnp.where(first, own, got), jnp.where(first, got, own)], axis=0)
    conv_ref[...] = whole[:conv_rows]
    down_ref[:, 0:128] = whole[conv_rows : conv_rows + down_rows]
    down_ref[:, 128:256] = whole[conv_rows + down_rows : conv_rows + 2 * down_rows]


def local(points, slot, voxel, conv_weight, down_weight, cotangent):
    tiles = lax.axis_size("tile")
    samples = lax.axis_size("sample")
    chips = tiles // 2
    capacity = 2 * (PTS_DEV // tiles)
    conv_rows = TAPS * CIN // samples
    down_rows = 8 * C1 // samples
    half_rows = -(-(conv_rows + 2 * down_rows) // 32) * 16

    hbm = jax.ShapeDtypeStruct
    shape = pltpu.VMEM
    coded = call(
        functools.partial(encode_kernel, capacity),
        shape((CODED, PTS_DEV), BF16),
        scratch=(
            pltpu.VMEM((1, PTS_DEV), I32),
            pltpu.VMEM((1, PTS_DEV), I32),
            pltpu.SemaphoreType.DMA((3,)),
        ),
        raw=3,
    )(points[0].T, slot, voxel)
    near = {0: coded}
    for k in range(1, chips):
        near[k] = send_column(near[2], 1, tiles) if (k == 3 and chips == 4) else send_column(coded, k, tiles)
    pieces = [(value, swap_core(value, tiles)) for value in near.values()]
    taps, pairs, cot, back = call(
        weights_kernel,
        (
            shape((9, 4 * CIN, 2 * C1), BF16),
            shape((4, 2 * C1, C2), BF16),
            shape((128, C2), BF16),
            shape((4, 128, 2 * C1), F32),
        ),
        loose=3,
    )(conv_weight, down_weight, cotangent.reshape(128, C2))
    sums = (shape((3 * LAYER, 4 * CIN), F32), shape((32, 32), F32))
    grid = call(first_points_kernel, sums, pinned=2)(*pieces[0])
    for pair in pieces[1:-1]:
        grid = call(more_points_kernel, sums, pinned=4)(*grid, *pair)

    down, mine, other = call(
        functools.partial(scene_kernel, samples, half_rows),
        (
            shape((128, C2), BF16),
            shape((samples, half_rows, 128), F32),
            shape((samples, half_rows, 128), BF16),
        ),
        scratch=(
            pltpu.VMEM((SX + 2, SZ + 2, 16, 4 * CIN), BF16),
            pltpu.VMEM((SX, SZ + 2, 16, 2 * C1), BF16),
            pltpu.VMEM((8 * C1, C2), F32),
            pltpu.VMEM((TAPS * CIN, C1), F32),
        ),
        pinned=8,
    )(*grid, *pieces[-1], taps, pairs, cot, back)

    got = swap_core(other, tiles)
    keep, *sends = call(
        functools.partial(share_samples_kernel, samples),
        [shape((half_rows, 128), F32)] + [shape((half_rows, 128), BF16)] * (samples - 1),
        pinned=2,
    )(mine, got)
    got = [send_sample(value, k, samples) for k, value in enumerate(sends, 1)]
    block = chips & -chips
    parts = chips // block
    steps = [1 << i for i in range(block.bit_length() - 1)]
    terms = (keep, *got)
    for at, step in enumerate(steps + [0]):
        last = at == len(steps) and parts == 1
        total = call(sum_kernel, shape((half_rows, 128), F32 if last else BF16), pinned=len(terms))(*terms)
        if step:
            terms = (total, send_column_by(total, lambda i: i ^ step, tiles))
    if parts > 1:
        got = [send_column_by(total, lambda i: (i + j * block) % chips, tiles) for j in range(1, parts)]
        total = call(
            functools.partial(ordered_sum_kernel, block),
            shape((half_rows, 128), F32),
            scratch=(pltpu.VMEM((parts, half_rows, 128), F32),),
            pinned=parts,
        )(total, *got)
    conv_grad, down_grad = call(
        functools.partial(finish_kernel, conv_rows, down_rows),
        (hbm((conv_rows, C1), F32), hbm((down_rows, C2), F32)),
        pinned=2,
    )(total, swap_core(total, tiles))
    return (down.reshape(1, SX // 2, SY // 2, SZ // 2, C2), conv_grad, down_grad)


def solution(mesh):
    placed = (
        P("sample", "tile", None),
        P("sample", "tile"),
        P("sample", "tile"),
        P(),
        P(),
        P("sample", "tile", None, None, None),
    )
    return jax.shard_map(
        local,
        mesh=mesh,
        in_specs=placed,
        out_specs=(P("sample", "tile", None, None, None), P("sample", None), P("sample", None)),
        check_vma=False,
    )
```

```python
import functools

import jax
import jax.numpy as jnp
from jax import lax
from jax.experimental import pallas as pl
from jax.experimental.pallas import tpu as pltpu
from jax.sharding import PartitionSpec as P

CIN = 64
C1 = 128
C2 = 256
SX = 4
SY = 32
SZ = 8
PTS_DEV = 1024
TAPS = 27
CODED = CIN + 8
LAYER = SZ * SY // 2
FAR = 3
BLOCK = 4
BF16 = jnp.bfloat16
F32 = jnp.float32
I32 = jnp.int32
NT = (((1,), (1,)), ((), ()))
TN = (((0,), (0,)), ((), ()))
VMEM_LIMIT = 24 * 1024 * 1024


def call(body, outs, scratch=(), pinned=0, loose=0, raw=0):
    single = not isinstance(outs, (list, tuple))
    vmem = pl.BlockSpec(memory_space=pltpu.VMEM)
    kernel = pl.pallas_call(
        body,
        out_shape=outs,
        in_specs=[vmem] * (pinned + loose) + [pl.BlockSpec(memory_space=pltpu.HBM)] * raw,
        out_specs=vmem if single else [vmem] * len(outs),
        scratch_shapes=list(scratch),
        compiler_params=pltpu.CompilerParams(vmem_limit_bytes=VMEM_LIMIT),
    )

    def run(*args):
        held = [pltpu.with_memory_space_constraint(a, pltpu.VMEM) for a in args[:pinned]]
        far = [pltpu.with_memory_space_constraint(a, pltpu.HBM) for a in args[pinned:]]
        return kernel(*held, *far)

    return run


def target(index, k, count):
    if count & (count - 1) == 0:
        return index ^ k
    return (index + k) % count


def swap_core(value, tiles):
    return lax.ppermute(value, "tile", [(i, i ^ 1) for i in range(tiles)])


def send_column(value, to, tiles):
    pairs = [(2 * i + c, 2 * to(i) + c) for i in range(tiles // 2) for c in range(2)]
    return lax.ppermute(value, "tile", pairs)


def send_sample(value, k, samples):
    return lax.ppermute(value, "sample", [(i, target(i, k, samples)) for i in range(samples)])


def encode_kernel(capacity, points_hbm, slot_hbm, voxel_hbm, out_ref, slot_ref, voxel_ref, sems):
    copies = [
        pltpu.make_async_copy(slot_hbm, slot_ref, sems.at[0]),
        pltpu.make_async_copy(voxel_hbm, voxel_ref, sems.at[1]),
        pltpu.make_async_copy(points_hbm, out_ref.at[0:CIN], sems.at[2]),
    ]
    for copy in copies:
        copy.start()
    copies[0].wait()
    copies[1].wait()
    slot = slot_ref[...]
    voxel = voxel_ref[...]
    if capacity & (capacity - 1) == 0:
        owner = slot >> (capacity.bit_length() - 1)
    else:
        owner = jnp.floor((slot.astype(F32) + 0.5) * (1.0 / capacity)).astype(I32)
    layer = owner * SX + (voxel >> 8) + 1
    z = voxel & 7
    y = (voxel >> 3) & 31
    place = ((z * 16 + (y >> 1)) << 1) + (y & 1)
    row = lax.broadcasted_iota(I32, (8, slot.shape[1]), 0)
    codes = jnp.where(row == 0, layer, jnp.where(row == 1, place, 0))
    out_ref[CIN:CODED, :] = codes.astype(F32).astype(BF16)
    copies[2].wait()


def slab_tiles():
    tile = lax.axis_index("tile")
    chip = tile >> 1
    core = tile & 1
    place = (chip >> 1) & 1
    low = jnp.where(place == 0, chip, chip ^ FAR)
    return (2 * low + core, 2 * (low ^ FAR) + core), place


def turn_matrix():
    here = lax.broadcasted_iota(I32, (128, 128), 0)
    there = lax.broadcasted_iota(I32, (128, 128), 1)
    return ((here >> 6) * 64 + (here & 3) * 16 + ((here >> 2) & 15) == there).astype(F32).astype(BF16)


def weights_kernel(conv_ref, down_ref, cot_ref, taps_ref, pairs_ref, turned_ref):
    zero_tap = jnp.zeros((CIN, C1), BF16)

    def tap(dx, dy, dz):
        start = ((dx * 3 + dy) * 3 + dz) * CIN
        return conv_ref[start : start + CIN, :]

    for dx in range(3):
        for dz in range(3):
            taps_ref[dx * 3 + dz] = jnp.concatenate(
                [
                    jnp.concatenate([tap(dx, 1, dz), tap(dx, 0, dz)], axis=1),
                    jnp.concatenate([tap(dx, 2, dz), tap(dx, 1, dz)], axis=1),
                    jnp.concatenate([tap(dx, 0, dz), zero_tap], axis=1),
                    jnp.concatenate([zero_tap, tap(dx, 2, dz)], axis=1),
                ],
                axis=0,
            )
    for ox in range(2):
        for oz in range(2):
            first = (ox * 4 + oz) * C1
            second = first + 2 * C1
            pairs_ref[ox * 2 + oz] = jnp.concatenate(
                [down_ref[first : first + C1, :], down_ref[second : second + C1, :]], axis=0
            )
    turned_ref[...] = lax.dot_general(turn_matrix(), cot_ref[...], TN, preferred_element_type=F32).astype(BF16)


def back_kernel(own_ref, got_ref, pairs_ref, cot_ref, back_ref):
    first = slab_tiles()[1] == 0
    own = own_ref[...].astype(F32)
    got = got_ref[...].astype(F32)
    cot = jnp.concatenate([jnp.where(first, own, got), jnp.where(first, got, own)], axis=0).astype(BF16)
    cot_ref[...] = cot
    for i in range(4):
        back_ref[i] = lax.dot_general(cot, pairs_ref[i], NT, preferred_element_type=F32)


def voxelize(ref):
    codes = ref[CIN:CODED, :].astype(F32).astype(I32)
    layer = codes[0:1, :]
    place = codes[1:2, :]
    odd = layer & 1
    spot = place >> 1
    side = place & 1
    row_iota = lax.broadcasted_iota(I32, (LAYER, PTS_DEV), 0).astype(F32).astype(BF16)
    small_iota = lax.broadcasted_iota(I32, (32, PTS_DEV), 0).astype(F32).astype(BF16)
    one = jnp.ones((), BF16)
    nought = jnp.zeros((), BF16)
    hot = []
    hot_plane = []
    for tile in slab_tiles()[0]:
        pair = (layer >> 1) - 2 * tile
        for p in range(3):
            code = jnp.where(pair == p, spot, 255).astype(F32).astype(BF16)
            hot.append(jnp.where(row_iota == code, one, nought))
        plane = (2 * pair + odd - 1) * SZ + (spot >> 4)
        plane = jnp.where((pair >= 0) & (pair <= 2) & (plane >= 0), plane, 255).astype(F32).astype(BF16)
        hot_plane.append(jnp.where(small_iota == plane, one, nought))
    group = odd * 2 + side
    features = ref[0:CIN, :]
    spread = jnp.concatenate(
        [features * (group == g).astype(F32).astype(BF16) for g in range(4)], axis=0
    )
    grid = lax.dot_general(jnp.concatenate(hot, axis=0), spread, NT, preferred_element_type=F32)
    line = ((spot & 15) * 2 + side).astype(F32).astype(BF16)
    hot_line = jnp.where(small_iota == line, one, nought)
    counts = lax.dot_general(
        jnp.concatenate(hot_plane, axis=0), hot_line, NT, preferred_element_type=F32
    )
    return grid, counts


def first_points_kernel(ref, grid_ref, counts_ref):
    grid_ref[...], counts_ref[...] = voxelize(ref)


def more_points_kernel(old_grid_ref, old_counts_ref, ref, grid_ref, counts_ref):
    grid, counts = voxelize(ref)
    grid_ref[...] = old_grid_ref[...] + grid
    counts_ref[...] = old_counts_ref[...] + counts


def add_grids_kernel(a_ref, a_counts_ref, b_ref, b_counts_ref, grid_ref, counts_ref):
    grid_ref[...] = a_ref[...] + b_ref[...]
    counts_ref[...] = a_counts_ref[...] + b_counts_ref[...]


def scene_kernel(
    samples, half_rows,
    grid_ref, counts_ref, more_grid_ref, more_counts_ref, taps_ref, cot_ref, back_ref,
    act_ref, mine_ref, other_ref, es_ref, pg_ref, wide_ref, tall_ref,
):
    counts = counts_ref[...] + more_counts_ref[...]

    es_ref[...] = jnp.zeros_like(es_ref)
    pg_ref[...] = jnp.zeros_like(pg_ref)
    line = lax.broadcasted_iota(I32, (LAYER, 2 * CIN), 0) & 15
    lane = lax.broadcasted_iota(I32, (LAYER, 2 * CIN), 1)
    for s in range(2):
        for x in range(SX + 2):
            rows = slice((s * 3 + x // 2) * LAYER, (s * 3 + x // 2 + 1) * LAYER)
            lanes = slice((x % 2) * 128, (x % 2 + 1) * 128)
            both = grid_ref[rows, lanes] + more_grid_ref[rows, lanes]
            turned = pltpu.roll(both, CIN, 1)
            before = jnp.where(line == 0, 0.0, pltpu.roll(turned, 1, 0))
            after = jnp.where(line == 15, 0.0, pltpu.roll(turned, LAYER - 1, 0))
            sides = jnp.where(lane < CIN, before, after)
            es_ref[s, x, 1 : SZ + 1, :, 0:128] = both.astype(BF16).reshape(SZ, 16, 128)
            es_ref[s, x, 1 : SZ + 1, :, 128:256] = sides.astype(BF16).reshape(SZ, 16, 128)

    full = 2 * SX * LAYER
    flags = (counts > 0.5).astype(F32).astype(BF16)
    row_plane = lax.broadcasted_iota(I32, (full, 64), 0) >> 4
    pick = (row_plane == lax.broadcasted_iota(I32, (full, 64), 1)).astype(F32).astype(BF16)
    lines = jnp.dot(pick, flags, preferred_element_type=F32)
    row_line = lax.broadcasted_iota(I32, (full, 32), 0) & 15
    lines = jnp.where(row_line == (lax.broadcasted_iota(I32, (full, 32), 1) >> 1), lines, 0.0).astype(BF16)
    expand = (
        (lax.broadcasted_iota(I32, (32, 256), 0) & 1) == (lax.broadcasted_iota(I32, (32, 256), 1) >> 7)
    ).astype(F32).astype(BF16)
    active = jnp.dot(lines, expand, preferred_element_type=F32) > 0.5

    pre = jnp.zeros((full, 2 * C1), F32)
    for dx in range(3):
        for dz in range(3):
            part = es_ref[:, dx : dx + SX, dz : dz + SZ].reshape(full, 4 * CIN)
            pre = pre + jnp.dot(part, taps_ref[dx * 3 + dz], preferred_element_type=F32)

    sigmoid = 1.0 / (1.0 + jnp.exp(-pre))
    act = jnp.where(active, pre * sigmoid, 0.0).astype(BF16)
    slope = jnp.where(active, sigmoid * (1.0 + pre * (1.0 - sigmoid)), 0.0)

    act = act.reshape(2, 2, 2, 4, 2, 16, 2 * C1)
    slope = slope.reshape(2, 2, 2, 4, 2, 16, 2 * C1)
    cot = cot_ref[...]
    for ox in range(2):
        for oz in range(2):
            block = act[:, :, ox, :, oz].reshape(256, 2 * C1)
            act_ref[0, ox * 2 + oz] = block[:128]
            act_ref[1, ox * 2 + oz] = block[128:]
            first = (ox * 4 + oz) * C1
            second = first + 2 * C1
            grad = lax.dot_general(block, cot, TN, preferred_element_type=F32)
            wide_ref[first : first + C1, :] = grad[0:C1]
            wide_ref[second : second + C1, :] = grad[C1:]
            back = back_ref[ox * 2 + oz]
            part = (back * slope[:, :, ox, :, oz].reshape(256, 2 * C1)).astype(BF16)
            part = part.reshape(2, 2, 4, 16, 2 * C1)
            for s in range(2):
                for u in range(2):
                    for w in range(4):
                        pg_ref[s, 2 * u + ox, 1 + 2 * w + oz] = part[s, u, w]

    flipped = es_ref[:, :, 1 : SZ + 1].reshape(2 * (SX + 2) * LAYER, 4 * CIN).T
    half = (SX + 2) * LAYER
    for dx in range(3):
        rows = jnp.concatenate(
            [flipped[:, s * half + dx * LAYER : s * half + (dx + SX) * LAYER] for s in range(2)], axis=1
        )
        for dz in range(3):
            part = pg_ref[:, :, 2 - dz : 2 - dz + SZ].reshape(full, 2 * C1)
            grad = jnp.dot(rows, part, preferred_element_type=F32)
            sums = (
                grad[0:64, 128:256] + grad[128:192, 0:128],
                grad[0:64, 0:128] + grad[64:128, 128:256],
                grad[64:128, 0:128] + grad[192:256, 128:256],
            )
            for dy in range(3):
                start = ((dx * 3 + dy) * 3 + dz) * CIN
                tall_ref[start : start + CIN, :] = sums[dy]

    conv_rows = TAPS * CIN // samples
    down_rows = 8 * C1 // samples
    filler = 2 * half_rows - conv_rows - 2 * down_rows

    def leave(mine_first):
        for s in range(samples):
            pieces = [
                tall_ref[s * conv_rows : (s + 1) * conv_rows, :],
                wide_ref[s * down_rows : (s + 1) * down_rows, 0:128],
                wide_ref[s * down_rows : (s + 1) * down_rows, 128:256],
            ]
            if filler:
                pieces.append(jnp.zeros((filler, 128), F32))
            chunk = jnp.concatenate(pieces, axis=0)
            low, high = chunk[:half_rows], chunk[half_rows:]
            mine, other = (low, high) if mine_first else (high, low)
            mine_ref[s] = mine
            other_ref[s] = other.astype(BF16)

    core = lax.axis_index("tile") & 1

    @pl.when(core == 0)
    def _():
        leave(True)

    @pl.when(core == 1)
    def _():
        leave(False)


def down_kernel(act_ref, pairs_ref, out_ref):
    place = slab_tiles()[1]
    down = jnp.zeros((128, C2), F32)
    for i in range(4):
        down = down + jnp.dot(act_ref[place, i], pairs_ref[i], preferred_element_type=F32)
    out_ref[...] = jnp.dot(turn_matrix(), down.astype(BF16), preferred_element_type=F32).astype(BF16)


def share_samples_kernel(samples, mine_ref, got_ref, keep_ref, *send_refs):
    me = lax.axis_index("sample")
    keep_ref[...] = mine_ref[me] + got_ref[me].astype(F32)
    for k, ref in enumerate(send_refs, 1):
        to = target(me, k, samples)
        ref[...] = (mine_ref[to] + got_ref[to].astype(F32)).astype(BF16)


def sum_kernel(*refs):
    total = refs[0][...].astype(F32)
    for ref in refs[1:-1]:
        total = total + ref[...].astype(F32)
    refs[-1][...] = total.astype(refs[-1].dtype)


def ordered_sum_kernel(own_ref, *refs):
    held_ref, out_ref = refs[-1], refs[-2]
    count = len(refs) - 1
    me = lax.axis_index("tile") // (2 * BLOCK)
    held_ref[me] = own_ref[...].astype(F32)
    for j, ref in enumerate(refs[:-2], 1):
        held_ref[lax.rem(me - j + count, count)] = ref[...].astype(F32)
    total = held_ref[0]
    for i in range(1, count):
        total = total + held_ref[i]
    out_ref[...] = total


def finish_kernel(conv_rows, down_rows, own_ref, got_ref, conv_ref, down_ref):
    first = (lax.axis_index("tile") & 1) == 0
    own = own_ref[...]
    got = got_ref[...]
    whole = jnp.concatenate([jnp.where(first, own, got), jnp.where(first, got, own)], axis=0)
    conv_ref[...] = whole[:conv_rows]
    down_ref[:, 0:128] = whole[conv_rows : conv_rows + down_rows]
    down_ref[:, 128:256] = whole[conv_rows + down_rows : conv_rows + 2 * down_rows]


def local(points, slot, voxel, conv_weight, down_weight, cotangent):
    tiles = lax.axis_size("tile")
    samples = lax.axis_size("sample")
    chips = tiles // 2
    capacity = 2 * (PTS_DEV // tiles)
    conv_rows = TAPS * CIN // samples
    down_rows = 8 * C1 // samples
    half_rows = -(-(conv_rows + 2 * down_rows) // 32) * 16

    hbm = jax.ShapeDtypeStruct
    shape = pltpu.VMEM
    coded = call(
        functools.partial(encode_kernel, capacity),
        shape((CODED, PTS_DEV), BF16),
        scratch=(
            pltpu.VMEM((1, PTS_DEV), I32),
            pltpu.VMEM((1, PTS_DEV), I32),
            pltpu.SemaphoreType.DMA((3,)),
        ),
        raw=3,
    )(points[0].T, slot, voxel)
    blocks = chips // BLOCK

    beyond = send_column(coded, lambda i: i ^ FAR, tiles)
    beside = send_column(coded, lambda i: i ^ 1, tiles)
    coded_swap = swap_core(coded, tiles)
    taps, pairs, cot = call(
        weights_kernel,
        (shape((9, 4 * CIN, 2 * C1), BF16), shape((4, 2 * C1, C2), BF16), shape((128, C2), BF16)),
        loose=3,
    )(conv_weight, down_weight, cotangent.reshape(128, C2))

    sums = (shape((6 * LAYER, 4 * CIN), F32), shape((64, 32), F32))

    def add(grid, piece):
        if grid is None:
            return call(first_points_kernel, sums, pinned=1)(piece)
        return call(more_points_kernel, sums, pinned=3)(*grid, piece)

    grid = add(None, coded)
    beyond, cot, pairs, grid = lax.optimization_barrier((beyond, cot, pairs, grid))
    across = send_column(beyond, lambda i: i ^ 1, tiles)
    cot_got = send_column(cot, lambda i: i ^ FAR, tiles)
    beside_swap = swap_core(beside, tiles)
    beyond_swap = swap_core(beyond, tiles)
    for piece in (coded_swap, beside, beside_swap):
        grid = add(grid, piece)
    more = add(add(None, beyond), beyond_swap)
    for j in range(1, blocks):
        got = [
            send_column(coded, lambda i: (i // BLOCK + j) % blocks * BLOCK + (i % BLOCK ^ m), tiles)
            for m in (0, 1, 3, 2)
        ]
        trees = []
        for first, second in ((got[0], got[1]), (got[2], got[3])):
            tree = None
            for piece in (first, swap_core(first, tiles), second, swap_core(second, tiles)):
                tree = add(tree, piece)
            trees.append(tree)
        both = call(add_grids_kernel, sums, pinned=4)(*trees[0], *trees[1])
        rest = both if j == 1 else call(add_grids_kernel, sums, pinned=4)(*rest, *both)
    cot, back = call(
        back_kernel, (shape((256, C2), BF16), shape((4, 256, 2 * C1), F32)), pinned=3
    )(cot, cot_got, pairs)
    across, grid, more, back = lax.optimization_barrier((across, grid, more, back))
    for piece in (across, swap_core(across, tiles)):
        more = add(more, piece)
    if blocks > 1:
        grid = call(add_grids_kernel, sums, pinned=4)(*grid, *more)
        more = rest

    act, mine, other = call(
        functools.partial(scene_kernel, samples, half_rows),
        (
            shape((2, 4, 128, 2 * C1), BF16),
            shape((samples, half_rows, 128), F32),
            shape((samples, half_rows, 128), BF16),
        ),
        scratch=(
            pltpu.VMEM((2, SX + 2, SZ + 2, 16, 4 * CIN), BF16),
            pltpu.VMEM((2, SX, SZ + 2, 16, 2 * C1), BF16),
            pltpu.VMEM((8 * C1, C2), F32),
            pltpu.VMEM((TAPS * CIN, C1), F32),
        ),
        pinned=7,
    )(*grid, *more, taps, cot, back)

    got = swap_core(other, tiles)
    keep, *sends = call(
        functools.partial(share_samples_kernel, samples),
        [shape((half_rows, 128), F32)] + [shape((half_rows, 128), BF16)] * (samples - 1),
        pinned=2,
    )(mine, got)
    down = call(down_kernel, shape((128, C2), BF16), pinned=2)(act, pairs)
    got = [send_sample(value, k, samples) for k, value in enumerate(sends, 1)]
    total = call(sum_kernel, shape((half_rows, 128), BF16), pinned=samples)(keep, *got)
    got = send_column(total, lambda i: i ^ 1, tiles)
    total = call(sum_kernel, shape((half_rows, 128), F32 if blocks == 1 else BF16), pinned=2)(total, got)
    if blocks > 1:
        got = [send_column(total, lambda i: (i + j * BLOCK) % chips, tiles) for j in range(1, blocks)]
        total = call(
            ordered_sum_kernel,
            shape((half_rows, 128), F32),
            scratch=(pltpu.VMEM((blocks, half_rows, 128), F32),),
            pinned=blocks,
        )(total, *got)
    conv_grad, down_grad = call(
        functools.partial(finish_kernel, conv_rows, down_rows),
        (hbm((conv_rows, C1), F32), hbm((down_rows, C2), F32)),
        pinned=2,
    )(total, swap_core(total, tiles))
    return (down.reshape(1, SX // 2, SY // 2, SZ // 2, C2), conv_grad, down_grad)


def solution(mesh):
    placed = (
        P("sample", "tile", None),
        P("sample", "tile"),
        P("sample", "tile"),
        P(),
        P(),
        P("sample", "tile", None, None, None),
    )
    return jax.shard_map(
        local,
        mesh=mesh,
        in_specs=placed,
        out_specs=(P("sample", "tile", None, None, None), P("sample", None), P("sample", None)),
        check_vma=False,
    )
```

```python
import functools

import jax
import jax.numpy as jnp
from jax import lax
from jax.experimental import pallas as pl
from jax.experimental.pallas import tpu as pltpu
from jax.sharding import PartitionSpec as P

CIN = 64
C1 = 128
C2 = 256
SX = 4
SY = 32
SZ = 8
PTS_DEV = 1024
TAPS = 27
CODED = CIN + 8
LAYER = SZ * SY // 2
FAR = 3
BLOCK = 4
BF16 = jnp.bfloat16
F32 = jnp.float32
I32 = jnp.int32
NT = (((1,), (1,)), ((), ()))
TN = (((0,), (0,)), ((), ()))
VMEM_LIMIT = 24 * 1024 * 1024


def call(body, outs, scratch=(), pinned=0, loose=0, raw=0):
    single = not isinstance(outs, (list, tuple))
    vmem = pl.BlockSpec(memory_space=pltpu.VMEM)
    kernel = pl.pallas_call(
        body,
        out_shape=outs,
        in_specs=[vmem] * (pinned + loose) + [pl.BlockSpec(memory_space=pltpu.HBM)] * raw,
        out_specs=vmem if single else [vmem] * len(outs),
        scratch_shapes=list(scratch),
        compiler_params=pltpu.CompilerParams(vmem_limit_bytes=VMEM_LIMIT),
    )

    def run(*args):
        held = [pltpu.with_memory_space_constraint(a, pltpu.VMEM) for a in args[:pinned]]
        far = [pltpu.with_memory_space_constraint(a, pltpu.HBM) for a in args[pinned:]]
        return kernel(*held, *far)

    return run


def target(index, k, count):
    if count & (count - 1) == 0:
        return index ^ k
    return (index + k) % count


def swap_core(value, tiles):
    return lax.ppermute(value, "tile", [(i, i ^ 1) for i in range(tiles)])


def send_column(value, to, tiles):
    pairs = [(2 * i + c, 2 * to(i) + c) for i in range(tiles // 2) for c in range(2)]
    return lax.ppermute(value, "tile", pairs)


def send_sample(value, k, samples):
    return lax.ppermute(value, "sample", [(i, target(i, k, samples)) for i in range(samples)])


def encode_kernel(capacity, points_hbm, slot_hbm, voxel_hbm, out_ref, slot_ref, voxel_ref, sems):
    copies = [
        pltpu.make_async_copy(slot_hbm, slot_ref, sems.at[0]),
        pltpu.make_async_copy(voxel_hbm, voxel_ref, sems.at[1]),
        pltpu.make_async_copy(points_hbm, out_ref.at[0:CIN], sems.at[2]),
    ]
    for copy in copies:
        copy.start()
    copies[0].wait()
    copies[1].wait()
    slot = slot_ref[...]
    voxel = voxel_ref[...]
    if capacity & (capacity - 1) == 0:
        owner = slot >> (capacity.bit_length() - 1)
    else:
        owner = jnp.floor((slot.astype(F32) + 0.5) * (1.0 / capacity)).astype(I32)
    layer = owner * SX + (voxel >> 8) + 1
    z = voxel & 7
    y = (voxel >> 3) & 31
    place = ((z * 16 + (y >> 1)) << 1) + (y & 1)
    row = lax.broadcasted_iota(I32, (8, slot.shape[1]), 0)
    codes = jnp.where(row == 0, layer, jnp.where(row == 1, place, 0))
    out_ref[CIN:CODED, :] = codes.astype(F32).astype(BF16)
    copies[2].wait()


def slab_tiles():
    tile = lax.axis_index("tile")
    chip = tile >> 1
    core = tile & 1
    place = (chip >> 1) & 1
    low = jnp.where(place == 0, chip, chip ^ FAR)
    return (2 * low + core, 2 * (low ^ FAR) + core), place


def turn_matrix():
    here = lax.broadcasted_iota(I32, (128, 128), 0)
    there = lax.broadcasted_iota(I32, (128, 128), 1)
    return ((here >> 6) * 64 + (here & 3) * 16 + ((here >> 2) & 15) == there).astype(F32).astype(BF16)


def weights_kernel(conv_ref, down_ref, cot_ref, taps_ref, pairs_ref, turned_ref):
    zero_tap = jnp.zeros((CIN, C1), BF16)

    def tap(dx, dy, dz):
        start = ((dx * 3 + dy) * 3 + dz) * CIN
        return conv_ref[start : start + CIN, :]

    for dx in range(3):
        for dz in range(3):
            taps_ref[dx * 3 + dz] = jnp.concatenate(
                [
                    jnp.concatenate([tap(dx, 1, dz), tap(dx, 0, dz)], axis=1),
                    jnp.concatenate([tap(dx, 2, dz), tap(dx, 1, dz)], axis=1),
                    jnp.concatenate([tap(dx, 0, dz), zero_tap], axis=1),
                    jnp.concatenate([zero_tap, tap(dx, 2, dz)], axis=1),
                ],
                axis=0,
            )
    for ox in range(2):
        for oz in range(2):
            first = (ox * 4 + oz) * C1
            second = first + 2 * C1
            pairs_ref[ox * 2 + oz] = jnp.concatenate(
                [down_ref[first : first + C1, :], down_ref[second : second + C1, :]], axis=0
            )
    turned_ref[...] = lax.dot_general(turn_matrix(), cot_ref[...], TN, preferred_element_type=F32).astype(BF16)


def back_kernel(own_ref, got_ref, pairs_ref, cot_ref, back_ref):
    first = slab_tiles()[1] == 0
    own = own_ref[...].astype(F32)
    got = got_ref[...].astype(F32)
    cot = jnp.concatenate([jnp.where(first, own, got), jnp.where(first, got, own)], axis=0).astype(BF16)
    cot_ref[...] = cot
    for i in range(4):
        back_ref[i] = lax.dot_general(cot, pairs_ref[i], NT, preferred_element_type=F32)


def voxelize(ref):
    codes = ref[CIN:CODED, :].astype(F32).astype(I32)
    layer = codes[0:1, :]
    place = codes[1:2, :]
    odd = layer & 1
    spot = place >> 1
    side = place & 1
    row_iota = lax.broadcasted_iota(I32, (LAYER, PTS_DEV), 0).astype(F32).astype(BF16)
    small_iota = lax.broadcasted_iota(I32, (32, PTS_DEV), 0).astype(F32).astype(BF16)
    one = jnp.ones((), BF16)
    nought = jnp.zeros((), BF16)
    hot = []
    hot_plane = []
    for tile in slab_tiles()[0]:
        pair = (layer >> 1) - 2 * tile
        for p in range(3):
            code = jnp.where(pair == p, spot, 255).astype(F32).astype(BF16)
            hot.append(jnp.where(row_iota == code, one, nought))
        plane = (2 * pair + odd - 1) * SZ + (spot >> 4)
        plane = jnp.where((pair >= 0) & (pair <= 2) & (plane >= 0), plane, 255).astype(F32).astype(BF16)
        hot_plane.append(jnp.where(small_iota == plane, one, nought))
    group = odd * 2 + side
    features = ref[0:CIN, :]
    spread = jnp.concatenate(
        [features * (group == g).astype(F32).astype(BF16) for g in range(4)], axis=0
    )
    grid = lax.dot_general(jnp.concatenate(hot, axis=0), spread, NT, preferred_element_type=F32)
    line = ((spot & 15) * 2 + side).astype(F32).astype(BF16)
    hot_line = jnp.where(small_iota == line, one, nought)
    counts = lax.dot_general(
        jnp.concatenate(hot_plane, axis=0), hot_line, NT, preferred_element_type=F32
    )
    return grid, counts


def first_points_kernel(at, ref, grid_ref, counts_ref):
    grid_ref[...], counts_ref[...] = voxelize(ref if at is None else ref.at[at])


def more_points_kernel(at, old_grid_ref, old_counts_ref, ref, grid_ref, counts_ref):
    grid, counts = voxelize(ref if at is None else ref.at[at])
    grid_ref[...] = old_grid_ref[...] + grid
    counts_ref[...] = old_counts_ref[...] + counts


def stack_kernel(*refs):
    for i, ref in enumerate(refs[:-1]):
        refs[-1][i] = ref[...]


def add_grids_kernel(*refs):
    grid_ref, counts_ref = refs[-2:]
    grid_ref[...] = (refs[0][...] + refs[2][...]) + (refs[4][...] + refs[6][...])
    counts_ref[...] = (refs[1][...] + refs[3][...]) + (refs[5][...] + refs[7][...])


def add_two_kernel(a_ref, a_counts_ref, b_ref, b_counts_ref, grid_ref, counts_ref):
    grid_ref[...] = a_ref[...] + b_ref[...]
    counts_ref[...] = a_counts_ref[...] + b_counts_ref[...]


def scene_kernel(
    samples, half_rows,
    grid0, counts0, grid1, counts1, grid2, counts2, grid3, counts3, taps_ref, cot_ref, back_ref,
    act_ref, mine_ref, other_ref, es_ref, pg_ref, wide_ref, tall_ref,
):
    counts = counts0[...] + counts1[...] + counts2[...] + counts3[...]

    es_ref[...] = jnp.zeros_like(es_ref)
    pg_ref[...] = jnp.zeros_like(pg_ref)
    line = lax.broadcasted_iota(I32, (LAYER, 2 * CIN), 0) & 15
    lane = lax.broadcasted_iota(I32, (LAYER, 2 * CIN), 1)
    for s in range(2):
        for x in range(SX + 2):
            rows = slice((s * 3 + x // 2) * LAYER, (s * 3 + x // 2 + 1) * LAYER)
            lanes = slice((x % 2) * 128, (x % 2 + 1) * 128)
            both = (grid0[rows, lanes] + grid1[rows, lanes]) + (grid2[rows, lanes] + grid3[rows, lanes])
            turned = pltpu.roll(both, CIN, 1)
            before = jnp.where(line == 0, 0.0, pltpu.roll(turned, 1, 0))
            after = jnp.where(line == 15, 0.0, pltpu.roll(turned, LAYER - 1, 0))
            sides = jnp.where(lane < CIN, before, after)
            es_ref[s, x, 1 : SZ + 1, :, 0:128] = both.astype(BF16).reshape(SZ, 16, 128)
            es_ref[s, x, 1 : SZ + 1, :, 128:256] = sides.astype(BF16).reshape(SZ, 16, 128)

    full = 2 * SX * LAYER
    flags = (counts > 0.5).astype(F32).astype(BF16)
    row_plane = lax.broadcasted_iota(I32, (full, 64), 0) >> 4
    pick = (row_plane == lax.broadcasted_iota(I32, (full, 64), 1)).astype(F32).astype(BF16)
    lines = jnp.dot(pick, flags, preferred_element_type=F32)
    row_line = lax.broadcasted_iota(I32, (full, 32), 0) & 15
    lines = jnp.where(row_line == (lax.broadcasted_iota(I32, (full, 32), 1) >> 1), lines, 0.0).astype(BF16)
    expand = (
        (lax.broadcasted_iota(I32, (32, 256), 0) & 1) == (lax.broadcasted_iota(I32, (32, 256), 1) >> 7)
    ).astype(F32).astype(BF16)
    active = jnp.dot(lines, expand, preferred_element_type=F32) > 0.5

    pre = jnp.zeros((full, 2 * C1), F32)
    for dx in range(3):
        for dz in range(3):
            part = es_ref[:, dx : dx + SX, dz : dz + SZ].reshape(full, 4 * CIN)
            pre = pre + jnp.dot(part, taps_ref[dx * 3 + dz], preferred_element_type=F32)

    sigmoid = 1.0 / (1.0 + jnp.exp(-pre))
    act = jnp.where(active, pre * sigmoid, 0.0).astype(BF16)
    slope = jnp.where(active, sigmoid * (1.0 + pre * (1.0 - sigmoid)), 0.0)

    act = act.reshape(2, 2, 2, 4, 2, 16, 2 * C1)
    slope = slope.reshape(2, 2, 2, 4, 2, 16, 2 * C1)
    cot = cot_ref[...]
    for ox in range(2):
        for oz in range(2):
            block = act[:, :, ox, :, oz].reshape(256, 2 * C1)
            act_ref[0, ox * 2 + oz] = block[:128]
            act_ref[1, ox * 2 + oz] = block[128:]
            first = (ox * 4 + oz) * C1
            second = first + 2 * C1
            grad = lax.dot_general(block, cot, TN, preferred_element_type=F32)
            wide_ref[first : first + C1, :] = grad[0:C1]
            wide_ref[second : second + C1, :] = grad[C1:]
            back = back_ref[ox * 2 + oz]
            part = (back * slope[:, :, ox, :, oz].reshape(256, 2 * C1)).astype(BF16)
            part = part.reshape(2, 2, 4, 16, 2 * C1)
            for s in range(2):
                for u in range(2):
                    for w in range(4):
                        pg_ref[s, 2 * u + ox, 1 + 2 * w + oz] = part[s, u, w]

    flipped = es_ref[:, :, 1 : SZ + 1].reshape(2 * (SX + 2) * LAYER, 4 * CIN).T
    half = (SX + 2) * LAYER
    for dx in range(3):
        rows = jnp.concatenate(
            [flipped[:, s * half + dx * LAYER : s * half + (dx + SX) * LAYER] for s in range(2)], axis=1
        )
        for dz in range(3):
            part = pg_ref[:, :, 2 - dz : 2 - dz + SZ].reshape(full, 2 * C1)
            grad = jnp.dot(rows, part, preferred_element_type=F32)
            sums = (
                grad[0:64, 128:256] + grad[128:192, 0:128],
                grad[0:64, 0:128] + grad[64:128, 128:256],
                grad[64:128, 0:128] + grad[192:256, 128:256],
            )
            for dy in range(3):
                start = ((dx * 3 + dy) * 3 + dz) * CIN
                tall_ref[start : start + CIN, :] = sums[dy]

    conv_rows = TAPS * CIN // samples
    down_rows = 8 * C1 // samples
    filler = 2 * half_rows - conv_rows - 2 * down_rows

    def leave(mine_first):
        for s in range(samples):
            pieces = [
                tall_ref[s * conv_rows : (s + 1) * conv_rows, :],
                wide_ref[s * down_rows : (s + 1) * down_rows, 0:128],
                wide_ref[s * down_rows : (s + 1) * down_rows, 128:256],
            ]
            if filler:
                pieces.append(jnp.zeros((filler, 128), F32))
            chunk = jnp.concatenate(pieces, axis=0)
            low, high = chunk[:half_rows], chunk[half_rows:]
            mine, other = (low, high) if mine_first else (high, low)
            mine_ref[s] = mine
            other_ref[s] = other.astype(BF16)

    core = lax.axis_index("tile") & 1

    @pl.when(core == 0)
    def _():
        leave(True)

    @pl.when(core == 1)
    def _():
        leave(False)


def down_kernel(act_ref, pairs_ref, out_ref):
    place = slab_tiles()[1]
    down = jnp.zeros((128, C2), F32)
    for i in range(4):
        down = down + jnp.dot(act_ref[place, i], pairs_ref[i], preferred_element_type=F32)
    out_ref[...] = jnp.dot(turn_matrix(), down.astype(BF16), preferred_element_type=F32).astype(BF16)


def share_samples_kernel(samples, mine_ref, got_ref, keep_ref, *send_refs):
    me = lax.axis_index("sample")
    keep_ref[...] = mine_ref[me] + got_ref[me].astype(F32)
    for k, ref in enumerate(send_refs, 1):
        to = target(me, k, samples)
        ref[...] = (mine_ref[to] + got_ref[to].astype(F32)).astype(BF16)


def sum_kernel(*refs):
    total = refs[0][...].astype(F32)
    for ref in refs[1:-1]:
        total = total + ref[...].astype(F32)
    refs[-1][...] = total.astype(refs[-1].dtype)


def ordered_sum_kernel(own_ref, *refs):
    held_ref, out_ref = refs[-1], refs[-2]
    count = len(refs) - 1
    me = lax.axis_index("tile") // (2 * BLOCK)
    held_ref[me] = own_ref[...].astype(F32)
    for j, ref in enumerate(refs[:-2], 1):
        held_ref[lax.rem(me - j + count, count)] = ref[...].astype(F32)
    total = held_ref[0]
    for i in range(1, count):
        total = total + held_ref[i]
    out_ref[...] = total


def finish_kernel(conv_rows, down_rows, own_ref, got_ref, conv_ref, down_ref):
    first = (lax.axis_index("tile") & 1) == 0
    own = own_ref[...]
    got = got_ref[...]
    whole = jnp.concatenate([jnp.where(first, own, got), jnp.where(first, got, own)], axis=0)
    conv_ref[...] = whole[:conv_rows]
    down_ref[:, 0:128] = whole[conv_rows : conv_rows + down_rows]
    down_ref[:, 128:256] = whole[conv_rows + down_rows : conv_rows + 2 * down_rows]


def local(points, slot, voxel, conv_weight, down_weight, cotangent):
    tiles = lax.axis_size("tile")
    samples = lax.axis_size("sample")
    chips = tiles // 2
    capacity = 2 * (PTS_DEV // tiles)
    conv_rows = TAPS * CIN // samples
    down_rows = 8 * C1 // samples
    half_rows = -(-(conv_rows + 2 * down_rows) // 32) * 16

    hbm = jax.ShapeDtypeStruct
    shape = pltpu.VMEM
    coded = call(
        functools.partial(encode_kernel, capacity),
        shape((CODED, PTS_DEV), BF16),
        scratch=(
            pltpu.VMEM((1, PTS_DEV), I32),
            pltpu.VMEM((1, PTS_DEV), I32),
            pltpu.SemaphoreType.DMA((3,)),
        ),
        raw=3,
    )(points[0].T, slot, voxel)
    blocks = chips // BLOCK

    sums = (shape((6 * LAYER, 4 * CIN), F32), shape((64, 32), F32))

    def add(grid, piece, at=None):
        if grid is None:
            return call(functools.partial(first_points_kernel, at), sums, pinned=1)(piece)
        return call(functools.partial(more_points_kernel, at), sums, pinned=3)(*grid, piece)

    beyond = send_column(coded, lambda i: i ^ FAR, tiles)
    own = add(None, coded)
    coded, own = lax.optimization_barrier((coded, own))
    beside = send_column(coded, lambda i: i ^ 1, tiles)
    taps, pairs, cot = call(
        weights_kernel,
        (shape((9, 4 * CIN, 2 * C1), BF16), shape((4, 2 * C1, C2), BF16), shape((128, C2), BF16)),
        loose=3,
    )(conv_weight, down_weight, cotangent.reshape(128, C2))
    beyond, taps, pairs, cot = lax.optimization_barrier((beyond, taps, pairs, cot))
    across = send_column(beyond, lambda i: i ^ 1, tiles)
    far = add(None, beyond)
    coded, beside, beyond, far, cot = lax.optimization_barrier((coded, beside, beyond, far, cot))
    near_swap = swap_core(
        call(stack_kernel, shape((3, CODED, PTS_DEV), BF16), pinned=3)(coded, beside, beyond), tiles
    )
    cot_got = send_column(cot, lambda i: i ^ FAR, tiles)
    own = add(own, beside)
    own_swap = add(add(None, near_swap, 0), near_swap, 1)
    far_swap = add(None, near_swap, 2)
    across, own, own_swap, far_swap, cot_got = lax.optimization_barrier((across, own, own_swap, far_swap, cot_got))
    across_swap = swap_core(across, tiles)
    far = add(far, across)
    cot, back = call(
        back_kernel, (shape((256, C2), BF16), shape((4, 256, 2 * C1), F32)), pinned=3
    )(cot, cot_got, pairs)
    across_swap, far, cot, back = lax.optimization_barrier((across_swap, far, cot, back))
    far_swap = add(far_swap, across_swap)
    grids = [own, own_swap, far, far_swap]
    if blocks > 1:
        rest = call(add_grids_kernel, sums, pinned=8)(*grids[0], *grids[1], *grids[2], *grids[3])
        for j in range(1, blocks):
            got = [
                send_column(coded, lambda i: (i // BLOCK + j) % blocks * BLOCK + (i % BLOCK ^ m), tiles)
                for m in (0, 1, FAR, FAR ^ 1)
            ]
            swapped = [swap_core(piece, tiles) for piece in got]
            trees = [
                add(add(None, first), second)
                for first, second in (got[:2], swapped[:2], got[2:], swapped[2:])
            ]
            both = call(add_grids_kernel, sums, pinned=8)(*trees[0], *trees[1], *trees[2], *trees[3])
            parts = both if j == 1 else call(add_two_kernel, sums, pinned=4)(*parts, *both)
        nothing = (jnp.zeros((6 * LAYER, 4 * CIN), F32), jnp.zeros((64, 32), F32))
        grids = [rest, nothing, parts, nothing]

    act, mine, other = call(
        functools.partial(scene_kernel, samples, half_rows),
        (
            shape((2, 4, 128, 2 * C1), BF16),
            shape((samples, half_rows, 128), F32),
            shape((samples, half_rows, 128), BF16),
        ),
        scratch=(
            pltpu.VMEM((2, SX + 2, SZ + 2, 16, 4 * CIN), BF16),
            pltpu.VMEM((2, SX, SZ + 2, 16, 2 * C1), BF16),
            pltpu.VMEM((8 * C1, C2), F32),
            pltpu.VMEM((TAPS * CIN, C1), F32),
        ),
        pinned=11,
    )(*grids[0], *grids[1], *grids[2], *grids[3], taps, cot, back)

    got = swap_core(other, tiles)
    keep, *sends = call(
        functools.partial(share_samples_kernel, samples),
        [shape((half_rows, 128), F32)] + [shape((half_rows, 128), BF16)] * (samples - 1),
        pinned=2,
    )(mine, got)
    down = call(down_kernel, shape((128, C2), BF16), pinned=2)(act, pairs)
    down = down.reshape(1, SX // 2, SY // 2, SZ // 2, C2)
    got = [send_sample(value, k, samples) for k, value in enumerate(sends, 1)]
    *got, down = lax.optimization_barrier((*got, down))
    total = call(sum_kernel, shape((half_rows, 128), BF16), pinned=samples)(keep, *got)
    got = send_column(total, lambda i: i ^ 1, tiles)
    total = call(sum_kernel, shape((half_rows, 128), F32 if blocks == 1 else BF16), pinned=2)(total, got)
    if blocks > 1:
        got = [send_column(total, lambda i: (i + j * BLOCK) % chips, tiles) for j in range(1, blocks)]
        total = call(
            ordered_sum_kernel,
            shape((half_rows, 128), F32),
            scratch=(pltpu.VMEM((blocks, half_rows, 128), F32),),
            pinned=blocks,
        )(total, *got)
    conv_grad, down_grad = call(
        functools.partial(finish_kernel, conv_rows, down_rows),
        (hbm((conv_rows, C1), F32), hbm((down_rows, C2), F32)),
        pinned=2,
    )(total, swap_core(total, tiles))
    return (down, conv_grad, down_grad)


def solution(mesh):
    placed = (
        P("sample", "tile", None),
        P("sample", "tile"),
        P("sample", "tile"),
        P(),
        P(),
        P("sample", "tile", None, None, None),
    )
    return jax.shard_map(
        local,
        mesh=mesh,
        in_specs=placed,
        out_specs=(P("sample", "tile", None, None, None), P("sample", None), P("sample", None)),
        check_vma=False,
    )
```

```python
import functools

import jax
import jax.numpy as jnp
from jax import lax
from jax.experimental import pallas as pl
from jax.experimental.pallas import tpu as pltpu
from jax.sharding import PartitionSpec as P

CIN = 64
C1 = 128
C2 = 256
SX = 4
SY = 32
SZ = 8
PTS_DEV = 1024
TAPS = 27
CODED = CIN + 8
LAYER = SZ * SY // 2
FAR = 3
BLOCK = 4
BF16 = jnp.bfloat16
F32 = jnp.float32
I32 = jnp.int32
NT = (((1,), (1,)), ((), ()))
TN = (((0,), (0,)), ((), ()))
VMEM_LIMIT = 24 * 1024 * 1024


def call(body, outs, scratch=(), pinned=0, loose=0, raw=0):
    single = not isinstance(outs, (list, tuple))
    vmem = pl.BlockSpec(memory_space=pltpu.VMEM)
    kernel = pl.pallas_call(
        body,
        out_shape=outs,
        in_specs=[vmem] * (pinned + loose) + [pl.BlockSpec(memory_space=pltpu.HBM)] * raw,
        out_specs=vmem if single else [vmem] * len(outs),
        scratch_shapes=list(scratch),
        compiler_params=pltpu.CompilerParams(vmem_limit_bytes=VMEM_LIMIT),
    )

    def run(*args):
        held = [pltpu.with_memory_space_constraint(a, pltpu.VMEM) for a in args[:pinned]]
        far = [pltpu.with_memory_space_constraint(a, pltpu.HBM) for a in args[pinned:]]
        return kernel(*held, *far)

    return run


def target(index, k, count):
    if count & (count - 1) == 0:
        return index ^ k
    return (index + k) % count


def swap_core(value, tiles):
    return lax.ppermute(value, "tile", [(i, i ^ 1) for i in range(tiles)])


def send_column(value, to, tiles):
    pairs = [(2 * i + c, 2 * to(i) + c) for i in range(tiles // 2) for c in range(2)]
    return lax.ppermute(value, "tile", pairs)


def send_sample(value, k, samples):
    return lax.ppermute(value, "sample", [(i, target(i, k, samples)) for i in range(samples)])


def encode_kernel(capacity, points_hbm, slot_hbm, voxel_hbm, out_ref, slot_ref, voxel_ref, sems):
    copies = [
        pltpu.make_async_copy(slot_hbm, slot_ref, sems.at[0]),
        pltpu.make_async_copy(voxel_hbm, voxel_ref, sems.at[1]),
        pltpu.make_async_copy(points_hbm, out_ref.at[0:CIN], sems.at[2]),
    ]
    for copy in copies:
        copy.start()
    copies[0].wait()
    copies[1].wait()
    slot = slot_ref[...]
    voxel = voxel_ref[...]
    if capacity & (capacity - 1) == 0:
        owner = slot >> (capacity.bit_length() - 1)
    else:
        owner = jnp.floor((slot.astype(F32) + 0.5) * (1.0 / capacity)).astype(I32)
    layer = owner * SX + (voxel >> 8) + 1
    z = voxel & 7
    y = (voxel >> 3) & 31
    place = ((z * 16 + (y >> 1)) << 1) + (y & 1)
    row = lax.broadcasted_iota(I32, (8, slot.shape[1]), 0)
    codes = jnp.where(row == 0, layer, jnp.where(row == 1, place, 0))
    out_ref[CIN:CODED, :] = codes.astype(F32).astype(BF16)
    copies[2].wait()


def slab_tiles():
    tile = lax.axis_index("tile")
    chip = tile >> 1
    core = tile & 1
    place = (chip >> 1) & 1
    low = jnp.where(place == 0, chip, chip ^ FAR)
    return (2 * low + core, 2 * (low ^ FAR) + core), place


def turn_matrix():
    here = lax.broadcasted_iota(I32, (128, 128), 0)
    there = lax.broadcasted_iota(I32, (128, 128), 1)
    return ((here >> 6) * 64 + (here & 3) * 16 + ((here >> 2) & 15) == there).astype(F32).astype(BF16)


def weights_kernel(conv_ref, down_ref, cot_ref, taps_ref, pairs_ref, turned_ref):
    zero_tap = jnp.zeros((CIN, C1), BF16)

    def tap(dx, dy, dz):
        start = ((dx * 3 + dy) * 3 + dz) * CIN
        return conv_ref[start : start + CIN, :]

    for dx in range(3):
        for dz in range(3):
            taps_ref[dx * 3 + dz] = jnp.concatenate(
                [
                    jnp.concatenate([tap(dx, 1, dz), tap(dx, 0, dz)], axis=1),
                    jnp.concatenate([tap(dx, 2, dz), tap(dx, 1, dz)], axis=1),
                    jnp.concatenate([tap(dx, 0, dz), zero_tap], axis=1),
                    jnp.concatenate([zero_tap, tap(dx, 2, dz)], axis=1),
                ],
                axis=0,
            )
    for ox in range(2):
        for oz in range(2):
            first = (ox * 4 + oz) * C1
            second = first + 2 * C1
            pairs_ref[ox * 2 + oz] = jnp.concatenate(
                [down_ref[first : first + C1, :], down_ref[second : second + C1, :]], axis=0
            )
    turned_ref[...] = lax.dot_general(turn_matrix(), cot_ref[...], TN, preferred_element_type=F32).astype(BF16)


def back_kernel(own_ref, got_ref, pairs_ref, cot_ref, back_ref):
    first = slab_tiles()[1] == 0
    own = own_ref[...].astype(F32)
    got = got_ref[...].astype(F32)
    cot = jnp.concatenate([jnp.where(first, own, got), jnp.where(first, got, own)], axis=0).astype(BF16)
    cot_ref[...] = cot
    for i in range(4):
        back_ref[i] = lax.dot_general(cot, pairs_ref[i], NT, preferred_element_type=F32)


def voxelize(ref):
    codes = ref[CIN:CODED, :].astype(F32).astype(I32)
    layer = codes[0:1, :]
    place = codes[1:2, :]
    odd = layer & 1
    spot = place >> 1
    side = place & 1
    row_iota = lax.broadcasted_iota(I32, (LAYER, PTS_DEV), 0).astype(F32).astype(BF16)
    small_iota = lax.broadcasted_iota(I32, (32, PTS_DEV), 0).astype(F32).astype(BF16)
    one = jnp.ones((), BF16)
    nought = jnp.zeros((), BF16)
    hot = []
    hot_plane = []
    for tile in slab_tiles()[0]:
        pair = (layer >> 1) - 2 * tile
        for p in range(3):
            code = jnp.where(pair == p, spot, 255).astype(F32).astype(BF16)
            hot.append(jnp.where(row_iota == code, one, nought))
        plane = (2 * pair + odd - 1) * SZ + (spot >> 4)
        plane = jnp.where((pair >= 0) & (pair <= 2) & (plane >= 0), plane, 255).astype(F32).astype(BF16)
        hot_plane.append(jnp.where(small_iota == plane, one, nought))
    group = odd * 2 + side
    features = ref[0:CIN, :]
    spread = jnp.concatenate(
        [features * (group == g).astype(F32).astype(BF16) for g in range(4)], axis=0
    )
    grid = lax.dot_general(jnp.concatenate(hot, axis=0), spread, NT, preferred_element_type=F32)
    line = ((spot & 15) * 2 + side).astype(F32).astype(BF16)
    hot_line = jnp.where(small_iota == line, one, nought)
    counts = lax.dot_general(
        jnp.concatenate(hot_plane, axis=0), hot_line, NT, preferred_element_type=F32
    )
    return grid, counts


def first_points_kernel(at, ref, grid_ref, counts_ref):
    grid_ref[...], counts_ref[...] = voxelize(ref if at is None else ref.at[at])


def more_points_kernel(at, old_grid_ref, old_counts_ref, ref, grid_ref, counts_ref):
    grid, counts = voxelize(ref if at is None else ref.at[at])
    grid_ref[...] = old_grid_ref[...] + grid
    counts_ref[...] = old_counts_ref[...] + counts


def stack_kernel(*refs):
    for i, ref in enumerate(refs[:-1]):
        refs[-1][i] = ref[...]


def add_grids_kernel(*refs):
    grid_ref, counts_ref = refs[-2:]
    grid_ref[...] = (refs[0][...] + refs[2][...]) + (refs[4][...] + refs[6][...])
    counts_ref[...] = (refs[1][...] + refs[3][...]) + (refs[5][...] + refs[7][...])


def add_two_kernel(a_ref, a_counts_ref, b_ref, b_counts_ref, grid_ref, counts_ref):
    grid_ref[...] = a_ref[...] + b_ref[...]
    counts_ref[...] = a_counts_ref[...] + b_counts_ref[...]


def scene_kernel(
    samples,
    grid0, counts0, grid1, counts1, grid2, counts2, grid3, counts3, taps_ref, cot_ref, back_ref,
    act_ref, es_ref, pg_ref, mine_ref, other_ref,
):
    counts = counts0[...] + counts1[...] + counts2[...] + counts3[...]

    es_ref[...] = jnp.zeros_like(es_ref)
    pg_ref[...] = jnp.zeros_like(pg_ref)
    line = lax.broadcasted_iota(I32, (LAYER, 2 * CIN), 0) & 15
    lane = lax.broadcasted_iota(I32, (LAYER, 2 * CIN), 1)
    for s in range(2):
        for x in range(SX + 2):
            rows = slice((s * 3 + x // 2) * LAYER, (s * 3 + x // 2 + 1) * LAYER)
            lanes = slice((x % 2) * 128, (x % 2 + 1) * 128)
            both = (grid0[rows, lanes] + grid1[rows, lanes]) + (grid2[rows, lanes] + grid3[rows, lanes])
            turned = pltpu.roll(both, CIN, 1)
            before = jnp.where(line == 0, 0.0, pltpu.roll(turned, 1, 0))
            after = jnp.where(line == 15, 0.0, pltpu.roll(turned, LAYER - 1, 0))
            sides = jnp.where(lane < CIN, before, after)
            es_ref[s, x, 1 : SZ + 1, :, 0:128] = both.astype(BF16).reshape(SZ, 16, 128)
            es_ref[s, x, 1 : SZ + 1, :, 128:256] = sides.astype(BF16).reshape(SZ, 16, 128)

    full = 2 * SX * LAYER
    flags = (counts > 0.5).astype(F32).astype(BF16)
    row_plane = lax.broadcasted_iota(I32, (full, 64), 0) >> 4
    pick = (row_plane == lax.broadcasted_iota(I32, (full, 64), 1)).astype(F32).astype(BF16)
    lines = jnp.dot(pick, flags, preferred_element_type=F32)
    row_line = lax.broadcasted_iota(I32, (full, 32), 0) & 15
    lines = jnp.where(row_line == (lax.broadcasted_iota(I32, (full, 32), 1) >> 1), lines, 0.0).astype(BF16)
    expand = (
        (lax.broadcasted_iota(I32, (32, 256), 0) & 1) == (lax.broadcasted_iota(I32, (32, 256), 1) >> 7)
    ).astype(F32).astype(BF16)
    active = jnp.dot(lines, expand, preferred_element_type=F32) > 0.5

    pre = jnp.zeros((full, 2 * C1), F32)
    for dx in range(3):
        for dz in range(3):
            part = es_ref[:, dx : dx + SX, dz : dz + SZ].reshape(full, 4 * CIN)
            pre = pre + jnp.dot(part, taps_ref[dx * 3 + dz], preferred_element_type=F32)

    sigmoid = 1.0 / (1.0 + jnp.exp(-pre))
    act = jnp.where(active, pre * sigmoid, 0.0).astype(BF16)
    slope = jnp.where(active, sigmoid * (1.0 + pre * (1.0 - sigmoid)), 0.0)

    act = act.reshape(2, 2, 2, 4, 2, 16, 2 * C1)
    slope = slope.reshape(2, 2, 2, 4, 2, 16, 2 * C1)
    cot = cot_ref[...]
    low = (lax.axis_index("tile") & 1) == 0
    down_rows = 8 * C1 // samples
    step = min(C1, down_rows)
    for ox in range(2):
        for oz in range(2):
            block = act[:, :, ox, :, oz].reshape(256, 2 * C1)
            act_ref[0, ox * 2 + oz] = block[:128]
            act_ref[1, ox * 2 + oz] = block[128:]
            grad = lax.dot_general(block, cot, TN, preferred_element_type=F32)
            for p in range(2):
                for i in range(0, C1, step):
                    chunk, row = divmod((ox * 4 + p * 2 + oz) * C1 + i, down_rows)
                    left = grad[p * C1 + i : p * C1 + i + step, 0:128]
                    right = grad[p * C1 + i : p * C1 + i + step, 128:256]
                    mine_ref[chunk, row : row + step, :] = jnp.where(low, left, right)
                    other_ref[chunk, row : row + step, :] = jnp.where(low, right, left).astype(BF16)
            back = back_ref[ox * 2 + oz]
            part = (back * slope[:, :, ox, :, oz].reshape(256, 2 * C1)).astype(BF16)
            part = part.reshape(2, 2, 4, 16, 2 * C1)
            for s in range(2):
                for u in range(2):
                    for w in range(4):
                        pg_ref[s, 2 * u + ox, 1 + 2 * w + oz] = part[s, u, w]


def conv_grad_kernel(samples, half_rows, es_ref, pg_ref, mine_ref, other_ref, tall_ref):
    full = 2 * SX * LAYER
    flipped = es_ref[:, :, 1 : SZ + 1].reshape(2 * (SX + 2) * LAYER, 4 * CIN).T
    half = (SX + 2) * LAYER
    for dx in range(3):
        rows = jnp.concatenate(
            [flipped[:, s * half + dx * LAYER : s * half + (dx + SX) * LAYER] for s in range(2)], axis=1
        )
        for dz in range(3):
            part = pg_ref[:, :, 2 - dz : 2 - dz + SZ].reshape(full, 2 * C1)
            grad = jnp.dot(rows, part, preferred_element_type=F32)
            sums = (
                grad[0:64, 128:256] + grad[128:192, 0:128],
                grad[0:64, 0:128] + grad[64:128, 128:256],
                grad[64:128, 0:128] + grad[192:256, 128:256],
            )
            for dy in range(3):
                start = ((dx * 3 + dy) * 3 + dz) * CIN
                tall_ref[start : start + CIN, :] = sums[dy]

    conv_rows = TAPS * CIN // samples
    filler = 2 * half_rows - conv_rows
    low = (lax.axis_index("tile") & 1) == 0
    for s in range(samples):
        first = tall_ref[s * conv_rows : s * conv_rows + half_rows, :]
        second = tall_ref[s * conv_rows + half_rows : (s + 1) * conv_rows, :]
        if filler:
            second = jnp.concatenate([second, jnp.zeros((filler, C1), F32)], axis=0)
        mine_ref[s] = jnp.where(low, first, second)
        other_ref[s] = jnp.where(low, second, first).astype(BF16)


def down_kernel(act_ref, pairs_ref, out_ref):
    place = slab_tiles()[1]
    down = jnp.zeros((128, C2), F32)
    for i in range(4):
        down = down + jnp.dot(act_ref[place, i], pairs_ref[i], preferred_element_type=F32)
    out_ref[...] = jnp.dot(turn_matrix(), down.astype(BF16), preferred_element_type=F32).astype(BF16)


def share_samples_kernel(samples, mine_ref, got_ref, mine_conv_ref, got_conv_ref, keep_ref, *send_refs):
    me = lax.axis_index("sample")
    rows = mine_ref.shape[1]
    for k, ref in enumerate((keep_ref, *send_refs)):
        to = target(me, k, samples) if k else me
        ref[:rows] = (mine_ref[to] + got_ref[to].astype(F32)).astype(ref.dtype)
        ref[rows:] = (mine_conv_ref[to] + got_conv_ref[to].astype(F32)).astype(ref.dtype)


def sum_kernel(*refs):
    total = refs[0][...].astype(F32)
    for ref in refs[1:-1]:
        total = total + ref[...].astype(F32)
    refs[-1][...] = total.astype(refs[-1].dtype)


def ordered_sum_kernel(own_ref, *refs):
    held_ref, out_ref = refs[-1], refs[-2]
    count = len(refs) - 1
    me = lax.axis_index("tile") // (2 * BLOCK)
    held_ref[me] = own_ref[...].astype(F32)
    for j, ref in enumerate(refs[:-2], 1):
        held_ref[lax.rem(me - j + count, count)] = ref[...].astype(F32)
    total = held_ref[0]
    for i in range(1, count):
        total = total + held_ref[i]
    out_ref[...] = total


def finish_kernel(down_rows, own_ref, got_ref, conv_ref, down_ref):
    low = (lax.axis_index("tile") & 1) == 0
    own = own_ref[...]
    got = got_ref[...]
    first = jnp.where(low, own, got)
    second = jnp.where(low, got, own)
    half_rows = first.shape[0] - down_rows
    down_ref[:, 0:128] = first[:down_rows]
    down_ref[:, 128:256] = second[:down_rows]
    conv_ref[0:half_rows, :] = first[down_rows:]
    conv_ref[half_rows:, :] = second[down_rows : down_rows + conv_ref.shape[0] - half_rows]


def local(points, slot, voxel, conv_weight, down_weight, cotangent):
    tiles = lax.axis_size("tile")
    samples = lax.axis_size("sample")
    chips = tiles // 2
    capacity = 2 * (PTS_DEV // tiles)
    conv_rows = TAPS * CIN // samples
    down_rows = 8 * C1 // samples
    half_rows = -(-conv_rows // 32) * 16

    hbm = jax.ShapeDtypeStruct
    shape = pltpu.VMEM
    coded = call(
        functools.partial(encode_kernel, capacity),
        shape((CODED, PTS_DEV), BF16),
        scratch=(
            pltpu.VMEM((1, PTS_DEV), I32),
            pltpu.VMEM((1, PTS_DEV), I32),
            pltpu.SemaphoreType.DMA((3,)),
        ),
        raw=3,
    )(points[0].T, slot, voxel)
    blocks = chips // BLOCK

    sums = (shape((6 * LAYER, 4 * CIN), F32), shape((64, 32), F32))

    def add(grid, piece, at=None):
        if grid is None:
            return call(functools.partial(first_points_kernel, at), sums, pinned=1)(piece)
        return call(functools.partial(more_points_kernel, at), sums, pinned=3)(*grid, piece)

    beyond = send_column(coded, lambda i: i ^ FAR, tiles)
    own = add(None, coded)
    coded, own = lax.optimization_barrier((coded, own))
    beside = send_column(coded, lambda i: i ^ 1, tiles)
    taps, pairs, cot = call(
        weights_kernel,
        (shape((9, 4 * CIN, 2 * C1), BF16), shape((4, 2 * C1, C2), BF16), shape((128, C2), BF16)),
        loose=3,
    )(conv_weight, down_weight, cotangent.reshape(128, C2))
    beyond, taps, pairs, cot = lax.optimization_barrier((beyond, taps, pairs, cot))
    across = send_column(beyond, lambda i: i ^ 1, tiles)
    far = add(None, beyond)
    coded, beside, beyond, far, cot = lax.optimization_barrier((coded, beside, beyond, far, cot))
    near_swap = swap_core(
        call(stack_kernel, shape((3, CODED, PTS_DEV), BF16), pinned=3)(coded, beside, beyond), tiles
    )
    cot_got = send_column(cot, lambda i: i ^ FAR, tiles)
    own = add(own, beside)
    own_swap = add(add(None, near_swap, 0), near_swap, 1)
    far_swap = add(None, near_swap, 2)
    across, own, own_swap, far_swap, cot_got = lax.optimization_barrier((across, own, own_swap, far_swap, cot_got))
    across_swap = swap_core(across, tiles)
    far = add(far, across)
    cot, back = call(
        back_kernel, (shape((256, C2), BF16), shape((4, 256, 2 * C1), F32)), pinned=3
    )(cot, cot_got, pairs)
    across_swap, far, cot, back = lax.optimization_barrier((across_swap, far, cot, back))
    far_swap = add(far_swap, across_swap)
    grids = [own, own_swap, far, far_swap]
    if blocks > 1:
        rest = call(add_grids_kernel, sums, pinned=8)(*grids[0], *grids[1], *grids[2], *grids[3])
        for j in range(1, blocks):
            got = [
                send_column(coded, lambda i: (i // BLOCK + j) % blocks * BLOCK + (i % BLOCK ^ m), tiles)
                for m in (0, 1, FAR, FAR ^ 1)
            ]
            swapped = [swap_core(piece, tiles) for piece in got]
            trees = [
                add(add(None, first), second)
                for first, second in (got[:2], swapped[:2], got[2:], swapped[2:])
            ]
            both = call(add_grids_kernel, sums, pinned=8)(*trees[0], *trees[1], *trees[2], *trees[3])
            parts = both if j == 1 else call(add_two_kernel, sums, pinned=4)(*parts, *both)
        nothing = (jnp.zeros((6 * LAYER, 4 * CIN), F32), jnp.zeros((64, 32), F32))
        grids = [rest, nothing, parts, nothing]

    act, es, pg, mine, other = call(
        functools.partial(scene_kernel, samples),
        (
            shape((2, 4, 128, 2 * C1), BF16),
            shape((2, SX + 2, SZ + 2, 16, 4 * CIN), BF16),
            shape((2, SX, SZ + 2, 16, 2 * C1), BF16),
            shape((samples, down_rows, 128), F32),
            shape((samples, down_rows, 128), BF16),
        ),
        pinned=11,
    )(*grids[0], *grids[1], *grids[2], *grids[3], taps, cot, back)

    got = swap_core(other, tiles)
    mine_conv, other_conv = call(
        functools.partial(conv_grad_kernel, samples, half_rows),
        (shape((samples, half_rows, C1), F32), shape((samples, half_rows, C1), BF16)),
        scratch=(pltpu.VMEM((TAPS * CIN, C1), F32),),
        pinned=2,
    )(es, pg)
    got, mine_conv, other_conv = lax.optimization_barrier((got, mine_conv, other_conv))
    sum_rows = down_rows + half_rows
    keep, *sends = call(
        functools.partial(share_samples_kernel, samples),
        [shape((sum_rows, 128), F32)] + [shape((sum_rows, 128), BF16)] * (samples - 1),
        pinned=4,
    )(mine, got, mine_conv, swap_core(other_conv, tiles))
    terms = [keep] + [send_sample(value, k, samples) for k, value in enumerate(sends, 1)]
    down = call(down_kernel, shape((128, C2), BF16), pinned=2)(act, pairs)
    down = down.reshape(1, SX // 2, SY // 2, SZ // 2, C2)
    *terms, down = lax.optimization_barrier((*terms, down))
    total = call(sum_kernel, shape((sum_rows, 128), BF16), pinned=samples)(*terms)
    got = send_column(total, lambda i: i ^ 1, tiles)
    total = call(sum_kernel, shape((sum_rows, 128), F32 if blocks == 1 else BF16), pinned=2)(total, got)
    if blocks > 1:
        got = [send_column(total, lambda i: (i + j * BLOCK) % chips, tiles) for j in range(1, blocks)]
        total = call(
            ordered_sum_kernel,
            shape((sum_rows, 128), F32),
            scratch=(pltpu.VMEM((blocks, sum_rows, 128), F32),),
            pinned=blocks,
        )(total, *got)
    conv_grad, down_grad = call(
        functools.partial(finish_kernel, down_rows),
        (hbm((conv_rows, C1), F32), hbm((down_rows, C2), F32)),
        pinned=2,
    )(total, swap_core(total, tiles))
    return (down, conv_grad, down_grad)


def solution(mesh):
    placed = (
        P("sample", "tile", None),
        P("sample", "tile"),
        P("sample", "tile"),
        P(),
        P(),
        P("sample", "tile", None, None, None),
    )
    return jax.shard_map(
        local,
        mesh=mesh,
        in_specs=placed,
        out_specs=(P("sample", "tile", None, None, None), P("sample", None), P("sample", None)),
        check_vma=False,
    )
```

```python
import functools

import jax
import jax.numpy as jnp
from jax import lax
from jax.experimental import pallas as pl
from jax.experimental.pallas import tpu as pltpu
from jax.sharding import PartitionSpec as P

CIN = 64
C1 = 128
C2 = 256
SX = 4
SY = 32
SZ = 8
PTS_DEV = 1024
TAPS = 27
CODED = CIN + 8
LAYER = SZ * SY // 2
FAR = 3
BLOCK = 4
BF16 = jnp.bfloat16
F32 = jnp.float32
I32 = jnp.int32
NT = (((1,), (1,)), ((), ()))
TN = (((0,), (0,)), ((), ()))
VMEM_LIMIT = 24 * 1024 * 1024


def call(body, outs, scratch=(), pinned=0, loose=0, raw=0):
    single = not isinstance(outs, (list, tuple))
    vmem = pl.BlockSpec(memory_space=pltpu.VMEM)
    kernel = pl.pallas_call(
        body,
        out_shape=outs,
        in_specs=[vmem] * (pinned + loose) + [pl.BlockSpec(memory_space=pltpu.HBM)] * raw,
        out_specs=vmem if single else [vmem] * len(outs),
        scratch_shapes=list(scratch),
        compiler_params=pltpu.CompilerParams(vmem_limit_bytes=VMEM_LIMIT),
    )

    def run(*args):
        held = [pltpu.with_memory_space_constraint(a, pltpu.VMEM) for a in args[:pinned]]
        far = [pltpu.with_memory_space_constraint(a, pltpu.HBM) for a in args[pinned:]]
        return kernel(*held, *far)

    return run


def target(index, k, count):
    if count & (count - 1) == 0:
        return index ^ k
    return (index + k) % count


def swap_core(value, tiles):
    return lax.ppermute(value, "tile", [(i, i ^ 1) for i in range(tiles)])


def send_column(value, to, tiles):
    pairs = [(2 * i + c, 2 * to(i) + c) for i in range(tiles // 2) for c in range(2)]
    return lax.ppermute(value, "tile", pairs)


def send_sample(value, k, samples):
    return lax.ppermute(value, "sample", [(i, target(i, k, samples)) for i in range(samples)])


def encode_kernel(capacity, points_hbm, slot_hbm, voxel_hbm, out_ref, slot_ref, voxel_ref, sems):
    copies = [
        pltpu.make_async_copy(slot_hbm, slot_ref, sems.at[0]),
        pltpu.make_async_copy(voxel_hbm, voxel_ref, sems.at[1]),
        pltpu.make_async_copy(points_hbm, out_ref.at[0:CIN], sems.at[2]),
    ]
    for copy in copies:
        copy.start()
    copies[0].wait()
    copies[1].wait()
    slot = slot_ref[...]
    voxel = voxel_ref[...]
    if capacity & (capacity - 1) == 0:
        owner = slot >> (capacity.bit_length() - 1)
    else:
        owner = jnp.floor((slot.astype(F32) + 0.5) * (1.0 / capacity)).astype(I32)
    layer = owner * SX + (voxel >> 8) + 1
    z = voxel & 7
    y = (voxel >> 3) & 31
    place = ((z * 16 + (y >> 1)) << 1) + (y & 1)
    row = lax.broadcasted_iota(I32, (8, slot.shape[1]), 0)
    codes = jnp.where(row == 0, layer, jnp.where(row == 1, place, 0))
    out_ref[CIN:CODED, :] = codes.astype(F32).astype(BF16)
    copies[2].wait()


def slab_tiles():
    tile = lax.axis_index("tile")
    chip = tile >> 1
    core = tile & 1
    place = (chip >> 1) & 1
    low = jnp.where(place == 0, chip, chip ^ FAR)
    return (2 * low + core, 2 * (low ^ FAR) + core), place


def turn_matrix():
    here = lax.broadcasted_iota(I32, (128, 128), 0)
    there = lax.broadcasted_iota(I32, (128, 128), 1)
    return ((here >> 6) * 64 + (here & 3) * 16 + ((here >> 2) & 15) == there).astype(F32).astype(BF16)


def weights_kernel(conv_ref, down_ref, cot_ref, taps_ref, pairs_ref, turned_ref):
    zero_tap = jnp.zeros((CIN, C1), BF16)

    def tap(dx, dy, dz):
        start = ((dx * 3 + dy) * 3 + dz) * CIN
        return conv_ref[start : start + CIN, :]

    for dx in range(3):
        for dz in range(3):
            taps_ref[dx * 3 + dz] = jnp.concatenate(
                [
                    jnp.concatenate([tap(dx, 1, dz), tap(dx, 0, dz)], axis=1),
                    jnp.concatenate([tap(dx, 2, dz), tap(dx, 1, dz)], axis=1),
                    jnp.concatenate([tap(dx, 0, dz), zero_tap], axis=1),
                    jnp.concatenate([zero_tap, tap(dx, 2, dz)], axis=1),
                ],
                axis=0,
            )
    for ox in range(2):
        for oz in range(2):
            first = (ox * 4 + oz) * C1
            second = first + 2 * C1
            pairs_ref[ox * 2 + oz] = jnp.concatenate(
                [down_ref[first : first + C1, :], down_ref[second : second + C1, :]], axis=0
            )
    turned_ref[...] = lax.dot_general(turn_matrix(), cot_ref[...], TN, preferred_element_type=F32).astype(BF16)


def voxelize(ref):
    codes = ref[CIN:CODED, :].astype(F32).astype(I32)
    layer = codes[0:1, :]
    place = codes[1:2, :]
    odd = layer & 1
    spot = place >> 1
    side = place & 1
    row_iota = lax.broadcasted_iota(I32, (LAYER, PTS_DEV), 0).astype(F32).astype(BF16)
    small_iota = lax.broadcasted_iota(I32, (32, PTS_DEV), 0).astype(F32).astype(BF16)
    one = jnp.ones((), BF16)
    nought = jnp.zeros((), BF16)
    hot = []
    hot_plane = []
    for tile in slab_tiles()[0]:
        pair = (layer >> 1) - 2 * tile
        for p in range(3):
            code = jnp.where(pair == p, spot, 255).astype(F32).astype(BF16)
            hot.append(jnp.where(row_iota == code, one, nought))
        plane = (2 * pair + odd - 1) * SZ + (spot >> 4)
        plane = jnp.where((pair >= 0) & (pair <= 2) & (plane >= 0), plane, 255).astype(F32).astype(BF16)
        hot_plane.append(jnp.where(small_iota == plane, one, nought))
    group = odd * 2 + side
    features = ref[0:CIN, :]
    spread = jnp.concatenate(
        [features * (group == g).astype(F32).astype(BF16) for g in range(4)], axis=0
    )
    grid = lax.dot_general(jnp.concatenate(hot, axis=0), spread, NT, preferred_element_type=F32)
    line = ((spot & 15) * 2 + side).astype(F32).astype(BF16)
    hot_line = jnp.where(small_iota == line, one, nought)
    counts = lax.dot_general(
        jnp.concatenate(hot_plane, axis=0), hot_line, NT, preferred_element_type=F32
    )
    return grid, counts


def first_points_kernel(at, ref, grid_ref, counts_ref):
    grid_ref[...], counts_ref[...] = voxelize(ref if at is None else ref.at[at])


def more_points_kernel(at, old_grid_ref, old_counts_ref, ref, grid_ref, counts_ref):
    grid, counts = voxelize(ref if at is None else ref.at[at])
    grid_ref[...] = old_grid_ref[...] + grid
    counts_ref[...] = old_counts_ref[...] + counts


def stack_kernel(*refs):
    for i, ref in enumerate(refs[:-1]):
        refs[-1][i] = ref[...]


def add_grids_kernel(*refs):
    grid_ref, counts_ref = refs[-2:]
    grid_ref[...] = (refs[0][...] + refs[2][...]) + (refs[4][...] + refs[6][...])
    counts_ref[...] = (refs[1][...] + refs[3][...]) + (refs[5][...] + refs[7][...])


def add_two_kernel(a_ref, a_counts_ref, b_ref, b_counts_ref, grid_ref, counts_ref):
    grid_ref[...] = a_ref[...] + b_ref[...]
    counts_ref[...] = a_counts_ref[...] + b_counts_ref[...]


def scene_kernel(
    grid0, counts0, grid1, counts1, grid2, counts2, grid3, counts3, taps_ref,
    act_ref, slope_ref, es_ref,
):
    counts = counts0[...] + counts1[...] + counts2[...] + counts3[...]

    edge = jnp.zeros((2, SX + 2, 1, 16, 4 * CIN), BF16)
    es_ref[:, :, 0:1] = edge
    es_ref[:, :, SZ + 1 : SZ + 2] = edge
    line = lax.broadcasted_iota(I32, (LAYER, 2 * CIN), 0) & 15
    lane = lax.broadcasted_iota(I32, (LAYER, 2 * CIN), 1)
    for s in range(2):
        for x in range(SX + 2):
            rows = slice((s * 3 + x // 2) * LAYER, (s * 3 + x // 2 + 1) * LAYER)
            lanes = slice((x % 2) * 128, (x % 2 + 1) * 128)
            both = (grid0[rows, lanes] + grid1[rows, lanes]) + (grid2[rows, lanes] + grid3[rows, lanes])
            turned = pltpu.roll(both, CIN, 1)
            before = jnp.where(line == 0, 0.0, pltpu.roll(turned, 1, 0))
            after = jnp.where(line == 15, 0.0, pltpu.roll(turned, LAYER - 1, 0))
            sides = jnp.where(lane < CIN, before, after)
            es_ref[s, x, 1 : SZ + 1, :, 0:128] = both.astype(BF16).reshape(SZ, 16, 128)
            es_ref[s, x, 1 : SZ + 1, :, 128:256] = sides.astype(BF16).reshape(SZ, 16, 128)

    full = 2 * SX * LAYER
    flags = (counts > 0.5).astype(F32).astype(BF16)
    row_plane = lax.broadcasted_iota(I32, (full, 64), 0) >> 4
    pick = (row_plane == lax.broadcasted_iota(I32, (full, 64), 1)).astype(F32).astype(BF16)
    lines = jnp.dot(pick, flags, preferred_element_type=F32)
    row_line = lax.broadcasted_iota(I32, (full, 32), 0) & 15
    lines = jnp.where(row_line == (lax.broadcasted_iota(I32, (full, 32), 1) >> 1), lines, 0.0).astype(BF16)
    expand = (
        (lax.broadcasted_iota(I32, (32, 256), 0) & 1) == (lax.broadcasted_iota(I32, (32, 256), 1) >> 7)
    ).astype(F32).astype(BF16)
    active = jnp.dot(lines, expand, preferred_element_type=F32) > 0.5

    part = jnp.concatenate(
        [
            es_ref[:, dx : dx + SX, dz : dz + SZ].reshape(full, 4 * CIN)
            for dx in range(3)
            for dz in range(3)
        ],
        axis=1,
    )
    pre = jnp.dot(part, taps_ref[...].reshape(36 * CIN, 2 * C1), preferred_element_type=F32)

    sigmoid = 1.0 / (1.0 + jnp.exp(-pre))
    act = jnp.where(active, pre * sigmoid, 0.0).astype(BF16)
    slope = jnp.where(active, sigmoid * (1.0 + pre * (1.0 - sigmoid)), 0.0)

    act = act.reshape(2, 2, 2, 4, 2, 16, 2 * C1)
    slope = slope.reshape(2, 2, 2, 4, 2, 16, 2 * C1)
    for ox in range(2):
        for oz in range(2):
            act_ref[ox * 2 + oz] = act[:, :, ox, :, oz].reshape(256, 2 * C1)
            slope_ref[ox * 2 + oz] = slope[:, :, ox, :, oz].reshape(256, 2 * C1)


def down_grad_kernel(samples, act_ref, slope_ref, own_ref, got_ref, pairs_ref, pg_ref, mine_ref, other_ref):
    first = slab_tiles()[1] == 0
    own = own_ref[...].astype(F32)
    got = got_ref[...].astype(F32)
    cot = jnp.concatenate([jnp.where(first, own, got), jnp.where(first, got, own)], axis=0).astype(BF16)
    edge = jnp.zeros((2, SX, 1, 16, 2 * C1), BF16)
    pg_ref[:, :, 0:1] = edge
    pg_ref[:, :, SZ + 1 : SZ + 2] = edge
    low = (lax.axis_index("tile") & 1) == 0
    down_rows = 8 * C1 // samples
    step = min(C1, down_rows)
    for ox in range(2):
        for oz in range(2):
            back = lax.dot_general(cot, pairs_ref[ox * 2 + oz], NT, preferred_element_type=F32)
            part = (back * slope_ref[ox * 2 + oz]).astype(BF16)
            part = part.reshape(2, 2, 4, 16, 2 * C1)
            for s in range(2):
                for u in range(2):
                    for w in range(4):
                        pg_ref[s, 2 * u + ox, 1 + 2 * w + oz] = part[s, u, w]
            grad = lax.dot_general(act_ref[ox * 2 + oz], cot, TN, preferred_element_type=F32)
            for p in range(2):
                for i in range(0, C1, step):
                    chunk, row = divmod((ox * 4 + p * 2 + oz) * C1 + i, down_rows)
                    left = grad[p * C1 + i : p * C1 + i + step, 0:128]
                    right = grad[p * C1 + i : p * C1 + i + step, 128:256]
                    mine_ref[chunk, row : row + step, :] = jnp.where(low, left, right)
                    other_ref[chunk, row : row + step, :] = jnp.where(low, right, left).astype(BF16)


def conv_grad_kernel(samples, half_rows, es_ref, pg_ref, mine_ref, other_ref, tall_ref):
    full = 2 * SX * LAYER
    flipped = es_ref[:, :, 1 : SZ + 1].reshape(2 * (SX + 2) * LAYER, 4 * CIN).T
    half = (SX + 2) * LAYER
    part = jnp.concatenate(
        [pg_ref[:, :, 2 - dz : 2 - dz + SZ].reshape(full, 2 * C1) for dz in range(3)], axis=1
    )
    for dx in range(3):
        rows = jnp.concatenate(
            [flipped[:, s * half + dx * LAYER : s * half + (dx + SX) * LAYER] for s in range(2)], axis=1
        )
        grads = jnp.dot(rows, part, preferred_element_type=F32)
        for dz in range(3):
            grad = grads[:, dz * 256 : (dz + 1) * 256]
            sums = (
                grad[0:64, 128:256] + grad[128:192, 0:128],
                grad[0:64, 0:128] + grad[64:128, 128:256],
                grad[64:128, 0:128] + grad[192:256, 128:256],
            )
            for dy in range(3):
                start = ((dx * 3 + dy) * 3 + dz) * CIN
                tall_ref[start : start + CIN, :] = sums[dy]

    conv_rows = TAPS * CIN // samples
    filler = 2 * half_rows - conv_rows
    low = (lax.axis_index("tile") & 1) == 0
    for s in range(samples):
        first = tall_ref[s * conv_rows : s * conv_rows + half_rows, :]
        second = tall_ref[s * conv_rows + half_rows : (s + 1) * conv_rows, :]
        if filler:
            second = jnp.concatenate([second, jnp.zeros((filler, C1), F32)], axis=0)
        mine_ref[s] = jnp.where(low, first, second)
        other_ref[s] = jnp.where(low, second, first).astype(BF16)


def down_kernel(act_ref, pairs_ref, out_ref):
    place = slab_tiles()[1]
    down = jnp.zeros((128, C2), F32)
    for i in range(4):
        rows = act_ref[i, pl.ds(pl.multiple_of(place * 128, 128), 128)]
        down = down + jnp.dot(rows, pairs_ref[i], preferred_element_type=F32)
    out_ref[...] = jnp.dot(turn_matrix(), down.astype(BF16), preferred_element_type=F32).astype(BF16)


def share_samples_kernel(samples, mine_ref, got_ref, mine_conv_ref, got_conv_ref, keep_ref, *send_refs):
    me = lax.axis_index("sample")
    rows = mine_ref.shape[1]
    for k, ref in enumerate((keep_ref, *send_refs)):
        to = target(me, k, samples) if k else me
        ref[:rows] = (mine_ref[to] + got_ref[to].astype(F32)).astype(ref.dtype)
        ref[rows:] = (mine_conv_ref[to] + got_conv_ref[to].astype(F32)).astype(ref.dtype)


def sum_kernel(*refs):
    total = refs[0][...].astype(F32)
    for ref in refs[1:-1]:
        total = total + ref[...].astype(F32)
    refs[-1][...] = total.astype(refs[-1].dtype)


def ordered_sum_kernel(own_ref, *refs):
    held_ref, out_ref = refs[-1], refs[-2]
    count = len(refs) - 1
    me = lax.axis_index("tile") // (2 * BLOCK)
    held_ref[me] = own_ref[...].astype(F32)
    for j, ref in enumerate(refs[:-2], 1):
        held_ref[lax.rem(me - j + count, count)] = ref[...].astype(F32)
    total = held_ref[0]
    for i in range(1, count):
        total = total + held_ref[i]
    out_ref[...] = total


def finish_kernel(down_rows, own_ref, got_ref, conv_ref, down_ref):
    low = (lax.axis_index("tile") & 1) == 0
    own = own_ref[...]
    got = got_ref[...]
    first = jnp.where(low, own, got)
    second = jnp.where(low, got, own)
    half_rows = first.shape[0] - down_rows
    down_ref[:, 0:128] = first[:down_rows]
    down_ref[:, 128:256] = second[:down_rows]
    conv_ref[0:half_rows, :] = first[down_rows:]
    conv_ref[half_rows:, :] = second[down_rows : down_rows + conv_ref.shape[0] - half_rows]


def local(points, slot, voxel, conv_weight, down_weight, cotangent):
    tiles = lax.axis_size("tile")
    samples = lax.axis_size("sample")
    chips = tiles // 2
    capacity = 2 * (PTS_DEV // tiles)
    conv_rows = TAPS * CIN // samples
    down_rows = 8 * C1 // samples
    half_rows = -(-conv_rows // 32) * 16

    hbm = jax.ShapeDtypeStruct
    shape = pltpu.VMEM
    coded = call(
        functools.partial(encode_kernel, capacity),
        shape((CODED, PTS_DEV), BF16),
        scratch=(
            pltpu.VMEM((1, PTS_DEV), I32),
            pltpu.VMEM((1, PTS_DEV), I32),
            pltpu.SemaphoreType.DMA((3,)),
        ),
        raw=3,
    )(points[0].T, slot, voxel)
    blocks = chips // BLOCK

    sums = (shape((6 * LAYER, 4 * CIN), F32), shape((64, 32), F32))

    def add(grid, piece, at=None):
        if grid is None:
            return call(functools.partial(first_points_kernel, at), sums, pinned=1)(piece)
        return call(functools.partial(more_points_kernel, at), sums, pinned=3)(*grid, piece)

    beyond = send_column(coded, lambda i: i ^ FAR, tiles)
    beside = send_column(coded, lambda i: i ^ 1, tiles)
    taps, pairs, cot = call(
        weights_kernel,
        (shape((9, 4 * CIN, 2 * C1), BF16), shape((4, 2 * C1, C2), BF16), shape((128, C2), BF16)),
        loose=3,
    )(conv_weight, down_weight, cotangent.reshape(128, C2))
    beyond, taps, pairs, cot, coded = lax.optimization_barrier((beyond, taps, pairs, cot, coded))
    across = send_column(beyond, lambda i: i ^ 1, tiles)
    far = add(None, beyond)
    coded, beyond, far, cot = lax.optimization_barrier((coded, beyond, far, cot))
    own = add(None, coded)
    coded_swap = swap_core(coded, tiles)
    beyond_swap = swap_core(beyond, tiles)
    cot_got = send_column(cot, lambda i: i ^ FAR, tiles)
    own = add(own, beside)
    beside, own = lax.optimization_barrier((beside, own))
    beside_swap = swap_core(beside, tiles)
    across, own, far, cot_got = lax.optimization_barrier((across, own, far, cot_got))
    across_swap = swap_core(across, tiles)
    far = add(far, across)
    own_swap = add(add(None, coded_swap), beside_swap)
    far_swap = add(None, beyond_swap)
    across_swap, far = lax.optimization_barrier((across_swap, far))
    far_swap = add(far_swap, across_swap)
    grids = [own, own_swap, far, far_swap]
    if blocks > 1:
        rest = call(add_grids_kernel, sums, pinned=8)(*grids[0], *grids[1], *grids[2], *grids[3])
        for j in range(1, blocks):
            got = [
                send_column(coded, lambda i: (i // BLOCK + j) % blocks * BLOCK + (i % BLOCK ^ m), tiles)
                for m in (0, 1, FAR, FAR ^ 1)
            ]
            swapped = [swap_core(piece, tiles) for piece in got]
            trees = [
                add(add(None, first), second)
                for first, second in (got[:2], swapped[:2], got[2:], swapped[2:])
            ]
            both = call(add_grids_kernel, sums, pinned=8)(*trees[0], *trees[1], *trees[2], *trees[3])
            parts = both if j == 1 else call(add_two_kernel, sums, pinned=4)(*parts, *both)
        nothing = (jnp.zeros((6 * LAYER, 4 * CIN), F32), jnp.zeros((64, 32), F32))
        grids = [rest, nothing, parts, nothing]

    act, slope, es = call(
        scene_kernel,
        (
            shape((4, 256, 2 * C1), BF16),
            shape((4, 256, 2 * C1), F32),
            shape((2, SX + 2, SZ + 2, 16, 4 * CIN), BF16),
        ),
        pinned=9,
    )(*grids[0], *grids[1], *grids[2], *grids[3], taps)
    pg, mine, other = call(
        functools.partial(down_grad_kernel, samples),
        (
            shape((2, SX, SZ + 2, 16, 2 * C1), BF16),
            shape((samples, down_rows, 128), F32),
            shape((samples, down_rows, 128), BF16),
        ),
        pinned=5,
    )(act, slope, cot, cot_got, pairs)

    got = swap_core(other, tiles)
    mine_conv, other_conv = call(
        functools.partial(conv_grad_kernel, samples, half_rows),
        (shape((samples, half_rows, C1), F32), shape((samples, half_rows, C1), BF16)),
        scratch=(pltpu.VMEM((TAPS * CIN, C1), F32),),
        pinned=2,
    )(es, pg)
    got, mine_conv, other_conv = lax.optimization_barrier((got, mine_conv, other_conv))
    sum_rows = down_rows + half_rows
    keep, *sends = call(
        functools.partial(share_samples_kernel, samples),
        [shape((sum_rows, 128), F32)] + [shape((sum_rows, 128), BF16)] * (samples - 1),
        pinned=4,
    )(mine, got, mine_conv, swap_core(other_conv, tiles))
    terms = [keep] + [send_sample(value, k, samples) for k, value in enumerate(sends, 1)]
    down = call(down_kernel, shape((128, C2), BF16), pinned=2)(act, pairs)
    down = down.reshape(1, SX // 2, SY // 2, SZ // 2, C2)
    *terms, down = lax.optimization_barrier((*terms, down))
    total = call(sum_kernel, shape((sum_rows, 128), BF16), pinned=samples)(*terms)
    got = send_column(total, lambda i: i ^ 1, tiles)
    total = call(sum_kernel, shape((sum_rows, 128), F32 if blocks == 1 else BF16), pinned=2)(total, got)
    if blocks > 1:
        got = [send_column(total, lambda i: (i + j * BLOCK) % chips, tiles) for j in range(1, blocks)]
        total = call(
            ordered_sum_kernel,
            shape((sum_rows, 128), F32),
            scratch=(pltpu.VMEM((blocks, sum_rows, 128), F32),),
            pinned=blocks,
        )(total, *got)
    conv_grad, down_grad = call(
        functools.partial(finish_kernel, down_rows),
        (hbm((conv_rows, C1), F32), hbm((down_rows, C2), F32)),
        pinned=2,
    )(total, swap_core(total, tiles))
    return (down, conv_grad, down_grad)


def solution(mesh):
    placed = (
        P("sample", "tile", None),
        P("sample", "tile"),
        P("sample", "tile"),
        P(),
        P(),
        P("sample", "tile", None, None, None),
    )
    return jax.shard_map(
        local,
        mesh=mesh,
        in_specs=placed,
        out_specs=(P("sample", "tile", None, None, None), P("sample", None), P("sample", None)),
        check_vma=False,
    )
```

```python
import functools

import jax
import jax.numpy as jnp
from jax import lax
from jax.experimental import pallas as pl
from jax.experimental.pallas import tpu as pltpu
from jax.sharding import PartitionSpec as P

CIN = 64
C1 = 128
C2 = 256
SX = 4
SY = 32
SZ = 8
PTS_DEV = 1024
TAPS = 27
CODED = CIN + 8
LAYER = SZ * SY // 2
FAR = 3
BLOCK = 4
BF16 = jnp.bfloat16
F32 = jnp.float32
I32 = jnp.int32
NT = (((1,), (1,)), ((), ()))
TN = (((0,), (0,)), ((), ()))
VMEM_LIMIT = 24 * 1024 * 1024


def call(body, outs, scratch=(), pinned=0, loose=0, raw=0):
    single = not isinstance(outs, (list, tuple))
    vmem = pl.BlockSpec(memory_space=pltpu.VMEM)
    kernel = pl.pallas_call(
        body,
        out_shape=outs,
        in_specs=[vmem] * (pinned + loose) + [pl.BlockSpec(memory_space=pltpu.HBM)] * raw,
        out_specs=vmem if single else [vmem] * len(outs),
        scratch_shapes=list(scratch),
        compiler_params=pltpu.CompilerParams(vmem_limit_bytes=VMEM_LIMIT),
    )

    def run(*args):
        held = [pltpu.with_memory_space_constraint(a, pltpu.VMEM) for a in args[:pinned]]
        far = [pltpu.with_memory_space_constraint(a, pltpu.HBM) for a in args[pinned:]]
        return kernel(*held, *far)

    return run


def target(index, k, count):
    if count & (count - 1) == 0:
        return index ^ k
    return (index + k) % count


def swap_core(value, tiles):
    return lax.ppermute(value, "tile", [(i, i ^ 1) for i in range(tiles)])


def send_column(value, to, tiles):
    pairs = [(2 * i + c, 2 * to(i) + c) for i in range(tiles // 2) for c in range(2)]
    return lax.ppermute(value, "tile", pairs)


def send_sample(value, k, samples):
    return lax.ppermute(value, "sample", [(i, target(i, k, samples)) for i in range(samples)])


def encode_kernel(capacity, points_hbm, slot_hbm, voxel_hbm, out_ref, slot_ref, voxel_ref, sems):
    copies = [
        pltpu.make_async_copy(slot_hbm, slot_ref, sems.at[0]),
        pltpu.make_async_copy(voxel_hbm, voxel_ref, sems.at[1]),
        pltpu.make_async_copy(points_hbm, out_ref.at[0:CIN], sems.at[2]),
    ]
    for copy in copies:
        copy.start()
    copies[0].wait()
    copies[1].wait()
    slot = slot_ref[...]
    voxel = voxel_ref[...]
    if capacity & (capacity - 1) == 0:
        owner = slot >> (capacity.bit_length() - 1)
    else:
        owner = jnp.floor((slot.astype(F32) + 0.5) * (1.0 / capacity)).astype(I32)
    layer = owner * SX + (voxel >> 8) + 1
    z = voxel & 7
    y = (voxel >> 3) & 31
    place = ((z * 16 + (y >> 1)) << 1) + (y & 1)
    row = lax.broadcasted_iota(I32, (8, slot.shape[1]), 0)
    codes = jnp.where(row == 0, layer, jnp.where(row == 1, place, 0))
    out_ref[CIN:CODED, :] = codes.astype(F32).astype(BF16)
    copies[2].wait()


def slab_tiles():
    tile = lax.axis_index("tile")
    chip = tile >> 1
    core = tile & 1
    place = (chip >> 1) & 1
    low = jnp.where(place == 0, chip, chip ^ FAR)
    return (2 * low + core, 2 * (low ^ FAR) + core), place


def turn_matrix():
    here = lax.broadcasted_iota(I32, (128, 128), 0)
    there = lax.broadcasted_iota(I32, (128, 128), 1)
    return ((here >> 6) * 64 + (here & 3) * 16 + ((here >> 2) & 15) == there).astype(F32).astype(BF16)


def weights_kernel(conv_ref, down_ref, cot_ref, taps_ref, pairs_ref, turned_ref):
    zero_tap = jnp.zeros((CIN, C1), BF16)

    def tap(dx, dy, dz):
        start = ((dx * 3 + dy) * 3 + dz) * CIN
        return conv_ref[start : start + CIN, :]

    for dx in range(3):
        for dz in range(3):
            taps_ref[dx * 3 + dz] = jnp.concatenate(
                [
                    jnp.concatenate([tap(dx, 1, dz), tap(dx, 0, dz)], axis=1),
                    jnp.concatenate([tap(dx, 2, dz), tap(dx, 1, dz)], axis=1),
                    jnp.concatenate([tap(dx, 0, dz), zero_tap], axis=1),
                    jnp.concatenate([zero_tap, tap(dx, 2, dz)], axis=1),
                ],
                axis=0,
            )
    for ox in range(2):
        for oz in range(2):
            first = (ox * 4 + oz) * C1
            second = first + 2 * C1
            pairs_ref[ox * 2 + oz] = jnp.concatenate(
                [down_ref[first : first + C1, :], down_ref[second : second + C1, :]], axis=0
            )
    turned_ref[...] = lax.dot_general(turn_matrix(), cot_ref[...], TN, preferred_element_type=F32).astype(BF16)


def voxelize(ref):
    codes = ref[CIN:CODED, :].astype(F32).astype(I32)
    layer = codes[0:1, :]
    place = codes[1:2, :]
    odd = layer & 1
    spot = place >> 1
    side = place & 1
    row_iota = lax.broadcasted_iota(I32, (LAYER, PTS_DEV), 0).astype(F32).astype(BF16)
    small_iota = lax.broadcasted_iota(I32, (32, PTS_DEV), 0).astype(F32).astype(BF16)
    one = jnp.ones((), BF16)
    nought = jnp.zeros((), BF16)
    hot = []
    hot_plane = []
    for tile in slab_tiles()[0]:
        pair = (layer >> 1) - 2 * tile
        for p in range(3):
            code = jnp.where(pair == p, spot, 255).astype(F32).astype(BF16)
            hot.append(jnp.where(row_iota == code, one, nought))
        plane = (2 * pair + odd - 1) * SZ + (spot >> 4)
        plane = jnp.where((pair >= 0) & (pair <= 2) & (plane >= 0), plane, 255).astype(F32).astype(BF16)
        hot_plane.append(jnp.where(small_iota == plane, one, nought))
    group = odd * 2 + side
    features = ref[0:CIN, :]
    spread = jnp.concatenate(
        [features * (group == g).astype(F32).astype(BF16) for g in range(4)], axis=0
    )
    grid = lax.dot_general(jnp.concatenate(hot, axis=0), spread, NT, preferred_element_type=F32)
    line = ((spot & 15) * 2 + side).astype(F32).astype(BF16)
    hot_line = jnp.where(small_iota == line, one, nought)
    counts = lax.dot_general(
        jnp.concatenate(hot_plane, axis=0), hot_line, NT, preferred_element_type=F32
    )
    return grid, counts


def first_points_kernel(at, ref, grid_ref, counts_ref):
    grid_ref[...], counts_ref[...] = voxelize(ref if at is None else ref.at[at])


def more_points_kernel(at, old_grid_ref, old_counts_ref, ref, grid_ref, counts_ref):
    grid, counts = voxelize(ref if at is None else ref.at[at])
    grid_ref[...] = old_grid_ref[...] + grid
    counts_ref[...] = old_counts_ref[...] + counts


def late_points_kernel(
    old_grid_ref, old_counts_ref, across_ref, coded_ref, beside_ref, beyond_ref,
    far_ref, far_counts_ref, own_ref, own_counts_ref, swap_ref, swap_counts_ref,
):
    first_points_kernel(None, coded_ref, own_ref, own_counts_ref)
    first_points_kernel(None, beyond_ref, swap_ref, swap_counts_ref)
    more_points_kernel(None, own_ref, own_counts_ref, beside_ref, own_ref, own_counts_ref)
    more_points_kernel(None, old_grid_ref, old_counts_ref, across_ref, far_ref, far_counts_ref)


def add_grids_kernel(*refs):
    grid_ref, counts_ref = refs[-2:]
    grid_ref[...] = (refs[0][...] + refs[2][...]) + (refs[4][...] + refs[6][...])
    counts_ref[...] = (refs[1][...] + refs[3][...]) + (refs[5][...] + refs[7][...])


def add_two_kernel(a_ref, a_counts_ref, b_ref, b_counts_ref, grid_ref, counts_ref):
    grid_ref[...] = a_ref[...] + b_ref[...]
    counts_ref[...] = a_counts_ref[...] + b_counts_ref[...]


def scene_kernel(
    grid0, counts0, grid1, counts1, grid2, counts2, grid3, counts3, taps_ref,
    act_ref, slope_ref, es_ref,
):
    counts = counts0[...] + counts1[...] + counts2[...] + counts3[...]

    edge = jnp.zeros((2, SX + 2, 1, 16, 4 * CIN), BF16)
    es_ref[:, :, 0:1] = edge
    es_ref[:, :, SZ + 1 : SZ + 2] = edge
    line = lax.broadcasted_iota(I32, (LAYER, 2 * CIN), 0) & 15
    lane = lax.broadcasted_iota(I32, (LAYER, 2 * CIN), 1)
    for s in range(2):
        for x in range(SX + 2):
            rows = slice((s * 3 + x // 2) * LAYER, (s * 3 + x // 2 + 1) * LAYER)
            lanes = slice((x % 2) * 128, (x % 2 + 1) * 128)
            both = (grid0[rows, lanes] + grid1[rows, lanes]) + (grid2[rows, lanes] + grid3[rows, lanes])
            turned = pltpu.roll(both, CIN, 1)
            before = jnp.where(line == 0, 0.0, pltpu.roll(turned, 1, 0))
            after = jnp.where(line == 15, 0.0, pltpu.roll(turned, LAYER - 1, 0))
            sides = jnp.where(lane < CIN, before, after)
            es_ref[s, x, 1 : SZ + 1, :, 0:128] = both.astype(BF16).reshape(SZ, 16, 128)
            es_ref[s, x, 1 : SZ + 1, :, 128:256] = sides.astype(BF16).reshape(SZ, 16, 128)

    full = 2 * SX * LAYER
    flags = (counts > 0.5).astype(F32).astype(BF16)
    row_plane = lax.broadcasted_iota(I32, (full, 64), 0) >> 4
    pick = (row_plane == lax.broadcasted_iota(I32, (full, 64), 1)).astype(F32).astype(BF16)
    lines = jnp.dot(pick, flags, preferred_element_type=F32)
    row_line = lax.broadcasted_iota(I32, (full, 32), 0) & 15
    lines = jnp.where(row_line == (lax.broadcasted_iota(I32, (full, 32), 1) >> 1), lines, 0.0).astype(BF16)
    expand = (
        (lax.broadcasted_iota(I32, (32, 256), 0) & 1) == (lax.broadcasted_iota(I32, (32, 256), 1) >> 7)
    ).astype(F32).astype(BF16)
    active = jnp.dot(lines, expand, preferred_element_type=F32) > 0.5

    part = jnp.concatenate(
        [
            es_ref[:, dx : dx + SX, dz : dz + SZ].reshape(full, 4 * CIN)
            for dx in range(3)
            for dz in range(3)
        ],
        axis=1,
    )
    pre = jnp.dot(part, taps_ref[...].reshape(36 * CIN, 2 * C1), preferred_element_type=F32)

    sigmoid = 1.0 / (1.0 + jnp.exp(-pre))
    act = jnp.where(active, pre * sigmoid, 0.0).astype(BF16)
    slope = jnp.where(active, sigmoid * (1.0 + pre * (1.0 - sigmoid)), 0.0)

    act = act.reshape(2, 2, 2, 4, 2, 16, 2 * C1)
    slope = slope.reshape(2, 2, 2, 4, 2, 16, 2 * C1)
    for ox in range(2):
        for oz in range(2):
            act_ref[ox * 2 + oz] = act[:, :, ox, :, oz].reshape(256, 2 * C1)
            slope_ref[ox * 2 + oz] = slope[:, :, ox, :, oz].reshape(256, 2 * C1)


def down_grad_kernel(samples, act_ref, slope_ref, own_ref, got_ref, pairs_ref, pg_ref, mine_ref, other_ref):
    first = slab_tiles()[1] == 0
    own = own_ref[...].astype(F32)
    got = got_ref[...].astype(F32)
    cot = jnp.concatenate([jnp.where(first, own, got), jnp.where(first, got, own)], axis=0).astype(BF16)
    edge = jnp.zeros((2, SX, 1, 16, 2 * C1), BF16)
    pg_ref[:, :, 0:1] = edge
    pg_ref[:, :, SZ + 1 : SZ + 2] = edge
    low = (lax.axis_index("tile") & 1) == 0
    down_rows = 8 * C1 // samples
    step = min(C1, down_rows)
    for ox in range(2):
        for oz in range(2):
            back = lax.dot_general(cot, pairs_ref[ox * 2 + oz], NT, preferred_element_type=F32)
            part = (back * slope_ref[ox * 2 + oz]).astype(BF16)
            part = part.reshape(2, 2, 4, 16, 2 * C1)
            for s in range(2):
                for u in range(2):
                    for w in range(4):
                        pg_ref[s, 2 * u + ox, 1 + 2 * w + oz] = part[s, u, w]
            grad = lax.dot_general(act_ref[ox * 2 + oz], cot, TN, preferred_element_type=F32)
            for p in range(2):
                for i in range(0, C1, step):
                    chunk, row = divmod((ox * 4 + p * 2 + oz) * C1 + i, down_rows)
                    left = grad[p * C1 + i : p * C1 + i + step, 0:128]
                    right = grad[p * C1 + i : p * C1 + i + step, 128:256]
                    mine_ref[chunk, row : row + step, :] = jnp.where(low, left, right)
                    other_ref[chunk, row : row + step, :] = jnp.where(low, right, left).astype(BF16)


def conv_grad_kernel(samples, half_rows, es_ref, pg_ref, mine_ref, other_ref, tall_ref):
    full = 2 * SX * LAYER
    flipped = es_ref[:, :, 1 : SZ + 1].reshape(2 * (SX + 2) * LAYER, 4 * CIN).T
    half = (SX + 2) * LAYER
    part = jnp.concatenate(
        [pg_ref[:, :, 2 - dz : 2 - dz + SZ].reshape(full, 2 * C1) for dz in range(3)], axis=1
    )
    for dx in range(3):
        rows = jnp.concatenate(
            [flipped[:, s * half + dx * LAYER : s * half + (dx + SX) * LAYER] for s in range(2)], axis=1
        )
        grads = jnp.dot(rows, part, preferred_element_type=F32)
        for dz in range(3):
            grad = grads[:, dz * 256 : (dz + 1) * 256]
            sums = (
                grad[0:64, 128:256] + grad[128:192, 0:128],
                grad[0:64, 0:128] + grad[64:128, 128:256],
                grad[64:128, 0:128] + grad[192:256, 128:256],
            )
            for dy in range(3):
                start = ((dx * 3 + dy) * 3 + dz) * CIN
                tall_ref[start : start + CIN, :] = sums[dy]

    conv_rows = TAPS * CIN // samples
    filler = 2 * half_rows - conv_rows
    low = (lax.axis_index("tile") & 1) == 0
    for s in range(samples):
        first = tall_ref[s * conv_rows : s * conv_rows + half_rows, :]
        second = tall_ref[s * conv_rows + half_rows : (s + 1) * conv_rows, :]
        if filler:
            second = jnp.concatenate([second, jnp.zeros((filler, C1), F32)], axis=0)
        mine_ref[s] = jnp.where(low, first, second)
        other_ref[s] = jnp.where(low, second, first).astype(BF16)


def down_kernel(act_ref, pairs_ref, out_ref):
    place = slab_tiles()[1]
    down = jnp.zeros((128, C2), F32)
    for i in range(4):
        rows = act_ref[i, pl.ds(pl.multiple_of(place * 128, 128), 128)]
        down = down + jnp.dot(rows, pairs_ref[i], preferred_element_type=F32)
    out_ref[...] = jnp.dot(turn_matrix(), down.astype(BF16), preferred_element_type=F32).astype(BF16)


def share_samples_kernel(samples, mine_ref, got_ref, mine_conv_ref, got_conv_ref, keep_ref, *send_refs):
    me = lax.axis_index("sample")
    rows = mine_ref.shape[1]
    for k, ref in enumerate((keep_ref, *send_refs)):
        to = target(me, k, samples) if k else me
        ref[:rows] = (mine_ref[to] + got_ref[to].astype(F32)).astype(ref.dtype)
        ref[rows:] = (mine_conv_ref[to] + got_conv_ref[to].astype(F32)).astype(ref.dtype)


def sum_kernel(*refs):
    total = refs[0][...].astype(F32)
    for ref in refs[1:-1]:
        total = total + ref[...].astype(F32)
    refs[-1][...] = total.astype(refs[-1].dtype)


def ordered_sum_kernel(own_ref, *refs):
    held_ref, out_ref = refs[-1], refs[-2]
    count = len(refs) - 1
    me = lax.axis_index("tile") // (2 * BLOCK)
    held_ref[me] = own_ref[...].astype(F32)
    for j, ref in enumerate(refs[:-2], 1):
        held_ref[lax.rem(me - j + count, count)] = ref[...].astype(F32)
    total = held_ref[0]
    for i in range(1, count):
        total = total + held_ref[i]
    out_ref[...] = total


def finish_kernel(down_rows, own_ref, got_ref, conv_ref, down_ref):
    low = (lax.axis_index("tile") & 1) == 0
    own = own_ref[...]
    got = got_ref[...]
    first = jnp.where(low, own, got)
    second = jnp.where(low, got, own)
    half_rows = first.shape[0] - down_rows
    down_ref[:, 0:128] = first[:down_rows]
    down_ref[:, 128:256] = second[:down_rows]
    conv_ref[0:half_rows, :] = first[down_rows:]
    conv_ref[half_rows:, :] = second[down_rows : down_rows + conv_ref.shape[0] - half_rows]


def local(points, slot, voxel, conv_weight, down_weight, cotangent):
    tiles = lax.axis_size("tile")
    samples = lax.axis_size("sample")
    chips = tiles // 2
    capacity = 2 * (PTS_DEV // tiles)
    conv_rows = TAPS * CIN // samples
    down_rows = 8 * C1 // samples
    half_rows = -(-conv_rows // 32) * 16

    hbm = jax.ShapeDtypeStruct
    shape = pltpu.VMEM
    coded = call(
        functools.partial(encode_kernel, capacity),
        shape((CODED, PTS_DEV), BF16),
        scratch=(
            pltpu.VMEM((1, PTS_DEV), I32),
            pltpu.VMEM((1, PTS_DEV), I32),
            pltpu.SemaphoreType.DMA((3,)),
        ),
        raw=3,
    )(points[0].T, slot, voxel)
    blocks = chips // BLOCK

    sums = (shape((6 * LAYER, 4 * CIN), F32), shape((64, 32), F32))

    def add(grid, piece, at=None):
        if grid is None:
            return call(functools.partial(first_points_kernel, at), sums, pinned=1)(piece)
        return call(functools.partial(more_points_kernel, at), sums, pinned=3)(*grid, piece)

    beyond = send_column(coded, lambda i: i ^ FAR, tiles)
    beside = send_column(coded, lambda i: i ^ 1, tiles)
    taps, pairs, cot = call(
        weights_kernel,
        (shape((9, 4 * CIN, 2 * C1), BF16), shape((4, 2 * C1, C2), BF16), shape((128, C2), BF16)),
        loose=3,
    )(conv_weight, down_weight, cotangent.reshape(128, C2))
    beyond, taps, pairs, cot, coded = lax.optimization_barrier((beyond, taps, pairs, cot, coded))
    across = send_column(beyond, lambda i: i ^ 1, tiles)
    far = add(None, beyond)
    coded, beyond, far, cot = lax.optimization_barrier((coded, beyond, far, cot))
    own = add(None, coded)
    coded_swap = swap_core(coded, tiles)
    beyond_swap = swap_core(beyond, tiles)
    cot_got = send_column(cot, lambda i: i ^ FAR, tiles)
    own = add(own, beside)
    beside, own = lax.optimization_barrier((beside, own))
    beside_swap = swap_core(beside, tiles)
    across, own, far = lax.optimization_barrier((across, own, far))
    across_swap = swap_core(across, tiles)
    late = call(late_points_kernel, sums * 3, pinned=6)(*far, across, coded_swap, beside_swap, beyond_swap)
    far, own_swap, far_swap = late[:2], late[2:4], late[4:]
    across_swap, far = lax.optimization_barrier((across_swap, far))
    far_swap = add(far_swap, across_swap)
    grids = [own, own_swap, far, far_swap]
    if blocks > 1:
        rest = call(add_grids_kernel, sums, pinned=8)(*grids[0], *grids[1], *grids[2], *grids[3])
        for j in range(1, blocks):
            got = [
                send_column(coded, lambda i: (i // BLOCK + j) % blocks * BLOCK + (i % BLOCK ^ m), tiles)
                for m in (0, 1, FAR, FAR ^ 1)
            ]
            swapped = [swap_core(piece, tiles) for piece in got]
            trees = [
                add(add(None, first), second)
                for first, second in (got[:2], swapped[:2], got[2:], swapped[2:])
            ]
            both = call(add_grids_kernel, sums, pinned=8)(*trees[0], *trees[1], *trees[2], *trees[3])
            parts = both if j == 1 else call(add_two_kernel, sums, pinned=4)(*parts, *both)
        nothing = (jnp.zeros((6 * LAYER, 4 * CIN), F32), jnp.zeros((64, 32), F32))
        grids = [rest, nothing, parts, nothing]

    act, slope, es = call(
        scene_kernel,
        (
            shape((4, 256, 2 * C1), BF16),
            shape((4, 256, 2 * C1), F32),
            shape((2, SX + 2, SZ + 2, 16, 4 * CIN), BF16),
        ),
        pinned=9,
    )(*grids[0], *grids[1], *grids[2], *grids[3], taps)
    pg, mine, other = call(
        functools.partial(down_grad_kernel, samples),
        (
            shape((2, SX, SZ + 2, 16, 2 * C1), BF16),
            shape((samples, down_rows, 128), F32),
            shape((samples, down_rows, 128), BF16),
        ),
        pinned=5,
    )(act, slope, cot, cot_got, pairs)

    got = swap_core(other, tiles)
    mine_conv, other_conv = call(
        functools.partial(conv_grad_kernel, samples, half_rows),
        (shape((samples, half_rows, C1), F32), shape((samples, half_rows, C1), BF16)),
        scratch=(pltpu.VMEM((TAPS * CIN, C1), F32),),
        pinned=2,
    )(es, pg)
    got, mine_conv, other_conv = lax.optimization_barrier((got, mine_conv, other_conv))
    sum_rows = down_rows + half_rows
    keep, *sends = call(
        functools.partial(share_samples_kernel, samples),
        [shape((sum_rows, 128), F32)] + [shape((sum_rows, 128), BF16)] * (samples - 1),
        pinned=4,
    )(mine, got, mine_conv, swap_core(other_conv, tiles))
    terms = [keep] + [send_sample(value, k, samples) for k, value in enumerate(sends, 1)]
    down = call(down_kernel, shape((128, C2), BF16), pinned=2)(act, pairs)
    down = down.reshape(1, SX // 2, SY // 2, SZ // 2, C2)
    *terms, down = lax.optimization_barrier((*terms, down))
    total = call(sum_kernel, shape((sum_rows, 128), BF16), pinned=samples)(*terms)
    got = send_column(total, lambda i: i ^ 1, tiles)
    total = call(sum_kernel, shape((sum_rows, 128), F32 if blocks == 1 else BF16), pinned=2)(total, got)
    if blocks > 1:
        got = [send_column(total, lambda i: (i + j * BLOCK) % chips, tiles) for j in range(1, blocks)]
        total = call(
            ordered_sum_kernel,
            shape((sum_rows, 128), F32),
            scratch=(pltpu.VMEM((blocks, sum_rows, 128), F32),),
            pinned=blocks,
        )(total, *got)
    conv_grad, down_grad = call(
        functools.partial(finish_kernel, down_rows),
        (hbm((conv_rows, C1), F32), hbm((down_rows, C2), F32)),
        pinned=2,
    )(total, swap_core(total, tiles))
    return (down, conv_grad, down_grad)


def solution(mesh):
    placed = (
        P("sample", "tile", None),
        P("sample", "tile"),
        P("sample", "tile"),
        P(),
        P(),
        P("sample", "tile", None, None, None),
    )
    return jax.shard_map(
        local,
        mesh=mesh,
        in_specs=placed,
        out_specs=(P("sample", "tile", None, None, None), P("sample", None), P("sample", None)),
        check_vma=False,
    )
```

```python
import functools

import jax
import jax.numpy as jnp
from jax import lax
from jax.experimental import pallas as pl
from jax.experimental.pallas import tpu as pltpu
from jax.sharding import PartitionSpec as P

CIN = 64
C1 = 128
C2 = 256
SX = 4
SY = 32
SZ = 8
PTS_DEV = 1024
TAPS = 27
CODED = CIN + 8
LAYER = SZ * SY // 2
FAR = 3
BLOCK = 4
BF16 = jnp.bfloat16
F32 = jnp.float32
I32 = jnp.int32
NT = (((1,), (1,)), ((), ()))
TN = (((0,), (0,)), ((), ()))
VMEM_LIMIT = 24 * 1024 * 1024


def call(body, outs, scratch=(), pinned=0, loose=0, raw=0):
    single = not isinstance(outs, (list, tuple))
    vmem = pl.BlockSpec(memory_space=pltpu.VMEM)
    kernel = pl.pallas_call(
        body,
        out_shape=outs,
        in_specs=[vmem] * (pinned + loose) + [pl.BlockSpec(memory_space=pltpu.HBM)] * raw,
        out_specs=vmem if single else [vmem] * len(outs),
        scratch_shapes=list(scratch),
        compiler_params=pltpu.CompilerParams(vmem_limit_bytes=VMEM_LIMIT),
    )

    def run(*args):
        held = [pltpu.with_memory_space_constraint(a, pltpu.VMEM) for a in args[:pinned]]
        far = [pltpu.with_memory_space_constraint(a, pltpu.HBM) for a in args[pinned:]]
        return kernel(*held, *far)

    return run


def target(index, k, count):
    if count & (count - 1) == 0:
        return index ^ k
    return (index + k) % count


def swap_core(value, tiles):
    return lax.ppermute(value, "tile", [(i, i ^ 1) for i in range(tiles)])


def send_column(value, to, tiles):
    pairs = [(2 * i + c, 2 * to(i) + c) for i in range(tiles // 2) for c in range(2)]
    return lax.ppermute(value, "tile", pairs)


def send_sample(value, k, samples):
    return lax.ppermute(value, "sample", [(i, target(i, k, samples)) for i in range(samples)])


def encode_kernel(capacity, points_hbm, slot_hbm, voxel_hbm, out_ref, slot_ref, voxel_ref, sems):
    copies = [
        pltpu.make_async_copy(slot_hbm, slot_ref, sems.at[0]),
        pltpu.make_async_copy(voxel_hbm, voxel_ref, sems.at[1]),
        pltpu.make_async_copy(points_hbm, out_ref.at[0:CIN], sems.at[2]),
    ]
    for copy in copies:
        copy.start()
    copies[0].wait()
    copies[1].wait()
    slot = slot_ref[...]
    voxel = voxel_ref[...]
    if capacity & (capacity - 1) == 0:
        owner = slot >> (capacity.bit_length() - 1)
    else:
        owner = jnp.floor((slot.astype(F32) + 0.5) * (1.0 / capacity)).astype(I32)
    layer = owner * SX + (voxel >> 8) + 1
    z = voxel & 7
    y = (voxel >> 3) & 31
    place = ((z * 16 + (y >> 1)) << 1) + (y & 1)
    row = lax.broadcasted_iota(I32, (8, slot.shape[1]), 0)
    codes = jnp.where(row == 0, layer, jnp.where(row == 1, place, 0))
    out_ref[CIN:CODED, :] = codes.astype(F32).astype(BF16)
    copies[2].wait()


def slab_tiles():
    tile = lax.axis_index("tile")
    chip = tile >> 1
    core = tile & 1
    place = (chip >> 1) & 1
    low = jnp.where(place == 0, chip, chip ^ FAR)
    return (2 * low + core, 2 * (low ^ FAR) + core), place


def turn_matrix():
    here = lax.broadcasted_iota(I32, (128, 128), 0)
    there = lax.broadcasted_iota(I32, (128, 128), 1)
    return ((here >> 6) * 64 + (here & 3) * 16 + ((here >> 2) & 15) == there).astype(F32).astype(BF16)


def weights_kernel(
    conv_ref, down_ref, cot_ref, taps_ref, pairs_ref, turned_ref, pick_ref, line_ref, expand_ref
):
    zero_tap = jnp.zeros((CIN, C1), BF16)

    def tap(dx, dy, dz):
        start = ((dx * 3 + dy) * 3 + dz) * CIN
        return conv_ref[start : start + CIN, :]

    for dx in range(3):
        for dz in range(3):
            taps_ref[dx * 3 + dz] = jnp.concatenate(
                [
                    jnp.concatenate([tap(dx, 1, dz), tap(dx, 0, dz)], axis=1),
                    jnp.concatenate([tap(dx, 2, dz), tap(dx, 1, dz)], axis=1),
                    jnp.concatenate([tap(dx, 0, dz), zero_tap], axis=1),
                    jnp.concatenate([zero_tap, tap(dx, 2, dz)], axis=1),
                ],
                axis=0,
            )
    for ox in range(2):
        for oz in range(2):
            first = (ox * 4 + oz) * C1
            second = first + 2 * C1
            pairs_ref[ox * 2 + oz] = jnp.concatenate(
                [down_ref[first : first + C1, :], down_ref[second : second + C1, :]], axis=0
            )
    full = 2 * SX * LAYER
    row_plane = lax.broadcasted_iota(I32, (full, 64), 0) >> 4
    pick_ref[...] = (row_plane == lax.broadcasted_iota(I32, (full, 64), 1)).astype(F32).astype(BF16)
    row_line = lax.broadcasted_iota(I32, (full, 32), 0) & 15
    line_ref[...] = (row_line == (lax.broadcasted_iota(I32, (full, 32), 1) >> 1)).astype(F32).astype(BF16)
    expand_ref[...] = (
        (lax.broadcasted_iota(I32, (32, 256), 0) & 1) == (lax.broadcasted_iota(I32, (32, 256), 1) >> 7)
    ).astype(F32).astype(BF16)
    turned_ref[...] = lax.dot_general(turn_matrix(), cot_ref[...], TN, preferred_element_type=F32).astype(BF16)


def voxelize(ref):
    codes = ref[CIN:CODED, :].astype(F32).astype(I32)
    layer = codes[0:1, :]
    place = codes[1:2, :]
    odd = layer & 1
    spot = place >> 1
    side = place & 1
    row_iota = lax.broadcasted_iota(I32, (LAYER, PTS_DEV), 0).astype(F32).astype(BF16)
    small_iota = lax.broadcasted_iota(I32, (32, PTS_DEV), 0).astype(F32).astype(BF16)
    one = jnp.ones((), BF16)
    nought = jnp.zeros((), BF16)
    hot = []
    hot_plane = []
    for tile in slab_tiles()[0]:
        pair = (layer >> 1) - 2 * tile
        for p in range(3):
            code = jnp.where(pair == p, spot, 255).astype(F32).astype(BF16)
            hot.append(jnp.where(row_iota == code, one, nought))
        plane = (2 * pair + odd - 1) * SZ + (spot >> 4)
        plane = jnp.where((pair >= 0) & (pair <= 2) & (plane >= 0), plane, 255).astype(F32).astype(BF16)
        hot_plane.append(jnp.where(small_iota == plane, one, nought))
    group = odd * 2 + side
    features = ref[0:CIN, :]
    spread = jnp.concatenate(
        [features * (group == g).astype(F32).astype(BF16) for g in range(4)], axis=0
    )
    grid = lax.dot_general(jnp.concatenate(hot, axis=0), spread, NT, preferred_element_type=F32)
    line = ((spot & 15) * 2 + side).astype(F32).astype(BF16)
    hot_line = jnp.where(small_iota == line, one, nought)
    counts = lax.dot_general(
        jnp.concatenate(hot_plane, axis=0), hot_line, NT, preferred_element_type=F32
    )
    return grid, counts


def first_points_kernel(at, ref, grid_ref, counts_ref):
    grid_ref[...], counts_ref[...] = voxelize(ref if at is None else ref.at[at])


def more_points_kernel(at, old_grid_ref, old_counts_ref, ref, grid_ref, counts_ref):
    grid, counts = voxelize(ref if at is None else ref.at[at])
    grid_ref[...] = old_grid_ref[...] + grid
    counts_ref[...] = old_counts_ref[...] + counts


def late_points_kernel(
    old_grid_ref, old_counts_ref, across_ref, coded_ref, beside_ref, beyond_ref,
    far_ref, far_counts_ref, own_ref, own_counts_ref, swap_ref, swap_counts_ref,
):
    first_points_kernel(None, coded_ref, own_ref, own_counts_ref)
    first_points_kernel(None, beyond_ref, swap_ref, swap_counts_ref)
    more_points_kernel(None, own_ref, own_counts_ref, beside_ref, own_ref, own_counts_ref)
    more_points_kernel(None, old_grid_ref, old_counts_ref, across_ref, far_ref, far_counts_ref)


def add_grids_kernel(*refs):
    grid_ref, counts_ref = refs[-2:]
    grid_ref[...] = (refs[0][...] + refs[2][...]) + (refs[4][...] + refs[6][...])
    counts_ref[...] = (refs[1][...] + refs[3][...]) + (refs[5][...] + refs[7][...])


def add_two_kernel(a_ref, a_counts_ref, b_ref, b_counts_ref, grid_ref, counts_ref):
    grid_ref[...] = a_ref[...] + b_ref[...]
    counts_ref[...] = a_counts_ref[...] + b_counts_ref[...]


def scene_kernel(
    grid0, counts0, grid1, counts1, grid2, counts2, grid3, counts3, taps_ref,
    pick_ref, line_ref, expand_ref,
    act_ref, slope_ref, es_ref,
):
    counts = counts0[...] + counts1[...] + counts2[...] + counts3[...]

    edge = jnp.zeros((2, SX + 2, 1, 16, 4 * CIN), BF16)
    es_ref[:, :, 0:1] = edge
    es_ref[:, :, SZ + 1 : SZ + 2] = edge
    line = lax.broadcasted_iota(I32, (LAYER, 2 * CIN), 0) & 15
    lane = lax.broadcasted_iota(I32, (LAYER, 2 * CIN), 1)
    for s in range(2):
        for x in range(SX + 2):
            rows = slice((s * 3 + x // 2) * LAYER, (s * 3 + x // 2 + 1) * LAYER)
            lanes = slice((x % 2) * 128, (x % 2 + 1) * 128)
            both = (grid0[rows, lanes] + grid1[rows, lanes]) + (grid2[rows, lanes] + grid3[rows, lanes])
            turned = pltpu.roll(both, CIN, 1)
            before = jnp.where(line == 0, 0.0, pltpu.roll(turned, 1, 0))
            after = jnp.where(line == 15, 0.0, pltpu.roll(turned, LAYER - 1, 0))
            sides = jnp.where(lane < CIN, before, after)
            es_ref[s, x, 1 : SZ + 1, :, 0:128] = both.astype(BF16).reshape(SZ, 16, 128)
            es_ref[s, x, 1 : SZ + 1, :, 128:256] = sides.astype(BF16).reshape(SZ, 16, 128)

    full = 2 * SX * LAYER
    flags = (counts > 0.5).astype(F32).astype(BF16)
    lines = jnp.dot(pick_ref[...], flags, preferred_element_type=F32)
    lines = lines.astype(BF16) * line_ref[...]
    active = jnp.dot(lines, expand_ref[...], preferred_element_type=F32) > 0.5

    part = jnp.concatenate(
        [
            es_ref[:, dx : dx + SX, dz : dz + SZ].reshape(full, 4 * CIN)
            for dx in range(3)
            for dz in range(3)
        ],
        axis=1,
    )
    pre = jnp.dot(part, taps_ref[...].reshape(36 * CIN, 2 * C1), preferred_element_type=F32)

    sigmoid = 1.0 / (1.0 + jnp.exp(-pre))
    act = jnp.where(active, pre * sigmoid, 0.0).astype(BF16)
    slope = jnp.where(active, sigmoid * (1.0 + pre * (1.0 - sigmoid)), 0.0)

    act = act.reshape(2, 2, 2, 4, 2, 16, 2 * C1)
    slope = slope.reshape(2, 2, 2, 4, 2, 16, 2 * C1)
    for ox in range(2):
        for oz in range(2):
            act_ref[ox * 2 + oz] = act[:, :, ox, :, oz].reshape(256, 2 * C1)
            slope_ref[ox * 2 + oz] = slope[:, :, ox, :, oz].reshape(256, 2 * C1)


def down_grad_kernel(samples, act_ref, slope_ref, own_ref, got_ref, pairs_ref, pg_ref, mine_ref, other_ref):
    first = slab_tiles()[1] == 0
    own = own_ref[...].astype(F32)
    got = got_ref[...].astype(F32)
    cot = jnp.concatenate([jnp.where(first, own, got), jnp.where(first, got, own)], axis=0).astype(BF16)
    edge = jnp.zeros((2, SX, 1, 16, 2 * C1), BF16)
    pg_ref[:, :, 0:1] = edge
    pg_ref[:, :, SZ + 1 : SZ + 2] = edge
    low = (lax.axis_index("tile") & 1) == 0
    down_rows = 8 * C1 // samples
    step = min(C1, down_rows)
    for ox in range(2):
        for oz in range(2):
            back = lax.dot_general(cot, pairs_ref[ox * 2 + oz], NT, preferred_element_type=F32)
            part = (back * slope_ref[ox * 2 + oz]).astype(BF16)
            part = part.reshape(2, 2, 4, 16, 2 * C1)
            for s in range(2):
                for u in range(2):
                    for w in range(4):
                        pg_ref[s, 2 * u + ox, 1 + 2 * w + oz] = part[s, u, w]
            grad = lax.dot_general(act_ref[ox * 2 + oz], cot, TN, preferred_element_type=F32)
            for p in range(2):
                for i in range(0, C1, step):
                    chunk, row = divmod((ox * 4 + p * 2 + oz) * C1 + i, down_rows)
                    left = grad[p * C1 + i : p * C1 + i + step, 0:128]
                    right = grad[p * C1 + i : p * C1 + i + step, 128:256]
                    mine_ref[chunk, row : row + step, :] = jnp.where(low, left, right)
                    other_ref[chunk, row : row + step, :] = jnp.where(low, right, left).astype(BF16)


def conv_grad_kernel(samples, half_rows, es_ref, pg_ref, mine_ref, other_ref, tall_ref):
    full = 2 * SX * LAYER
    flipped = es_ref[:, :, 1 : SZ + 1].reshape(2 * (SX + 2) * LAYER, 4 * CIN).T
    half = (SX + 2) * LAYER
    part = jnp.concatenate(
        [pg_ref[:, :, 2 - dz : 2 - dz + SZ].reshape(full, 2 * C1) for dz in range(3)], axis=1
    )
    for dx in range(3):
        rows = jnp.concatenate(
            [flipped[:, s * half + dx * LAYER : s * half + (dx + SX) * LAYER] for s in range(2)], axis=1
        )
        grads = jnp.dot(rows, part, preferred_element_type=F32)
        for dz in range(3):
            grad = grads[:, dz * 256 : (dz + 1) * 256]
            sums = (
                grad[0:64, 128:256] + grad[128:192, 0:128],
                grad[0:64, 0:128] + grad[64:128, 128:256],
                grad[64:128, 0:128] + grad[192:256, 128:256],
            )
            for dy in range(3):
                start = ((dx * 3 + dy) * 3 + dz) * CIN
                tall_ref[start : start + CIN, :] = sums[dy]

    conv_rows = TAPS * CIN // samples
    filler = 2 * half_rows - conv_rows
    low = (lax.axis_index("tile") & 1) == 0
    for s in range(samples):
        first = tall_ref[s * conv_rows : s * conv_rows + half_rows, :]
        second = tall_ref[s * conv_rows + half_rows : (s + 1) * conv_rows, :]
        if filler:
            second = jnp.concatenate([second, jnp.zeros((filler, C1), F32)], axis=0)
        mine_ref[s] = jnp.where(low, first, second)
        other_ref[s] = jnp.where(low, second, first).astype(BF16)


def down_kernel(act_ref, pairs_ref, out_ref):
    place = slab_tiles()[1]
    down = jnp.zeros((128, C2), F32)
    for i in range(4):
        rows = act_ref[i, pl.ds(pl.multiple_of(place * 128, 128), 128)]
        down = down + jnp.dot(rows, pairs_ref[i], preferred_element_type=F32)
    out_ref[...] = jnp.dot(turn_matrix(), down.astype(BF16), preferred_element_type=F32).astype(BF16)


def share_samples_kernel(samples, mine_ref, got_ref, mine_conv_ref, got_conv_ref, keep_ref, *send_refs):
    me = lax.axis_index("sample")
    rows = mine_ref.shape[1]
    for k, ref in enumerate((keep_ref, *send_refs)):
        to = target(me, k, samples) if k else me
        ref[:rows] = (mine_ref[to] + got_ref[to].astype(F32)).astype(ref.dtype)
        ref[rows:] = (mine_conv_ref[to] + got_conv_ref[to].astype(F32)).astype(ref.dtype)


def sum_kernel(*refs):
    total = refs[0][...].astype(F32)
    for ref in refs[1:-1]:
        total = total + ref[...].astype(F32)
    refs[-1][...] = total.astype(refs[-1].dtype)


def ordered_sum_kernel(own_ref, *refs):
    held_ref, out_ref = refs[-1], refs[-2]
    count = len(refs) - 1
    me = lax.axis_index("tile") // (2 * BLOCK)
    held_ref[me] = own_ref[...].astype(F32)
    for j, ref in enumerate(refs[:-2], 1):
        held_ref[lax.rem(me - j + count, count)] = ref[...].astype(F32)
    total = held_ref[0]
    for i in range(1, count):
        total = total + held_ref[i]
    out_ref[...] = total


def finish_kernel(down_rows, own_ref, got_ref, conv_ref, down_ref):
    low = (lax.axis_index("tile") & 1) == 0
    own = own_ref[...]
    got = got_ref[...]
    first = jnp.where(low, own, got)
    second = jnp.where(low, got, own)
    half_rows = first.shape[0] - down_rows
    down_ref[:, 0:128] = first[:down_rows]
    down_ref[:, 128:256] = second[:down_rows]
    conv_ref[0:half_rows, :] = first[down_rows:]
    conv_ref[half_rows:, :] = second[down_rows : down_rows + conv_ref.shape[0] - half_rows]


def local(points, slot, voxel, conv_weight, down_weight, cotangent):
    tiles = lax.axis_size("tile")
    samples = lax.axis_size("sample")
    chips = tiles // 2
    capacity = 2 * (PTS_DEV // tiles)
    conv_rows = TAPS * CIN // samples
    down_rows = 8 * C1 // samples
    half_rows = -(-conv_rows // 32) * 16

    hbm = jax.ShapeDtypeStruct
    shape = pltpu.VMEM
    coded = call(
        functools.partial(encode_kernel, capacity),
        shape((CODED, PTS_DEV), BF16),
        scratch=(
            pltpu.VMEM((1, PTS_DEV), I32),
            pltpu.VMEM((1, PTS_DEV), I32),
            pltpu.SemaphoreType.DMA((3,)),
        ),
        raw=3,
    )(points[0].T, slot, voxel)
    blocks = chips // BLOCK

    sums = (shape((6 * LAYER, 4 * CIN), F32), shape((64, 32), F32))

    def add(grid, piece, at=None):
        if grid is None:
            return call(functools.partial(first_points_kernel, at), sums, pinned=1)(piece)
        return call(functools.partial(more_points_kernel, at), sums, pinned=3)(*grid, piece)

    beyond = send_column(coded, lambda i: i ^ FAR, tiles)
    beside = send_column(coded, lambda i: i ^ 1, tiles)
    taps, pairs, cot, *masks = call(
        weights_kernel,
        (
            shape((9, 4 * CIN, 2 * C1), BF16),
            shape((4, 2 * C1, C2), BF16),
            shape((128, C2), BF16),
            shape((2 * SX * LAYER, 64), BF16),
            shape((2 * SX * LAYER, 32), BF16),
            shape((32, 2 * C1), BF16),
        ),
        loose=3,
    )(conv_weight, down_weight, cotangent.reshape(128, C2))
    beyond, taps, pairs, cot, coded = lax.optimization_barrier((beyond, taps, pairs, cot, coded))
    across = send_column(beyond, lambda i: i ^ 1, tiles)
    far = add(None, beyond)
    coded, beyond, far, cot = lax.optimization_barrier((coded, beyond, far, cot))
    own = add(None, coded)
    coded_swap = swap_core(coded, tiles)
    beyond_swap = swap_core(beyond, tiles)
    cot_got = send_column(cot, lambda i: i ^ FAR, tiles)
    own = add(own, beside)
    beside, own = lax.optimization_barrier((beside, own))
    beside_swap = swap_core(beside, tiles)
    across, own, far = lax.optimization_barrier((across, own, far))
    across_swap = swap_core(across, tiles)
    late = call(late_points_kernel, sums * 3, pinned=6)(*far, across, coded_swap, beside_swap, beyond_swap)
    far, own_swap, far_swap = late[:2], late[2:4], late[4:]
    across_swap, far = lax.optimization_barrier((across_swap, far))
    far_swap = add(far_swap, across_swap)
    grids = [own, own_swap, far, far_swap]
    if blocks > 1:
        rest = call(add_grids_kernel, sums, pinned=8)(*grids[0], *grids[1], *grids[2], *grids[3])
        for j in range(1, blocks):
            got = [
                send_column(coded, lambda i: (i // BLOCK + j) % blocks * BLOCK + (i % BLOCK ^ m), tiles)
                for m in (0, 1, FAR, FAR ^ 1)
            ]
            swapped = [swap_core(piece, tiles) for piece in got]
            trees = [
                add(add(None, first), second)
                for first, second in (got[:2], swapped[:2], got[2:], swapped[2:])
            ]
            both = call(add_grids_kernel, sums, pinned=8)(*trees[0], *trees[1], *trees[2], *trees[3])
            parts = both if j == 1 else call(add_two_kernel, sums, pinned=4)(*parts, *both)
        nothing = (jnp.zeros((6 * LAYER, 4 * CIN), F32), jnp.zeros((64, 32), F32))
        grids = [rest, nothing, parts, nothing]

    act, slope, es = call(
        scene_kernel,
        (
            shape((4, 256, 2 * C1), BF16),
            shape((4, 256, 2 * C1), F32),
            shape((2, SX + 2, SZ + 2, 16, 4 * CIN), BF16),
        ),
        pinned=12,
    )(*grids[0], *grids[1], *grids[2], *grids[3], taps, *masks)
    pg, mine, other = call(
        functools.partial(down_grad_kernel, samples),
        (
            shape((2, SX, SZ + 2, 16, 2 * C1), BF16),
            shape((samples, down_rows, 128), F32),
            shape((samples, down_rows, 128), BF16),
        ),
        pinned=5,
    )(act, slope, cot, cot_got, pairs)

    got = swap_core(other, tiles)
    mine_conv, other_conv = call(
        functools.partial(conv_grad_kernel, samples, half_rows),
        (shape((samples, half_rows, C1), F32), shape((samples, half_rows, C1), BF16)),
        scratch=(pltpu.VMEM((TAPS * CIN, C1), F32),),
        pinned=2,
    )(es, pg)
    got, mine_conv, other_conv = lax.optimization_barrier((got, mine_conv, other_conv))
    sum_rows = down_rows + half_rows
    keep, *sends = call(
        functools.partial(share_samples_kernel, samples),
        [shape((sum_rows, 128), F32)] + [shape((sum_rows, 128), BF16)] * (samples - 1),
        pinned=4,
    )(mine, got, mine_conv, swap_core(other_conv, tiles))
    terms = [keep] + [send_sample(value, k, samples) for k, value in enumerate(sends, 1)]
    down = call(down_kernel, shape((128, C2), BF16), pinned=2)(act, pairs)
    down = down.reshape(1, SX // 2, SY // 2, SZ // 2, C2)
    *terms, down = lax.optimization_barrier((*terms, down))
    total = call(sum_kernel, shape((sum_rows, 128), BF16), pinned=samples)(*terms)
    got = send_column(total, lambda i: i ^ 1, tiles)
    total = call(sum_kernel, shape((sum_rows, 128), F32 if blocks == 1 else BF16), pinned=2)(total, got)
    if blocks > 1:
        got = [send_column(total, lambda i: (i + j * BLOCK) % chips, tiles) for j in range(1, blocks)]
        total = call(
            ordered_sum_kernel,
            shape((sum_rows, 128), F32),
            scratch=(pltpu.VMEM((blocks, sum_rows, 128), F32),),
            pinned=blocks,
        )(total, *got)
    conv_grad, down_grad = call(
        functools.partial(finish_kernel, down_rows),
        (hbm((conv_rows, C1), F32), hbm((down_rows, C2), F32)),
        pinned=2,
    )(total, swap_core(total, tiles))
    return (down, conv_grad, down_grad)


def solution(mesh):
    placed = (
        P("sample", "tile", None),
        P("sample", "tile"),
        P("sample", "tile"),
        P(),
        P(),
        P("sample", "tile", None, None, None),
    )
    return jax.shard_map(
        local,
        mesh=mesh,
        in_specs=placed,
        out_specs=(P("sample", "tile", None, None, None), P("sample", None), P("sample", None)),
        check_vma=False,
    )
```

```python
import functools

import jax
import jax.numpy as jnp
from jax import lax
from jax.experimental import pallas as pl
from jax.experimental.pallas import tpu as pltpu
from jax.sharding import PartitionSpec as P

CIN = 64
C1 = 128
C2 = 256
SX = 4
SY = 32
SZ = 8
PTS_DEV = 1024
TAPS = 27
CODED = CIN + 8
LAYER = SZ * SY // 2
FAR = 3
BLOCK = 4
BF16 = jnp.bfloat16
F32 = jnp.float32
I32 = jnp.int32
NT = (((1,), (1,)), ((), ()))
TN = (((0,), (0,)), ((), ()))
VMEM_LIMIT = 24 * 1024 * 1024


def call(body, outs, scratch=(), pinned=0, loose=0, raw=0, out_space=pltpu.VMEM):
    single = not isinstance(outs, (list, tuple))
    vmem = pl.BlockSpec(memory_space=pltpu.VMEM)
    result = pl.BlockSpec(memory_space=out_space)
    kernel = pl.pallas_call(
        body,
        out_shape=outs,
        in_specs=[vmem] * (pinned + loose) + [pl.BlockSpec(memory_space=pltpu.HBM)] * raw,
        out_specs=result if single else [result] * len(outs),
        scratch_shapes=list(scratch),
        compiler_params=pltpu.CompilerParams(vmem_limit_bytes=VMEM_LIMIT),
    )

    def run(*args):
        held = [pltpu.with_memory_space_constraint(a, pltpu.VMEM) for a in args[:pinned]]
        far = [pltpu.with_memory_space_constraint(a, pltpu.HBM) for a in args[pinned:]]
        return kernel(*held, *far)

    return run


def target(index, k, count):
    if count & (count - 1) == 0:
        return index ^ k
    return (index + k) % count


def swap_core(value, tiles):
    return lax.ppermute(value, "tile", [(i, i ^ 1) for i in range(tiles)])


def send_column(value, to, tiles):
    pairs = [(2 * i + c, 2 * to(i) + c) for i in range(tiles // 2) for c in range(2)]
    return lax.ppermute(value, "tile", pairs)


def send_sample(value, k, samples):
    return lax.ppermute(value, "sample", [(i, target(i, k, samples)) for i in range(samples)])


def encode_kernel(capacity, points_hbm, slot_hbm, voxel_hbm, out_ref, slot_ref, voxel_ref, sems):
    copies = [
        pltpu.make_async_copy(slot_hbm, slot_ref, sems.at[0]),
        pltpu.make_async_copy(voxel_hbm, voxel_ref, sems.at[1]),
        pltpu.make_async_copy(points_hbm, out_ref.at[0:CIN], sems.at[2]),
    ]
    for copy in copies:
        copy.start()
    copies[0].wait()
    copies[1].wait()
    slot = slot_ref[...]
    voxel = voxel_ref[...]
    if capacity & (capacity - 1) == 0:
        owner = slot >> (capacity.bit_length() - 1)
    else:
        owner = jnp.floor((slot.astype(F32) + 0.5) * (1.0 / capacity)).astype(I32)
    layer = owner * SX + (voxel >> 8) + 1
    z = voxel & 7
    y = (voxel >> 3) & 31
    place = ((z * 16 + (y >> 1)) << 1) + (y & 1)
    row = lax.broadcasted_iota(I32, (8, slot.shape[1]), 0)
    codes = jnp.where(row == 0, layer, jnp.where(row == 1, place, 0))
    out_ref[CIN:CODED, :] = codes.astype(F32).astype(BF16)
    copies[2].wait()


def slab_tiles():
    tile = lax.axis_index("tile")
    chip = tile >> 1
    core = tile & 1
    place = (chip >> 1) & 1
    low = jnp.where(place == 0, chip, chip ^ FAR)
    return (2 * low + core, 2 * (low ^ FAR) + core), place


def turn_matrix():
    here = lax.broadcasted_iota(I32, (128, 128), 0)
    there = lax.broadcasted_iota(I32, (128, 128), 1)
    return ((here >> 6) * 64 + (here & 3) * 16 + ((here >> 2) & 15) == there).astype(F32).astype(BF16)


def weights_kernel(
    conv_ref, down_ref, cot_ref, taps_ref, pairs_ref, turned_ref, pick_ref, line_ref, expand_ref
):
    zero_tap = jnp.zeros((CIN, C1), BF16)

    def tap(dx, dy, dz):
        start = ((dx * 3 + dy) * 3 + dz) * CIN
        return conv_ref[start : start + CIN, :]

    for dx in range(3):
        for dz in range(3):
            taps_ref[dx * 3 + dz] = jnp.concatenate(
                [
                    jnp.concatenate([tap(dx, 1, dz), tap(dx, 0, dz)], axis=1),
                    jnp.concatenate([tap(dx, 2, dz), tap(dx, 1, dz)], axis=1),
                    jnp.concatenate([tap(dx, 0, dz), zero_tap], axis=1),
                    jnp.concatenate([zero_tap, tap(dx, 2, dz)], axis=1),
                ],
                axis=0,
            )
    for ox in range(2):
        for oz in range(2):
            first = (ox * 4 + oz) * C1
            second = first + 2 * C1
            pairs_ref[ox * 2 + oz] = jnp.concatenate(
                [down_ref[first : first + C1, :], down_ref[second : second + C1, :]], axis=0
            )
    full = 2 * SX * LAYER
    row_plane = lax.broadcasted_iota(I32, (full, 64), 0) >> 4
    pick_ref[...] = (row_plane == lax.broadcasted_iota(I32, (full, 64), 1)).astype(F32).astype(BF16)
    row_line = lax.broadcasted_iota(I32, (full, 32), 0) & 15
    line_ref[...] = (row_line == (lax.broadcasted_iota(I32, (full, 32), 1) >> 1)).astype(F32).astype(BF16)
    expand_ref[...] = (
        (lax.broadcasted_iota(I32, (32, 256), 0) & 1) == (lax.broadcasted_iota(I32, (32, 256), 1) >> 7)
    ).astype(F32).astype(BF16)
    turned_ref[...] = lax.dot_general(turn_matrix(), cot_ref[...], TN, preferred_element_type=F32).astype(BF16)


def voxelize(ref):
    codes = ref[CIN:CODED, :].astype(F32).astype(I32)
    layer = codes[0:1, :]
    place = codes[1:2, :]
    odd = layer & 1
    spot = place >> 1
    side = place & 1
    row_iota = lax.broadcasted_iota(I32, (LAYER, PTS_DEV), 0).astype(F32).astype(BF16)
    small_iota = lax.broadcasted_iota(I32, (32, PTS_DEV), 0).astype(F32).astype(BF16)
    one = jnp.ones((), BF16)
    nought = jnp.zeros((), BF16)
    hot = []
    hot_plane = []
    for tile in slab_tiles()[0]:
        pair = (layer >> 1) - 2 * tile
        for p in range(3):
            code = jnp.where(pair == p, spot, 255).astype(F32).astype(BF16)
            hot.append(jnp.where(row_iota == code, one, nought))
        plane = (2 * pair + odd - 1) * SZ + (spot >> 4)
        plane = jnp.where((pair >= 0) & (pair <= 2) & (plane >= 0), plane, 255).astype(F32).astype(BF16)
        hot_plane.append(jnp.where(small_iota == plane, one, nought))
    group = odd * 2 + side
    features = ref[0:CIN, :]
    spread = jnp.concatenate(
        [features * (group == g).astype(F32).astype(BF16) for g in range(4)], axis=0
    )
    grid = lax.dot_general(jnp.concatenate(hot, axis=0), spread, NT, preferred_element_type=F32)
    line = ((spot & 15) * 2 + side).astype(F32).astype(BF16)
    hot_line = jnp.where(small_iota == line, one, nought)
    counts = lax.dot_general(
        jnp.concatenate(hot_plane, axis=0), hot_line, NT, preferred_element_type=F32
    )
    return grid, counts


def first_points_kernel(at, ref, grid_ref, counts_ref):
    grid_ref[...], counts_ref[...] = voxelize(ref if at is None else ref.at[at])


def more_points_kernel(at, old_grid_ref, old_counts_ref, ref, grid_ref, counts_ref):
    grid, counts = voxelize(ref if at is None else ref.at[at])
    grid_ref[...] = old_grid_ref[...] + grid
    counts_ref[...] = old_counts_ref[...] + counts


def late_points_kernel(
    old_grid_ref, old_counts_ref, across_ref, coded_ref, beside_ref, beyond_ref,
    far_ref, far_counts_ref, own_ref, own_counts_ref, swap_ref, swap_counts_ref,
):
    first_points_kernel(None, coded_ref, own_ref, own_counts_ref)
    first_points_kernel(None, beyond_ref, swap_ref, swap_counts_ref)
    more_points_kernel(None, own_ref, own_counts_ref, beside_ref, own_ref, own_counts_ref)
    more_points_kernel(None, old_grid_ref, old_counts_ref, across_ref, far_ref, far_counts_ref)


def add_grids_kernel(*refs):
    grid_ref, counts_ref = refs[-2:]
    grid_ref[...] = (refs[0][...] + refs[2][...]) + (refs[4][...] + refs[6][...])
    counts_ref[...] = (refs[1][...] + refs[3][...]) + (refs[5][...] + refs[7][...])


def add_two_kernel(a_ref, a_counts_ref, b_ref, b_counts_ref, grid_ref, counts_ref):
    grid_ref[...] = a_ref[...] + b_ref[...]
    counts_ref[...] = a_counts_ref[...] + b_counts_ref[...]


def scene_kernel(
    grid0, counts0, grid1, counts1, grid2, counts2, grid3, counts3, taps_ref,
    pick_ref, line_ref, expand_ref,
    act_ref, slope_ref, es_ref,
):
    counts = counts0[...] + counts1[...] + counts2[...] + counts3[...]

    edge = jnp.zeros((2, SX + 2, 1, 16, 4 * CIN), BF16)
    es_ref[:, :, 0:1] = edge
    es_ref[:, :, SZ + 1 : SZ + 2] = edge
    line = lax.broadcasted_iota(I32, (LAYER, 2 * CIN), 0) & 15
    lane = lax.broadcasted_iota(I32, (LAYER, 2 * CIN), 1)
    for s in range(2):
        for x in range(SX + 2):
            rows = slice((s * 3 + x // 2) * LAYER, (s * 3 + x // 2 + 1) * LAYER)
            lanes = slice((x % 2) * 128, (x % 2 + 1) * 128)
            both = (grid0[rows, lanes] + grid1[rows, lanes]) + (grid2[rows, lanes] + grid3[rows, lanes])
            turned = pltpu.roll(both, CIN, 1)
            before = jnp.where(line == 0, 0.0, pltpu.roll(turned, 1, 0))
            after = jnp.where(line == 15, 0.0, pltpu.roll(turned, LAYER - 1, 0))
            sides = jnp.where(lane < CIN, before, after)
            es_ref[s, x, 1 : SZ + 1, :, 0:128] = both.astype(BF16).reshape(SZ, 16, 128)
            es_ref[s, x, 1 : SZ + 1, :, 128:256] = sides.astype(BF16).reshape(SZ, 16, 128)

    full = 2 * SX * LAYER
    flags = (counts > 0.5).astype(F32).astype(BF16)
    lines = jnp.dot(pick_ref[...], flags, preferred_element_type=F32)
    lines = lines.astype(BF16) * line_ref[...]
    active = jnp.dot(lines, expand_ref[...], preferred_element_type=F32) > 0.5

    part = jnp.concatenate(
        [
            es_ref[:, dx : dx + SX, dz : dz + SZ].reshape(full, 4 * CIN)
            for dx in range(3)
            for dz in range(3)
        ],
        axis=1,
    )
    pre = jnp.dot(part, taps_ref[...].reshape(36 * CIN, 2 * C1), preferred_element_type=F32)

    sigmoid = 1.0 / (1.0 + jnp.exp(-pre))
    act = jnp.where(active, pre * sigmoid, 0.0).astype(BF16)
    slope = jnp.where(active, sigmoid * (1.0 + pre * (1.0 - sigmoid)), 0.0)

    act = act.reshape(2, 2, 2, 4, 2, 16, 2 * C1)
    slope = slope.reshape(2, 2, 2, 4, 2, 16, 2 * C1)
    for ox in range(2):
        for oz in range(2):
            act_ref[ox * 2 + oz] = act[:, :, ox, :, oz].reshape(256, 2 * C1)
            slope_ref[ox * 2 + oz] = slope[:, :, ox, :, oz].reshape(256, 2 * C1)


def down_grad_kernel(samples, act_ref, slope_ref, own_ref, got_ref, pairs_ref, pg_ref, mine_ref, other_ref):
    first = slab_tiles()[1] == 0
    own = own_ref[...].astype(F32)
    got = got_ref[...].astype(F32)
    cot = jnp.concatenate([jnp.where(first, own, got), jnp.where(first, got, own)], axis=0).astype(BF16)
    edge = jnp.zeros((2, SX, 1, 16, 2 * C1), BF16)
    pg_ref[:, :, 0:1] = edge
    pg_ref[:, :, SZ + 1 : SZ + 2] = edge
    low = (lax.axis_index("tile") & 1) == 0
    down_rows = 8 * C1 // samples
    step = min(C1, down_rows)
    for ox in range(2):
        for oz in range(2):
            back = lax.dot_general(cot, pairs_ref[ox * 2 + oz], NT, preferred_element_type=F32)
            part = (back * slope_ref[ox * 2 + oz]).astype(BF16)
            part = part.reshape(2, 2, 4, 16, 2 * C1)
            for s in range(2):
                for u in range(2):
                    for w in range(4):
                        pg_ref[s, 2 * u + ox, 1 + 2 * w + oz] = part[s, u, w]
            grad = lax.dot_general(act_ref[ox * 2 + oz], cot, TN, preferred_element_type=F32)
            for p in range(2):
                for i in range(0, C1, step):
                    chunk, row = divmod((ox * 4 + p * 2 + oz) * C1 + i, down_rows)
                    left = grad[p * C1 + i : p * C1 + i + step, 0:128]
                    right = grad[p * C1 + i : p * C1 + i + step, 128:256]
                    mine_ref[chunk, row : row + step, :] = jnp.where(low, left, right)
                    other_ref[chunk, row : row + step, :] = jnp.where(low, right, left).astype(BF16)


def conv_grad_kernel(samples, half_rows, es_ref, pg_ref, mine_ref, other_ref, tall_ref):
    full = 2 * SX * LAYER
    flipped = es_ref[:, :, 1 : SZ + 1].reshape(2 * (SX + 2) * LAYER, 4 * CIN).T
    half = (SX + 2) * LAYER
    part = jnp.concatenate(
        [pg_ref[:, :, 2 - dz : 2 - dz + SZ].reshape(full, 2 * C1) for dz in range(3)], axis=1
    )
    for dx in range(3):
        rows = jnp.concatenate(
            [flipped[:, s * half + dx * LAYER : s * half + (dx + SX) * LAYER] for s in range(2)], axis=1
        )
        grads = jnp.dot(rows, part, preferred_element_type=F32)
        for dz in range(3):
            grad = grads[:, dz * 256 : (dz + 1) * 256]
            sums = (
                grad[0:64, 128:256] + grad[128:192, 0:128],
                grad[0:64, 0:128] + grad[64:128, 128:256],
                grad[64:128, 0:128] + grad[192:256, 128:256],
            )
            for dy in range(3):
                start = ((dx * 3 + dy) * 3 + dz) * CIN
                tall_ref[start : start + CIN, :] = sums[dy]

    conv_rows = TAPS * CIN // samples
    filler = 2 * half_rows - conv_rows
    low = (lax.axis_index("tile") & 1) == 0
    for s in range(samples):
        first = tall_ref[s * conv_rows : s * conv_rows + half_rows, :]
        second = tall_ref[s * conv_rows + half_rows : (s + 1) * conv_rows, :]
        if filler:
            second = jnp.concatenate([second, jnp.zeros((filler, C1), F32)], axis=0)
        mine_ref[s] = jnp.where(low, first, second)
        other_ref[s] = jnp.where(low, second, first).astype(BF16)


def down_kernel(act_ref, pairs_ref, out_ref):
    place = slab_tiles()[1]
    down = jnp.zeros((128, C2), F32)
    for i in range(4):
        rows = act_ref[i, pl.ds(pl.multiple_of(place * 128, 128), 128)]
        down = down + jnp.dot(rows, pairs_ref[i], preferred_element_type=F32)
    out_ref[...] = jnp.dot(turn_matrix(), down.astype(BF16), preferred_element_type=F32).astype(BF16)


def share_samples_kernel(samples, mine_ref, got_ref, mine_conv_ref, got_conv_ref, keep_ref, *send_refs):
    me = lax.axis_index("sample")
    rows = mine_ref.shape[1]
    for k, ref in enumerate((keep_ref, *send_refs)):
        to = target(me, k, samples) if k else me
        ref[:rows] = (mine_ref[to] + got_ref[to].astype(F32)).astype(ref.dtype)
        ref[rows:] = (mine_conv_ref[to] + got_conv_ref[to].astype(F32)).astype(ref.dtype)


def sum_kernel(*refs):
    total = refs[0][...].astype(F32)
    for ref in refs[1:-1]:
        total = total + ref[...].astype(F32)
    refs[-1][...] = total.astype(refs[-1].dtype)


def ordered_sum_kernel(own_ref, *refs):
    held_ref, out_ref = refs[-1], refs[-2]
    count = len(refs) - 1
    me = lax.axis_index("tile") // (2 * BLOCK)
    held_ref[me] = own_ref[...].astype(F32)
    for j, ref in enumerate(refs[:-2], 1):
        held_ref[lax.rem(me - j + count, count)] = ref[...].astype(F32)
    total = held_ref[0]
    for i in range(1, count):
        total = total + held_ref[i]
    out_ref[...] = total


def finish_kernel(down_rows, own_ref, got_ref, conv_hbm, down_hbm, sems):
    half_rows = own_ref.shape[0] - down_rows
    rest = conv_hbm.shape[0] - half_rows
    core = lax.axis_index("tile") & 1

    def leave(first, second):
        copies = [
            pltpu.make_async_copy(first.at[:down_rows], down_hbm.at[:, 0:128], sems.at[0]),
            pltpu.make_async_copy(second.at[:down_rows], down_hbm.at[:, 128:256], sems.at[1]),
            pltpu.make_async_copy(
                first.at[down_rows : down_rows + half_rows], conv_hbm.at[0:half_rows], sems.at[2]
            ),
            pltpu.make_async_copy(
                second.at[down_rows : down_rows + rest], conv_hbm.at[half_rows : half_rows + rest], sems.at[3]
            ),
        ]
        for copy in copies:
            copy.start()
        for copy in copies:
            copy.wait()

    @pl.when(core == 0)
    def _():
        leave(own_ref, got_ref)

    @pl.when(core == 1)
    def _():
        leave(got_ref, own_ref)


def local(points, slot, voxel, conv_weight, down_weight, cotangent):
    tiles = lax.axis_size("tile")
    samples = lax.axis_size("sample")
    chips = tiles // 2
    capacity = 2 * (PTS_DEV // tiles)
    conv_rows = TAPS * CIN // samples
    down_rows = 8 * C1 // samples
    half_rows = -(-conv_rows // 32) * 16

    hbm = jax.ShapeDtypeStruct
    shape = pltpu.VMEM
    coded = call(
        functools.partial(encode_kernel, capacity),
        shape((CODED, PTS_DEV), BF16),
        scratch=(
            pltpu.VMEM((1, PTS_DEV), I32),
            pltpu.VMEM((1, PTS_DEV), I32),
            pltpu.SemaphoreType.DMA((3,)),
        ),
        raw=3,
    )(points[0].T, slot, voxel)
    blocks = chips // BLOCK

    sums = (shape((6 * LAYER, 4 * CIN), F32), shape((64, 32), F32))

    def add(grid, piece, at=None):
        if grid is None:
            return call(functools.partial(first_points_kernel, at), sums, pinned=1)(piece)
        return call(functools.partial(more_points_kernel, at), sums, pinned=3)(*grid, piece)

    beyond = send_column(coded, lambda i: i ^ FAR, tiles)
    beside = send_column(coded, lambda i: i ^ 1, tiles)
    taps, pairs, cot, *masks = call(
        weights_kernel,
        (
            shape((9, 4 * CIN, 2 * C1), BF16),
            shape((4, 2 * C1, C2), BF16),
            shape((128, C2), BF16),
            shape((2 * SX * LAYER, 64), BF16),
            shape((2 * SX * LAYER, 32), BF16),
            shape((32, 2 * C1), BF16),
        ),
        loose=3,
    )(conv_weight, down_weight, cotangent.reshape(128, C2))
    beyond, taps, pairs, cot, coded = lax.optimization_barrier((beyond, taps, pairs, cot, coded))
    across = send_column(beyond, lambda i: i ^ 1, tiles)
    far = add(None, beyond)
    coded, beyond, far, cot = lax.optimization_barrier((coded, beyond, far, cot))
    own = add(None, coded)
    coded_swap = swap_core(coded, tiles)
    beyond_swap = swap_core(beyond, tiles)
    cot_got = send_column(cot, lambda i: i ^ FAR, tiles)
    own = add(own, beside)
    beside, own = lax.optimization_barrier((beside, own))
    beside_swap = swap_core(beside, tiles)
    across, own, far = lax.optimization_barrier((across, own, far))
    across_swap = swap_core(across, tiles)
    late = call(late_points_kernel, sums * 3, pinned=6)(*far, across, coded_swap, beside_swap, beyond_swap)
    far, own_swap, far_swap = late[:2], late[2:4], late[4:]
    across_swap, far = lax.optimization_barrier((across_swap, far))
    far_swap = add(far_swap, across_swap)
    grids = [own, own_swap, far, far_swap]
    if blocks > 1:
        rest = call(add_grids_kernel, sums, pinned=8)(*grids[0], *grids[1], *grids[2], *grids[3])
        for j in range(1, blocks):
            got = [
                send_column(coded, lambda i: (i // BLOCK + j) % blocks * BLOCK + (i % BLOCK ^ m), tiles)
                for m in (0, 1, FAR, FAR ^ 1)
            ]
            swapped = [swap_core(piece, tiles) for piece in got]
            trees = [
                add(add(None, first), second)
                for first, second in (got[:2], swapped[:2], got[2:], swapped[2:])
            ]
            both = call(add_grids_kernel, sums, pinned=8)(*trees[0], *trees[1], *trees[2], *trees[3])
            parts = both if j == 1 else call(add_two_kernel, sums, pinned=4)(*parts, *both)
        nothing = (jnp.zeros((6 * LAYER, 4 * CIN), F32), jnp.zeros((64, 32), F32))
        grids = [rest, nothing, parts, nothing]

    act, slope, es = call(
        scene_kernel,
        (
            shape((4, 256, 2 * C1), BF16),
            shape((4, 256, 2 * C1), F32),
            shape((2, SX + 2, SZ + 2, 16, 4 * CIN), BF16),
        ),
        pinned=12,
    )(*grids[0], *grids[1], *grids[2], *grids[3], taps, *masks)
    pg, mine, other = call(
        functools.partial(down_grad_kernel, samples),
        (
            shape((2, SX, SZ + 2, 16, 2 * C1), BF16),
            shape((samples, down_rows, 128), F32),
            shape((samples, down_rows, 128), BF16),
        ),
        pinned=5,
    )(act, slope, cot, cot_got, pairs)

    got = swap_core(other, tiles)
    mine_conv, other_conv = call(
        functools.partial(conv_grad_kernel, samples, half_rows),
        (shape((samples, half_rows, C1), F32), shape((samples, half_rows, C1), BF16)),
        scratch=(pltpu.VMEM((TAPS * CIN, C1), F32),),
        pinned=2,
    )(es, pg)
    got, mine_conv, other_conv = lax.optimization_barrier((got, mine_conv, other_conv))
    sum_rows = down_rows + half_rows
    keep, *sends = call(
        functools.partial(share_samples_kernel, samples),
        [shape((sum_rows, 128), F32)] + [shape((sum_rows, 128), BF16)] * (samples - 1),
        pinned=4,
    )(mine, got, mine_conv, swap_core(other_conv, tiles))
    terms = [keep] + [send_sample(value, k, samples) for k, value in enumerate(sends, 1)]
    down = call(down_kernel, shape((128, C2), BF16), pinned=2)(act, pairs)
    down = down.reshape(1, SX // 2, SY // 2, SZ // 2, C2)
    *terms, down = lax.optimization_barrier((*terms, down))
    total = call(sum_kernel, shape((sum_rows, 128), BF16), pinned=samples)(*terms)
    got = send_column(total, lambda i: i ^ 1, tiles)
    total = call(sum_kernel, shape((sum_rows, 128), F32 if blocks == 1 else BF16), pinned=2)(total, got)
    if blocks > 1:
        got = [send_column(total, lambda i: (i + j * BLOCK) % chips, tiles) for j in range(1, blocks)]
        total = call(
            ordered_sum_kernel,
            shape((sum_rows, 128), F32),
            scratch=(pltpu.VMEM((blocks, sum_rows, 128), F32),),
            pinned=blocks,
        )(total, *got)
    conv_grad, down_grad = call(
        functools.partial(finish_kernel, down_rows),
        (hbm((conv_rows, C1), F32), hbm((down_rows, C2), F32)),
        scratch=(pltpu.SemaphoreType.DMA((4,)),),
        pinned=2,
        out_space=pltpu.HBM,
    )(total, swap_core(total, tiles))
    return (down, conv_grad, down_grad)


def solution(mesh):
    placed = (
        P("sample", "tile", None),
        P("sample", "tile"),
        P("sample", "tile"),
        P(),
        P(),
        P("sample", "tile", None, None, None),
    )
    return jax.shard_map(
        local,
        mesh=mesh,
        in_specs=placed,
        out_specs=(P("sample", "tile", None, None, None), P("sample", None), P("sample", None)),
        check_vma=False,
    )
```
